32 devices in a mesh: gx: 4 (over z), gy: 8 (over y, x, core).
Axes of the slice: x: 2, y: 2, z: 4, core: 2. Of those that a mesh axis runs over, the one named last changes fastest.
Arguments:
- conductivity: float32 [128, 256, 128], P('gx', 'gy'), may hold values from 0.25 to 4
- source: float32 [128, 256, 128], P('gx', 'gy'), may hold values from -12 to 12
- initial: float32 [128, 256, 128], P('gx', 'gy'), may hold values from -3 to 3
Outputs:
- solution: float32 [128, 256, 128], P('gx', 'gy')
The draws below stay inside these ranges and needn't reach their ends.
All inputs are finite; a program needn't handle non-finite values.
Results may differ from the reference program's by a relative error of at most 0.0003.
Values sent between devices are 32-bit elements; how exact they have to be, the bound alone decides.
A program may use at most 64 MiB of HBM per device.

```python
import math
import jax
import jax.numpy as jnp
from jax import lax

BS = 16
NU = 3
CG_ITERS = 32
NX = 128
NY = 256
NZ = 128
N_GX = 4
N_GY = 8


def draw_source(key, part):
    return 4.0 * jax.random.truncated_normal(key, -3.0, 3.0, (NX, NY, NZ), jnp.float32)


def level_of(key, dims, split, smallest, high):
    def one(dim, blocks):
        heights = jax.random.uniform(jax.random.fold_in(jax.random.fold_in(key, 6), dim), (blocks,), jnp.float32, smallest / len(split), high / len(split))
        return jnp.repeat(jnp.exp(heights), dims[dim] // blocks).reshape((-1,) + (1,) * (len(dims) - dim - 1))

    level = one(*split[0])
    for cut in split[1:]:
        level = level * one(*cut)
    return level


def bell_draw(own_key, dims, spread, reach, shards=(), kind=jnp.bfloat16):
    values = jax.random.normal(own_key, dims, jnp.float32) * spread
    if len(shards) > 0:
        values = level_of(own_key, dims, shards, -0.22, 0.18) * values
    return jnp.clip(values, min=-reach, max=reach).astype(kind)


def setup_inputs(seed: int = 0) -> dict:
    seeds = jax.random.split(jax.random.key(seed), 4)
    return {
        "conductivity": jnp.clip(jnp.exp(math.log(4.0) - 2.7725887 * jax.random.uniform(seeds[0], (NX, NY, NZ), jnp.float32) ** level_of(seeds[0], (NX, NY, NZ), ((0, 4), (1, 8)), -0.2, 0.2)), 0.25, 4.0),
        "source": draw_source(jax.random.fold_in(seeds[3], 71), 0),
        "initial": bell_draw(seeds[2], (NX, NY, NZ), 0.5, 3.0, ((0, 4), (1, 8)), jnp.float32),
    }


relax_weight = 0.8


def operate(padded, cond_pad):
    center_cond = cond_pad[1:-1, 1:-1]
    center = padded[1:-1, 1:-1]
    face_east = 0.5 * (center_cond + cond_pad[2:, 1:-1])
    face_west = 0.5 * (center_cond + cond_pad[:-2, 1:-1])
    face_north = 0.5 * (center_cond + cond_pad[1:-1, 2:])
    face_south = 0.5 * (center_cond + cond_pad[1:-1, :-2])
    between = 0.5 * (center_cond[:, :, 1:] + center_cond[:, :, :-1])
    zero_plane = jnp.zeros(center.shape[:2] + (1,), center.dtype)
    face_up = jnp.concatenate([between, zero_plane], 2)
    face_down = jnp.concatenate([zero_plane, between], 2)
    value_up = jnp.concatenate([center[:, :, 1:], zero_plane], 2)
    value_down = jnp.concatenate([zero_plane, center[:, :, :-1]], 2)
    diagonal = face_east + face_west + face_north + face_south + face_up + face_down
    neighbor_sum = (face_east * padded[2:, 1:-1] + face_west * padded[:-2, 1:-1]
                    + face_north * padded[1:-1, 2:] + face_south * padded[1:-1, :-2]
                    + face_up * value_up + face_down * value_down)
    return diagonal * center - neighbor_sum, diagonal, center_cond, center


def smooth_once(padded, cond_pad, source):
    applied, diagonal, center_cond, center = operate(padded, cond_pad)
    inside = center_cond > 0
    update = relax_weight * (source - applied) / jnp.where(inside, diagonal, 1.0)
    return jnp.where(inside, center + update, 0.0)


def coarse_apply(estimate, coarse_diag, flow_east, flow_north):
    edge_rows = jnp.zeros((1, estimate.shape[1]), estimate.dtype)
    edge_cols = jnp.zeros((estimate.shape[0], 1), estimate.dtype)
    ahead_x = jnp.concatenate([estimate[1:], edge_rows], 0)
    carried_x = flow_east * estimate
    behind_x = jnp.concatenate([edge_rows, carried_x[:-1]], 0)
    ahead_y = jnp.concatenate([estimate[:, 1:], edge_cols], 1)
    carried_y = flow_north * estimate
    behind_y = jnp.concatenate([edge_cols, carried_y[:, :-1]], 1)
    return coarse_diag * estimate - flow_east * ahead_x - behind_x - flow_north * ahead_y - behind_y


def coarse_solve(coarse_source, coarse_diag, flow_east, flow_north):
    def iterate_once(counter, carried):
        estimate, remainder, search, norm_now = carried
        product = coarse_apply(search, coarse_diag, flow_east, flow_north)
        alpha_step = norm_now / jnp.sum(search * product)
        estimate = estimate + alpha_step * search
        remainder = remainder - alpha_step * product
        norm_next = jnp.sum(remainder * remainder)
        search = remainder + (norm_next / norm_now) * search
        return estimate, remainder, search, norm_next

    start_state = (jnp.zeros_like(coarse_source), coarse_source, coarse_source,
                   jnp.sum(coarse_source * coarse_source))
    return lax.fori_loop(0, CG_ITERS, iterate_once, start_state)[0]


def reference(conductivity, source, initial):
    extent_x = 2 * BS
    extent_y = 2 * BS
    margins = ((1, 1), (1, 1), (0, 0))
    cond_pad = jnp.pad(conductivity, margins)
    starts = jnp.arange(N_GX, dtype=jnp.int32) * extent_x

    def sweep_all(iterate):
        padded = jnp.pad(iterate, margins)

        def one_slab(offset):
            return smooth_once(lax.dynamic_slice_in_dim(padded, offset, extent_x + 2, 0),
                               lax.dynamic_slice_in_dim(cond_pad, offset, extent_x + 2, 0),
                               lax.dynamic_slice_in_dim(source, offset, extent_x, 0))

        return lax.map(one_slab, starts).reshape(conductivity.shape)

    iterate = initial
    for repeat in range(NU):
        iterate = sweep_all(iterate)
    padded = jnp.pad(iterate, margins)

    def slab_residual(offset):
        applied = operate(lax.dynamic_slice_in_dim(padded, offset, extent_x + 2, 0),
                          lax.dynamic_slice_in_dim(cond_pad, offset, extent_x + 2, 0))[0]
        remainder = lax.dynamic_slice_in_dim(source, offset, extent_x, 0) - applied
        return jnp.sum(remainder.reshape(extent_x, N_GY, extent_y, -1), axis=(0, 2, 3))

    coarse_source = lax.map(slab_residual, starts)
    whole_x = conductivity.shape[0]
    high_x = jnp.pad(conductivity, ((0, 1), (0, 0), (0, 0)))
    plane = 0.5 * (conductivity[extent_x - 1::extent_x] + high_x[extent_x::extent_x])
    flow_east = jnp.sum(plane.reshape(N_GX, N_GY, extent_y, -1), axis=(2, 3))
    low_x = jnp.pad(conductivity, ((1, 0), (0, 0), (0, 0)))
    plane = 0.5 * (conductivity[0::extent_x] + low_x[0:whole_x:extent_x])
    flow_west = jnp.sum(plane.reshape(N_GX, N_GY, extent_y, -1), axis=(2, 3))
    high_y = jnp.pad(conductivity, ((0, 0), (0, 1), (0, 0)))
    plane = 0.5 * (conductivity[:, extent_y - 1::extent_y] + high_y[:, extent_y::extent_y])
    flow_north = jnp.sum(plane.reshape(N_GX, extent_x, N_GY, -1), axis=(1, 3))
    low_y = jnp.pad(conductivity, ((0, 0), (1, 0), (0, 0)))
    plane = 0.5 * (conductivity[:, 0::extent_y] + low_y[:, 0:conductivity.shape[1]:extent_y])
    flow_south = jnp.sum(plane.reshape(N_GX, extent_x, N_GY, -1), axis=(1, 3))
    coarse_diag = flow_east + flow_west + flow_north + flow_south
    correction = coarse_solve(coarse_source, coarse_diag, flow_east, flow_north)
    iterate = iterate + jnp.repeat(jnp.repeat(correction, extent_x, 0), extent_y, 1)[:, :, None]
    for repeat in range(NU):
        iterate = sweep_all(iterate)
    return iterate
```

```python
import functools

import jax
import jax.numpy as jnp
from jax import lax
from jax.experimental import pallas as pl
from jax.experimental.pallas import tpu as pltpu
from jax.sharding import PartitionSpec as P

NU = 3
CG_ITERS = 32
H = NU + 1
WIDTH = (NU, NU - 1, NU)

relax_weight = 0.8
MESH = pl.DeviceIdType.MESH
DIRS = [(1, 0), (-1, 0), (0, 1), (0, -1), (1, 1), (1, -1), (-1, 1), (-1, -1)]


def inside(ix, iy, cx, cy):
    return (ix >= 0) & (ix < cx) & (iy >= 0) & (iy < cy)


def rows_loop(lo, hi, step, carry):
    count = hi - lo
    pairs = count // 2

    def two(i, c):
        x = lo + 2 * i
        return step(x + 1, step(x, c))

    carry = lax.fori_loop(0, pairs, two, carry)
    if count % 2:
        carry = step(hi - 1, carry)
    return carry


ROWS = 8
DIRECT = 64


def blocks_loop(lo, hi, block, carry):
    count = (hi - lo) // ROWS
    carry = lax.fori_loop(0, count, lambda i, c: block(lo + ROWS * i, c, ROWS), carry)
    if (hi - lo) % ROWS:
        carry = block(lo + ROWS * count, carry, (hi - lo) % ROWS)
    return carry


def kernel(cx, cy, nx, ny, *refs):
    (k_in, f_in, u_in, k1, f1, u1, out,
     K, F, U, V, CE, CN, CU, CD, W, YLO_K, YLO_F, YLO_U, YHI_K, YHI_F, YHI_U,
     XLO2, XHI2, YLO2, YHI2, PLO, PHI, GS, E, R,
     lsem, ssem, rsem, ssem2, rsem2,
     s1s, s1r, s2s, s2r, das, dar, chain) = refs
    X = nx + 2 * H
    Y = ny + 2 * H
    ix = lax.axis_index("gx")
    iy = lax.axis_index("gy")
    full = [k_in, f_in, u_in]
    thin = [k1, f1, u1]
    ext = [K, F, U]
    YLO = [YLO_K, YLO_F, YLO_U]
    YHI = [YHI_K, YHI_F, YHI_U]

    direct = cx * cy <= DIRECT
    barrier = pltpu.get_barrier_semaphore()

    def greet_x(k, c):
        pl.semaphore_signal(barrier, inc=1, device_id=(lax.rem(ix + k, cx), iy), device_id_type=MESH)
        return c

    def greet_y(k, c):
        pl.semaphore_signal(barrier, inc=1, device_id=(ix, lax.rem(iy + k, cy)), device_id_type=MESH)
        return c

    for dx, dy in (DIRS[:2] if direct else []) + DIRS[4:]:
        @pl.when(inside(ix + dx, iy + dy, cx, cy))
        def _(dx=dx, dy=dy):
            pl.semaphore_signal(barrier, inc=1, device_id=(ix + dx, iy + dy), device_id_type=MESH)
    if not direct:
        lax.fori_loop(1, cx, greet_x, 0)
    lax.fori_loop(1, cy, greet_y, 0)

    local = [pltpu.make_async_copy(full[a], ext[a].at[H:H + nx, 0:ny, :], lsem.at[a]) for a in range(3)]
    for copy in local:
        copy.start()

    sides_x = (ix > 0).astype(jnp.int32) + (ix < cx - 1).astype(jnp.int32)
    sides_y = (iy > 0).astype(jnp.int32) + (iy < cy - 1).astype(jnp.int32)
    pl.semaphore_wait(barrier, (sides_x if direct else cx - 1) + (cy - 1) + sides_x * sides_y)

    def chain_signal(k):
        for dx in (1, -1):
            @pl.when((ix + dx >= 0) & (ix + dx < cx))
            def _(dx=dx):
                pl.semaphore_signal(chain.at[k], inc=1, device_id=(ix + dx, iy), device_id_type=MESH)

    def chain_wait(k):
        pl.semaphore_wait(chain.at[k], sides_x)

    def spans(dx, w):
        src = {1: (nx - w, nx), -1: (0, w), 0: (0, nx)}[dx]
        dst = {1: (H - w, H), -1: (X - H, X - H + w), 0: (H, H + nx)}[dx]
        return src, dst

    def halo(a, d):
        dx, dy = DIRS[d]
        slot = a * 8 + d
        w = WIDTH[a]
        src_rows, dst_rows = spans(dx, w)
        if dy == 0:
            src = full[a].at[src_rows[0]:src_rows[1]]
            dst = ext[a].at[dst_rows[0]:dst_rows[1], 0:ny, :]
        else:
            cols = (ny - w, ny) if dy == 1 else (0, w)
            src = thin[a].at[src_rows[0]:src_rows[1], cols[0]:cols[1]]
            dst = (YLO if dy == 1 else YHI)[a].at[dst_rows[0]:dst_rows[1]]
        return pltpu.make_async_remote_copy(
            src_ref=src, dst_ref=dst, send_sem=ssem.at[slot], recv_sem=rsem.at[slot],
            device_id=(ix + dx, iy + dy), device_id_type=MESH)

    def each(d, sign, act):
        dx, dy = DIRS[d]
        pl.when(inside(ix + sign * dx, iy + sign * dy, cx, cy))(act)

    links = cx - 1 if direct else 0
    if links:
        chain_signal(0)
    for d in range(8):
        def start(d=d):
            for a in range(3):
                halo(a, d).start()
        each(d, 1, start)

    def clear_when_absent(d):
        dx, dy = DIRS[d]

        @pl.when(jnp.logical_not(inside(ix - dx, iy - dy, cx, cy)))
        def _():
            for a in range(3):
                w = WIDTH[a]
                lo, hi = spans(dx, w)[1]
                if dy == 0:
                    ext[a][lo:hi, 0:ny, :] = jnp.zeros((w, ny, 128), jnp.float32)
                else:
                    (YLO if dy == 1 else YHI)[a][lo:hi] = jnp.zeros((hi - lo, w, 1, 128), jnp.float32)
            if dy == 0:
                (XLO2 if dx == 1 else XHI2)[...] = jnp.zeros((NU, ny, 128), jnp.float32)
            else:
                lo, hi = spans(dx, H)[1]
                (YLO2 if dy == 1 else YHI2)[lo:hi] = jnp.zeros((hi - lo, H, 128), jnp.float32)

    for d in range(8):
        clear_when_absent(d)

    for copy in local:
        copy.wait()

    def along_x(G, ss, rs):
        def of(k):
            return pltpu.make_async_remote_copy(
                src_ref=G.at[iy, ix], dst_ref=G.at[iy, ix], send_sem=ss.at[k - 1], recv_sem=rs.at[k - 1],
                device_id=(lax.rem(ix + k, cx), iy), device_id_type=MESH)
        return of

    def along_y(G, ss, rs):
        def of(k):
            return pltpu.make_async_remote_copy(
                src_ref=G.at[iy], dst_ref=G.at[iy], send_sem=ss.at[k - 1], recv_sem=rs.at[k - 1],
                device_id=(ix, lax.rem(iy + k, cy)), device_id_type=MESH)
        return of

    def to_all(k):
        target = lax.rem(ix * cy + iy + k, cx * cy)
        return pltpu.make_async_remote_copy(
            src_ref=GS.at[iy, ix], dst_ref=GS.at[iy, ix], send_sem=das.at[k - 1], recv_sem=dar.at[k - 1],
            device_id=(target // cy, lax.rem(target, cy)), device_id_type=MESH)

    def run(of, count, method):
        def go(k, c):
            getattr(of(k), method)()
            return c
        lax.fori_loop(1, count, go, 0)

    sum_x, sum_y = along_x(GS, s1s, s1r), along_y(GS, s2s, s2r)

    lane_row = lax.broadcasted_iota(jnp.int32, (1, 128), 1)

    def whole(v):
        return jnp.sum(jnp.sum(v, axis=0, keepdims=True), axis=1, keepdims=True)

    def in_lanes(values):
        row = jnp.zeros((1, 128), jnp.float32)
        for k, v in enumerate(values):
            row = jnp.where(lane_row == k, v, row)
        return row

    def outer(x, c):
        return c[0] + K[x, 0:1, :], c[1] + K[x, ny - 1:ny, :]

    none = jnp.zeros((1, 128), jnp.float32)
    y_first, y_last = rows_loop(H, H + nx, outer, (none, none))
    edges = [whole(K[H, 0:ny, :]), whole(K[H + nx - 1, 0:ny, :]), whole(y_first), whole(y_last)]
    f_total = rows_loop(H, H + nx, lambda x, c: c + F[x, 0:ny, :], jnp.zeros((ny, 128), jnp.float32))
    f_total = jnp.sum(f_total, axis=0, keepdims=True)

    for k in range(links):
        chain_wait(k)
        if k + 1 < links:
            chain_signal(k + 1)

    for d in range(8):
        def finish(d=d):
            for a in range(3):
                halo(a, d).wait_recv()
        each(d, -1, finish)

    def unpack(x, c):
        for a in range(3):
            w = WIDTH[a]
            ext[a][x, ny:ny + w, :] = YHI[a][x, :, 0, :]
            ext[a][x, Y - w:Y, :] = YLO[a][x, :, 0, :]
        return c

    rows_loop(1, X - 1, unpack, 0)

    lane = lax.broadcasted_iota(jnp.int32, (Y, 128), 1)
    up_half = jnp.where(lane < 127, 0.5, 0.0)
    down_half = jnp.where(lane > 0, 0.5, 0.0)

    def next_y(v):
        return pltpu.roll(v, Y - 1, 0)

    def last_y(v):
        return pltpu.roll(v, 1, 0)

    def next_z(v):
        return pltpu.roll(v, 127, 1)

    def last_z(v):
        return pltpu.roll(v, 1, 1)

    def faces(x, c, rows):
        k, west = c
        ks = [k] + [K[x + 1 + r] for r in range(rows)]
        ups = [next_z(ks[r]) for r in range(rows)]
        downs = [last_z(ks[r]) for r in range(rows)]
        for r in range(rows):
            k = ks[r]
            east = 0.5 * (k + ks[r + 1])
            north = 0.5 * (k + next_y(k))
            up = up_half * (k + ups[r])
            down = down_half * (k + downs[r])
            d = east + west + north + last_y(north) + up + down
            CE[x + r] = east
            CN[x + r] = north
            CU[x + r] = up
            CD[x + r] = down
            W[x + r] = jnp.where(k > 0, relax_weight / jnp.where(k > 0, d, 1.0), 0.0)
            west = east
        return ks[rows], west

    zero = jnp.zeros((Y, 128), jnp.float32)
    CE[1] = 0.5 * (K[1] + K[2])
    blocks_loop(2, X - 2, faces, (K[2], CE[1]))

    def sweep(src, dst, lo, hi, final=False, last=False):
        def block(x, c, rows):
            u, west, low, high = c
            us = [u] + [src[x + 1 + r] for r in range(rows)]
            ups = [next_z(us[r]) for r in range(rows)]
            downs = [last_z(us[r]) for r in range(rows)]
            for r in range(rows):
                u = us[r]
                east = CE[x + r] * (us[r + 1] - u)
                cn = CN[x + r]
                north = cn * (next_y(u) - u)
                change = ((east - west) + (north - last_y(north))
                          + (CU[x + r] * (ups[r] - u) + CD[x + r] * (downs[r] - u)))
                new = u + W[x + r] * (F[x + r] + change)
                if last:
                    dst[x + r - H] = new[0:ny]
                else:
                    dst[x + r] = new
                if final:
                    low, high = low + cn[Y - 1:Y] * new[0:1], high + cn[ny - 1:ny] * new[ny - 1:ny]
                west = east
            return us[rows], west, low, high

        start = (src[lo], CE[lo - 1] * (src[lo] - src[lo - 1]))
        start += (none, none) if final else (0, 0)
        return blocks_loop(lo, hi, block, start)[2:]

    sweep(U, V, 2, X - 2)
    sweep(V, U, 3, X - 3)
    y_low, y_high = sweep(U, V, 4, X - 4, True)

    x_low = jnp.sum(CE[H - 1, 0:ny, :] * V[H, 0:ny, :], axis=0, keepdims=True)
    x_high = jnp.sum(CE[X - H - 1, 0:ny, :] * V[X - H - 1, 0:ny, :], axis=0, keepdims=True)
    own = f_total - x_low - x_high - y_low - y_high
    GS[iy, ix] = in_lanes([whole(v) for v in (own, x_low, x_high, y_low, y_high)] + edges)
    if direct:
        run(to_all, cx * cy, "start")
    else:
        run(sum_x, cx, "start")

    def pack(x, c):
        PLO[x] = V[H + x, 0:H, :]
        PHI[x] = V[H + x, ny - H:ny, :]
        return c

    rows_loop(0, nx, pack, 0)

    def halo2(d):
        dx, dy = DIRS[d]
        src_rows = {1: (nx - H, nx), -1: (0, H), 0: (0, nx)}[dx]
        dst_rows = {1: (0, H), -1: (X - H, X), 0: (H, H + nx)}[dx]
        if dy == 0:
            src = V.at[nx + 1:nx + H, 0:ny, :] if dx == 1 else V.at[H:H + NU, 0:ny, :]
            dst = XLO2 if dx == 1 else XHI2
        else:
            src = (PHI if dy == 1 else PLO).at[src_rows[0]:src_rows[1]]
            dst = (YLO2 if dy == 1 else YHI2).at[dst_rows[0]:dst_rows[1]]
        return pltpu.make_async_remote_copy(
            src_ref=src, dst_ref=dst, send_sem=ssem2.at[d], recv_sem=rsem2.at[d],
            device_id=(ix + dx, iy + dy), device_id_type=MESH)

    row_y = lax.broadcasted_iota(jnp.int32, (cy, 128), 0)

    def tidy(G):
        for x in range(cx):
            for y in range(cy):
                R[x, y:y + 1, :] = G[y, x]
        return [R[x] for x in range(cx)]

    def lane_of(rows, k):
        return [jnp.broadcast_to(r[:, k:k + 1], (cy, 128)) for r in rows]

    def after_y(v):
        return jnp.where(row_y < cy - 1, pltpu.roll(v, cy - 1, 0), 0.0)

    def before_y(v):
        return jnp.where(row_y > 0, pltpu.roll(v, 1, 0), 0.0)

    if not direct:
        run(sum_x, cx, "wait_recv")
        run(sum_y, cy, "start")
    for d in range(8):
        each(d, 1, lambda d=d: halo2(d).start())
    run(*((to_all, cx * cy) if direct else (sum_y, cy)), "wait_recv")
    coarse_rows = tidy(GS)
    nil = jnp.zeros((cy, 128), jnp.float32)
    x_first, x_last, y_first, y_last = [lane_of(coarse_rows, k) for k in range(5, 9)]
    east = [0.5 * (a + b) for a, b in zip(x_last, x_first[1:] + [nil])]
    west = [0.5 * (a + b) for a, b in zip(x_first, [nil] + x_last[:-1])]
    north = [0.5 * (a + after_y(b)) for a, b in zip(y_last, y_first)]
    south = [0.5 * (a + before_y(b)) for a, b in zip(y_first, y_last)]
    diag = [a + b + c + d for a, b, c, d in zip(east, west, north, south)]
    north = [jnp.where(row_y < cy - 1, n, 0.0) for n in north]
    south = [pltpu.roll(n, 1, 0) for n in north]

    own, x_low, x_high, y_low, y_high = [lane_of(coarse_rows, k) for k in range(5)]
    coarse_source = [
        (a + after_y(b)) + (before_y(c) + d + e)
        for a, b, c, d, e in zip(own, y_low, y_high, x_low[1:] + [nil], [nil] + x_high[:-1])]

    def dot(a, b):
        total = a[0] * b[0]
        for x in range(1, cx):
            total = total + a[x] * b[x]
        return jnp.sum(total, axis=0, keepdims=True)

    def coarse_apply(p):
        product = []
        for x in range(cx):
            v = diag[x] * p[x] - north[x] * pltpu.roll(p[x], cy - 1, 0) - south[x] * pltpu.roll(p[x], 1, 0)
            if x < cx - 1:
                v = v - east[x] * p[x + 1]
            if x > 0:
                v = v - east[x - 1] * p[x - 1]
            product.append(v)
        return product

    def iterate_once(counter, carried):
        estimate, remainder, search, norm_now = carried
        product = coarse_apply(search)
        alpha = norm_now / dot(search, product)
        estimate = [e + alpha * s for e, s in zip(estimate, search)]
        remainder = [r - alpha * q for r, q in zip(remainder, product)]
        norm_next = dot(remainder, remainder)
        beta = norm_next / norm_now
        search = [r + beta * s for r, s in zip(remainder, search)]
        return estimate, remainder, search, norm_next

    state = ([jnp.zeros((cy, 128), jnp.float32)] * cx, coarse_source, coarse_source,
             dot(coarse_source, coarse_source))
    estimate = lax.fori_loop(0, CG_ITERS, iterate_once, state)[0]
    for x in range(cx):
        E[x] = estimate[x]

    ring = lax.broadcasted_iota(jnp.int32, (Y, 128), 0)

    def share(dx):
        def one(dy):
            jx, jy = ix + dx, iy + dy
            row = E[jnp.clip(jx, 0, cx - 1), pl.ds(jnp.clip(jy, 0, cy - 1), 1), :]
            keep = inside(jx, jy, cx, cy).astype(jnp.float32)
            return jnp.broadcast_to(row * keep, (Y, 128))
        return jnp.where(ring < ny, one(0), jnp.where(ring < ny + H, one(1), one(-1)))

    shares = {dx: share(dx) for dx in (-1, 0, 1)}

    for d in range(8):
        each(d, -1, lambda d=d: halo2(d).wait_recv())
    for d in range(8):
        each(d, 1, lambda d=d: halo2(d).wait_send())

    def edge(x, dx):
        V[x, ny:ny + H, :] = YHI2[x]
        V[x, ny + H:Y, :] = YLO2[x]
        V[x] = V[x] + shares[dx]

    for i in range(NU):
        V[1 + i, 0:ny, :] = XLO2[i]
        V[X - H + i, 0:ny, :] = XHI2[i]
    for i in range(NU):
        edge(1 + i, -1)
        edge(X - H + i, 1)

    def middle(x, c):
        edge(x, 0)
        return c

    rows_loop(H, H + nx, middle, 0)

    sweep(V, U, 2, X - 2)
    sweep(U, V, 3, X - 3)
    sweep(V, out, H, H + nx, last=True)

    for d in range(8):
        def sent(d=d):
            for a in range(3):
                halo(a, d).wait_send()
        each(d, 1, sent)
    if direct:
        run(to_all, cx * cy, "wait_send")
    else:
        run(sum_x, cx, "wait_send")
        run(sum_y, cy, "wait_send")


def body(conductivity, source, initial):
    nx, ny, nz = conductivity.shape
    cx, cy = lax.axis_size("gx"), lax.axis_size("gy")
    X, Y = nx + 2 * H, ny + 2 * H
    args = (conductivity, source, initial)
    thin = tuple(a.reshape(nx, ny, 1, nz) for a in args)
    wide = pltpu.VMEM((X, Y, nz), jnp.float32)
    dma = pltpu.SemaphoreType.DMA

    def vmem(*shape):
        return pltpu.VMEM(shape, jnp.float32)

    return pl.pallas_call(
        functools.partial(kernel, cx, cy, nx, ny),
        out_shape=vmem(nx, ny, nz),
        in_specs=[pl.BlockSpec(memory_space=pltpu.HBM)] * 6,
        out_specs=pl.BlockSpec(memory_space=pltpu.VMEM),
        scratch_shapes=[wide] * 9 + [
            *[vmem(X, w, 1, nz) for w in WIDTH + WIDTH],
            vmem(NU, ny, nz), vmem(NU, ny, nz), vmem(X, H, nz), vmem(X, H, nz),
            vmem(nx, H, nz), vmem(nx, H, nz),
            vmem(cy, cx, 1, nz), vmem(cx, cy, nz), vmem(cx, cy, nz),
            dma((3,)),
            dma((24,)), dma((24,)), dma((8,)), dma((8,)),
            dma((cx - 1,)), dma((cx - 1,)), dma((cy - 1,)), dma((cy - 1,)),
            dma((min(cx * cy, DIRECT) - 1,)), dma((min(cx * cy, DIRECT) - 1,)),
            pltpu.SemaphoreType.REGULAR((cx - 1,)),
        ],
        compiler_params=pltpu.CompilerParams(collective_id=0, has_side_effects=True),
        name="cycle",
    )(*args, *thin)


def solution(mesh):
    return jax.shard_map(
        body,
        mesh=mesh,
        in_specs=(P("gx", "gy", None), P("gx", "gy", None), P("gx", "gy", None)),
        out_specs=P("gx", "gy", None),
        check_vma=False,
    )
```

```python
import functools

import jax
import jax.numpy as jnp
from jax import lax
from jax.experimental import pallas as pl
from jax.experimental.pallas import tpu as pltpu
from jax.sharding import PartitionSpec as P

NU = 3
CG_ITERS = 32
H = NU + 1
G = NU
WIDTH = (NU, NU - 1, NU)

relax_weight = 0.8
MESH = pl.DeviceIdType.MESH
DIRS = [(1, 0), (-1, 0), (0, 1), (0, -1), (1, 1), (1, -1), (-1, 1), (-1, -1)]


def inside(ix, iy, cx, cy):
    return (ix >= 0) & (ix < cx) & (iy >= 0) & (iy < cy)


def rows_loop(lo, hi, step, carry):
    count = hi - lo
    pairs = count // 2

    def two(i, c):
        x = lo + 2 * i
        return step(x + 1, step(x, c))

    carry = lax.fori_loop(0, pairs, two, carry)
    if count % 2:
        carry = step(hi - 1, carry)
    return carry


ROWS = 8
DIRECT = 64


def blocks_loop(lo, hi, block, carry):
    count = (hi - lo) // ROWS
    carry = lax.fori_loop(0, count, lambda i, c: block(lo + ROWS * i, c, ROWS), carry)
    if (hi - lo) % ROWS:
        carry = block(lo + ROWS * count, carry, (hi - lo) % ROWS)
    return carry


def kernel(cx, cy, nx, ny, *refs):
    (k_in, f_in, u_in, k1, f1, u1, out,
     K, F, L0, L1, L2, L3, L4, L5, L6, CE, CN, CS, CU, CD, W, SK, SF, SU,
     YLO_K, YLO_F, YLO_U, YHI_K, YHI_F, YHI_U, XLO_K, XLO_F, XLO_U, XHI_K, XHI_F, XHI_U,
     XLO2, XHI2, YLO2, YHI2, QLO, QHI, PLO, PHI, GS, E, R,
     lsem, ssem, rsem, ssem2, rsem2,
     s1s, s1r, s2s, s2r, das, dar, chain) = refs
    X = nx + 2 * H
    Y = ny + 8
    ix = lax.axis_index("gx")
    iy = lax.axis_index("gy")
    full = [k_in, f_in, u_in]
    thin = [k1, f1, u1]
    ext = [K, F, L0]
    stage = [SK, SF, SU]
    XLO = [XLO_K, XLO_F, XLO_U]
    XHI = [XHI_K, XHI_F, XHI_U]
    YLO = [YLO_K, YLO_F, YLO_U]
    YHI = [YHI_K, YHI_F, YHI_U]

    direct = cx * cy <= DIRECT
    barrier = pltpu.get_barrier_semaphore()

    def greet_x(k, c):
        pl.semaphore_signal(barrier, inc=1, device_id=(lax.rem(ix + k, cx), iy), device_id_type=MESH)
        return c

    def greet_y(k, c):
        pl.semaphore_signal(barrier, inc=1, device_id=(ix, lax.rem(iy + k, cy)), device_id_type=MESH)
        return c

    for dx, dy in (DIRS[:2] if direct else []) + DIRS[4:]:
        @pl.when(inside(ix + dx, iy + dy, cx, cy))
        def _(dx=dx, dy=dy):
            pl.semaphore_signal(barrier, inc=1, device_id=(ix + dx, iy + dy), device_id_type=MESH)
    if not direct:
        lax.fori_loop(1, cx, greet_x, 0)
    lax.fori_loop(1, cy, greet_y, 0)

    local = [pltpu.make_async_copy(full[a], stage[a], lsem.at[a]) for a in range(3)]
    for copy in local:
        copy.start()

    sides_x = (ix > 0).astype(jnp.int32) + (ix < cx - 1).astype(jnp.int32)
    sides_y = (iy > 0).astype(jnp.int32) + (iy < cy - 1).astype(jnp.int32)
    pl.semaphore_wait(barrier, (sides_x if direct else cx - 1) + (cy - 1) + sides_x * sides_y)

    def chain_signal(k):
        for dx in (1, -1):
            @pl.when((ix + dx >= 0) & (ix + dx < cx))
            def _(dx=dx):
                pl.semaphore_signal(chain.at[k], inc=1, device_id=(ix + dx, iy), device_id_type=MESH)

    def chain_wait(k):
        pl.semaphore_wait(chain.at[k], sides_x)

    def spans(dx, w):
        src = {1: (nx - w, nx), -1: (0, w), 0: (0, nx)}[dx]
        dst = {1: (H - w, H), -1: (X - H, X - H + w), 0: (H, H + nx)}[dx]
        return src, dst

    def halo(a, d):
        dx, dy = DIRS[d]
        slot = a * 8 + d
        w = WIDTH[a]
        src_rows, dst_rows = spans(dx, w)
        if dy == 0:
            src = full[a].at[src_rows[0]:src_rows[1]]
            dst = (XLO if dx == 1 else XHI)[a]
        else:
            cols = (ny - w, ny) if dy == 1 else (0, w)
            src = thin[a].at[src_rows[0]:src_rows[1], cols[0]:cols[1]]
            dst = (YLO if dy == 1 else YHI)[a].at[dst_rows[0]:dst_rows[1]]
        return pltpu.make_async_remote_copy(
            src_ref=src, dst_ref=dst, send_sem=ssem.at[slot], recv_sem=rsem.at[slot],
            device_id=(ix + dx, iy + dy), device_id_type=MESH)

    def each(d, sign, act):
        dx, dy = DIRS[d]
        pl.when(inside(ix + sign * dx, iy + sign * dy, cx, cy))(act)

    links = cx - 1 if direct else 0
    if links:
        chain_signal(0)
    for a in (0, 2, 1):
        for d in range(8):
            each(d, 1, lambda a=a, d=d: halo(a, d).start())

    def clear_when_absent(d):
        dx, dy = DIRS[d]

        @pl.when(jnp.logical_not(inside(ix - dx, iy - dy, cx, cy)))
        def _():
            for a in range(3):
                w = WIDTH[a]
                lo, hi = spans(dx, w)[1]
                if dy == 0:
                    (XLO if dx == 1 else XHI)[a][...] = jnp.zeros((w, ny, 128), jnp.float32)
                else:
                    (YLO if dy == 1 else YHI)[a][lo:hi] = jnp.zeros((hi - lo, w, 1, 128), jnp.float32)
            if dy == 0:
                (XLO2 if dx == 1 else XHI2)[...] = jnp.zeros((NU, ny, 128), jnp.float32)
            else:
                lo, hi = spans(dx, H)[1]
                (YLO2 if dy == 1 else YHI2)[lo:hi] = jnp.zeros((hi - lo, H, 128), jnp.float32)

    for d in range(8):
        clear_when_absent(d)

    for copy in local:
        copy.wait()

    def along_x(G, ss, rs):
        def of(k):
            return pltpu.make_async_remote_copy(
                src_ref=G.at[iy, ix], dst_ref=G.at[iy, ix], send_sem=ss.at[k - 1], recv_sem=rs.at[k - 1],
                device_id=(lax.rem(ix + k, cx), iy), device_id_type=MESH)
        return of

    def along_y(G, ss, rs):
        def of(k):
            return pltpu.make_async_remote_copy(
                src_ref=G.at[iy], dst_ref=G.at[iy], send_sem=ss.at[k - 1], recv_sem=rs.at[k - 1],
                device_id=(ix, lax.rem(iy + k, cy)), device_id_type=MESH)
        return of

    def around(i, k, count):
        return jnp.where(i + k < count, i + k, i + k - count)

    def to_all(method):
        for kx in range(cx):
            for ky in range(cy):
                k = kx * cy + ky
                if k:
                    copy = pltpu.make_async_remote_copy(
                        src_ref=GS.at[iy, ix], dst_ref=GS.at[iy, ix], send_sem=das.at[k - 1], recv_sem=dar.at[k - 1],
                        device_id=(around(ix, kx, cx), around(iy, ky, cy)), device_id_type=MESH)
                    getattr(copy, method)()

    def run(of, count, method):
        def go(k, c):
            getattr(of(k), method)()
            return c
        lax.fori_loop(1, count, go, 0)

    sum_x, sum_y = along_x(GS, s1s, s1r), along_y(GS, s2s, s2r)

    lane_row = lax.broadcasted_iota(jnp.int32, (1, 128), 1)

    def whole(v):
        return jnp.sum(jnp.sum(v, axis=0, keepdims=True), axis=1, keepdims=True)

    def in_lanes(values):
        row = jnp.zeros((1, 128), jnp.float32)
        for k, v in enumerate(values):
            row = jnp.where(lane_row == k, v, row)
        return row

    def place(x, c):
        for a in range(3):
            ext[a][x, G:G + ny, :] = stage[a][x - H]
        return c

    rows_loop(H, H + nx, place, 0)

    lane = lax.broadcasted_iota(jnp.int32, (Y, 128), 1)
    up_half = jnp.where(lane < 127, 0.5, 0.0)
    down_half = jnp.where(lane > 0, 0.5, 0.0)
    ALL, LOW, HIGH = (0, Y), (0, 8), (Y - 8, Y)

    def at(ref, x, g):
        return ref[x] if g == ALL else ref[x, g[0]:g[1], :]

    def put(ref, x, g, v):
        if g == ALL:
            ref[x] = v
        else:
            ref[x, g[0]:g[1], :] = v

    def next_y(ref, x, g, v):
        return pltpu.roll(v, g[1] - g[0] - 1, 0) if g[1] == Y else ref[x, g[0] + 1:g[1] + 1, :]

    def last_y(ref, x, g, v):
        return pltpu.roll(v, 1, 0) if g[0] == 0 else ref[x, g[0] - 1:g[1] - 1, :]

    def next_z(v):
        return pltpu.roll(v, 127, 1)

    def last_z(v):
        return pltpu.roll(v, 1, 1)

    def faces_at(g):
        n = g[1] - g[0]

        def block(x, c, rows):
            k, west = c
            ks = [k] + [at(K, x + 1 + r, g) for r in range(rows)]
            ups = [next_z(ks[r]) for r in range(rows)]
            downs = [last_z(ks[r]) for r in range(rows)]
            for r in range(rows):
                k = ks[r]
                east = 0.5 * (k + ks[r + 1])
                north = 0.5 * (k + next_y(K, x + r, g, k))
                south = 0.5 * (k + last_y(K, x + r, g, k))
                up = up_half[0:n] * (k + ups[r])
                down = down_half[0:n] * (k + downs[r])
                d = east + west + north + south + up + down
                put(CE, x + r, g, east)
                put(CN, x + r, g, north)
                put(CS, x + r, g, south)
                put(CU, x + r, g, up)
                put(CD, x + r, g, down)
                put(W, x + r, g, jnp.where(k > 0, relax_weight / jnp.where(k > 0, d, 1.0), 0.0))
                west = east
            return ks[rows], west
        return block

    def faces(lo, hi, slabs):
        def start(g):
            k, before = at(K, lo, g), at(K, lo - 1, g)
            west = 0.5 * (k + before)
            put(CE, lo - 1, g, west)
            return k, west

        def block(x, c, rows):
            return tuple(faces_at(g)(x, v, rows) for g, v in zip(slabs, c))

        blocks_loop(lo, hi, block, tuple(start(g) for g in slabs))

    def sweep_at(src, dst, g):
        def block(x, c, rows):
            u, west = c
            us = [u] + [at(src, x + 1 + r, g) for r in range(rows)]
            ups = [next_z(us[r]) for r in range(rows)]
            downs = [last_z(us[r]) for r in range(rows)]
            for r in range(rows):
                u = us[r]
                east = at(CE, x + r, g) * (us[r + 1] - u)
                north = at(CN, x + r, g) * (next_y(src, x + r, g, u) - u)
                if g == ALL:
                    south = pltpu.roll(north, 1, 0)
                else:
                    south = at(CS, x + r, g) * (u - last_y(src, x + r, g, u))
                change = ((east - west) + (north - south)
                          + (at(CU, x + r, g) * (ups[r] - u) + at(CD, x + r, g) * (downs[r] - u)))
                put(dst, x + r, g, u + at(W, x + r, g) * (at(F, x + r, g) + change))
                west = east
            return us[rows], west
        return block

    def sweep(src, dst, lo, hi, slabs):
        def start(g):
            u = at(src, lo, g)
            return u, at(CE, lo - 1, g) * (u - at(src, lo - 1, g))

        def block(x, c, rows):
            return tuple(sweep_at(src, dst, g)(x, v, rows) for g, v in zip(slabs, c))

        blocks_loop(lo, hi, block, tuple(start(g) for g in slabs))

    def interior(src, dst, s):
        sweep(src, dst, H + s, H + nx - s, [ALL])

    def rims(src, dst, s):
        for lo in (H - NU + s, H + nx - s):
            sweep(src, dst, lo, lo + NU, [ALL])
        sweep(src, dst, H + s, H + nx - s, [LOW, HIGH])

    faces(H + 1, H + nx - 1, [ALL])

    for k in range(links):
        chain_wait(k)
        if k + 1 < links:
            chain_signal(k + 1)
        if k == 0:
            interior(L0, L1, 1)
        if k == 1:
            interior(L1, L2, 2)
    if links < 1:
        interior(L0, L1, 1)
    if links < 2:
        interior(L1, L2, 2)
    interior(L2, L3, 3)

    def outer(x, c):
        return c[0] + SK[x, 0:1, :], c[1] + SK[x, ny - 1:ny, :]

    none = jnp.zeros((1, 128), jnp.float32)
    y_first, y_last = rows_loop(0, nx, outer, (none, none))
    edges = [whole(SK[0]), whole(SK[nx - 1]), whole(y_first), whole(y_last)]
    f_total = rows_loop(0, nx, lambda x, c: c + SF[x], jnp.zeros((ny, 128), jnp.float32))
    f_total = jnp.sum(f_total, axis=0, keepdims=True)

    def unpack(arrays):
        def one(x, c):
            for a in arrays:
                w = WIDTH[a]
                ext[a][x, G + ny:G + ny + w, :] = YHI[a][x, :, 0, :]
                ext[a][x, G - w:G, :] = YLO[a][x, :, 0, :]
            return c

        rows_loop(1, X - 1, one, 0)
        for a in arrays:
            w = WIDTH[a]
            for i in range(w):
                ext[a][H - w + i, G:G + ny, :] = XLO[a][i]
                ext[a][H + nx + i, G:G + ny, :] = XHI[a][i]

    for d in range(8):
        each(d, -1, lambda d=d: halo(0, d).wait_recv())
    unpack([0])
    for lo in (H - NU + 1, H + nx - 1):
        faces(lo, lo + NU, [ALL])
    faces(H + 1, H + nx - 1, [LOW, HIGH])
    for a in (2, 1):
        for d in range(8):
            each(d, -1, lambda a=a, d=d: halo(a, d).wait_recv())
    unpack([2, 1])
    rims(L0, L1, 1)
    rims(L1, L2, 2)
    rims(L2, L3, 3)

    def sides(x, c):
        return c[0] + CS[x, 0:8, :] * L3[x, 0:8, :], c[1] + CN[x, Y - 8:Y, :] * L3[x, Y - 8:Y, :]

    none = jnp.zeros((8, 128), jnp.float32)
    y_low, y_high = rows_loop(H, H + nx, sides, (none, none))
    y_low, y_high = y_low[G:G + 1], y_high[G - 1:G]
    x_low = jnp.sum(CE[H - 1, G:G + ny, :] * L3[H, G:G + ny, :], axis=0, keepdims=True)
    x_high = jnp.sum(CE[X - H - 1, G:G + ny, :] * L3[X - H - 1, G:G + ny, :], axis=0, keepdims=True)
    own = f_total - x_low - x_high - y_low - y_high
    GS[iy, ix] = in_lanes([whole(v) for v in (own, x_low, x_high, y_low, y_high)] + edges)
    if direct:
        to_all("start")
    else:
        run(sum_x, cx, "start")

    def pack(x, c):
        PLO[x] = L3[H + x, G:G + H, :]
        PHI[x] = L3[H + x, G + ny - H:G + ny, :]
        return c

    rows_loop(0, nx, pack, 0)
    for i in range(NU):
        QLO[i] = L3[H + i, G:G + ny, :]
        QHI[i] = L3[H + nx - NU + i, G:G + ny, :]

    def halo2(d):
        dx, dy = DIRS[d]
        src_rows = {1: (nx - H, nx), -1: (0, H), 0: (0, nx)}[dx]
        dst_rows = {1: (0, H), -1: (X - H, X), 0: (H, H + nx)}[dx]
        if dy == 0:
            src = QHI if dx == 1 else QLO
            dst = XLO2 if dx == 1 else XHI2
        else:
            src = (PHI if dy == 1 else PLO).at[src_rows[0]:src_rows[1]]
            dst = (YLO2 if dy == 1 else YHI2).at[dst_rows[0]:dst_rows[1]]
        return pltpu.make_async_remote_copy(
            src_ref=src, dst_ref=dst, send_sem=ssem2.at[d], recv_sem=rsem2.at[d],
            device_id=(ix + dx, iy + dy), device_id_type=MESH)

    if not direct:
        run(sum_x, cx, "wait_recv")
        run(sum_y, cy, "start")
    for d in range(8):
        each(d, 1, lambda d=d: halo2(d).start())
    interior(L3, L4, 1)
    interior(L4, L5, 2)
    interior(L5, L6, 3)

    row_y = lax.broadcasted_iota(jnp.int32, (cy, 128), 0)

    def tidy(G):
        for x in range(cx):
            for y in range(cy):
                R[x, y:y + 1, :] = G[y, x]
        return [R[x] for x in range(cx)]

    def lane_of(rows, k):
        return [jnp.broadcast_to(r[:, k:k + 1], (cy, 128)) for r in rows]

    def after_y(v):
        return jnp.where(row_y < cy - 1, pltpu.roll(v, cy - 1, 0), 0.0)

    def before_y(v):
        return jnp.where(row_y > 0, pltpu.roll(v, 1, 0), 0.0)

    if direct:
        to_all("wait_recv")
    else:
        run(sum_y, cy, "wait_recv")
    coarse_rows = tidy(GS)
    nil = jnp.zeros((cy, 128), jnp.float32)
    x_first, x_last, y_first, y_last = [lane_of(coarse_rows, k) for k in range(5, 9)]
    east = [0.5 * (a + b) for a, b in zip(x_last, x_first[1:] + [nil])]
    west = [0.5 * (a + b) for a, b in zip(x_first, [nil] + x_last[:-1])]
    north = [0.5 * (a + after_y(b)) for a, b in zip(y_last, y_first)]
    south = [0.5 * (a + before_y(b)) for a, b in zip(y_first, y_last)]
    diag = [a + b + c + d for a, b, c, d in zip(east, west, north, south)]
    north = [jnp.where(row_y < cy - 1, n, 0.0) for n in north]
    south = [pltpu.roll(n, 1, 0) for n in north]

    own, x_low, x_high, y_low, y_high = [lane_of(coarse_rows, k) for k in range(5)]
    coarse_source = [
        (a + after_y(b)) + (before_y(c) + d + e)
        for a, b, c, d, e in zip(own, y_low, y_high, x_low[1:] + [nil], [nil] + x_high[:-1])]

    def dot(a, b):
        total = a[0] * b[0]
        for x in range(1, cx):
            total = total + a[x] * b[x]
        return jnp.sum(total, axis=0, keepdims=True)

    def coarse_apply(p):
        product = []
        for x in range(cx):
            v = diag[x] * p[x] - north[x] * pltpu.roll(p[x], cy - 1, 0) - south[x] * pltpu.roll(p[x], 1, 0)
            if x < cx - 1:
                v = v - east[x] * p[x + 1]
            if x > 0:
                v = v - east[x - 1] * p[x - 1]
            product.append(v)
        return product

    def iterate_once(counter, carried):
        estimate, remainder, search, norm_now = carried
        product = coarse_apply(search)
        alpha = norm_now / dot(search, product)
        estimate = [e + alpha * s for e, s in zip(estimate, search)]
        remainder = [r - alpha * q for r, q in zip(remainder, product)]
        norm_next = dot(remainder, remainder)
        beta = norm_next / norm_now
        search = [r + beta * s for r, s in zip(remainder, search)]
        return estimate, remainder, search, norm_next

    state = ([jnp.zeros((cy, 128), jnp.float32)] * cx, coarse_source, coarse_source,
             dot(coarse_source, coarse_source))
    estimate = lax.fori_loop(0, CG_ITERS, iterate_once, state)[0]
    for x in range(cx):
        E[x] = estimate[x]

    own_share = E[ix, pl.ds(iy, 1), :]

    def share(dx, dy):
        jx, jy = ix + dx, iy + dy
        row = E[jnp.clip(jx, 0, cx - 1), pl.ds(jnp.clip(jy, 0, cy - 1), 1), :]
        return row * inside(jx, jy, cx, cy).astype(jnp.float32) - own_share

    for d in range(8):
        each(d, -1, lambda d=d: halo2(d).wait_recv())

    def edge(x, low, high):
        L3[x, 0:G, :] = YLO2[x, H - G:H, :] + low
        L3[x, G + ny:G + ny + NU, :] = YHI2[x, 0:NU, :] + high

    for dx, lo, got in ((-1, H - NU, XLO2), (1, H + nx, XHI2)):
        low, middle, high = [share(dx, dy) for dy in (-1, 0, 1)]
        for i in range(NU):
            L3[lo + i, G:G + ny, :] = got[i] + middle
            edge(lo + i, low, high)
    low, high = share(0, -1), share(0, 1)

    def inner(x, c):
        edge(x, low, high)
        return c

    rows_loop(H, H + nx, inner, 0)

    rims(L3, L4, 1)
    rims(L4, L5, 2)
    rims(L5, L6, 3)

    def give(x, c):
        out[x] = L6[H + x, G:G + ny, :] + own_share
        return c

    rows_loop(0, nx, give, 0)

    for d in range(8):
        each(d, 1, lambda d=d: halo2(d).wait_send())
    for d in range(8):
        def sent(d=d):
            for a in range(3):
                halo(a, d).wait_send()
        each(d, 1, sent)
    if direct:
        to_all("wait_send")
    else:
        run(sum_x, cx, "wait_send")
        run(sum_y, cy, "wait_send")


def body(conductivity, source, initial):
    nx, ny, nz = conductivity.shape
    cx, cy = lax.axis_size("gx"), lax.axis_size("gy")
    X, Y = nx + 2 * H, ny + 8
    args = (conductivity, source, initial)
    thin = tuple(a.reshape(nx, ny, 1, nz) for a in args)
    wide = pltpu.VMEM((X, Y, nz), jnp.float32)
    dma = pltpu.SemaphoreType.DMA

    def vmem(*shape):
        return pltpu.VMEM(shape, jnp.float32)

    return pl.pallas_call(
        functools.partial(kernel, cx, cy, nx, ny),
        out_shape=vmem(nx, ny, nz),
        in_specs=[pl.BlockSpec(memory_space=pltpu.HBM)] * 6,
        out_specs=pl.BlockSpec(memory_space=pltpu.VMEM),
        scratch_shapes=[wide] * 15 + [
            *[vmem(nx, ny, nz)] * 3,
            *[vmem(X, w, 1, nz) for w in WIDTH + WIDTH],
            *[vmem(w, ny, nz) for w in WIDTH + WIDTH],
            vmem(NU, ny, nz), vmem(NU, ny, nz), vmem(X, H, nz), vmem(X, H, nz), vmem(NU, ny, nz), vmem(NU, ny, nz),
            vmem(nx, H, nz), vmem(nx, H, nz),
            vmem(cy, cx, 1, nz), vmem(cx, cy, nz), vmem(cx, cy, nz),
            dma((3,)),
            dma((24,)), dma((24,)), dma((8,)), dma((8,)),
            dma((cx - 1,)), dma((cx - 1,)), dma((cy - 1,)), dma((cy - 1,)),
            dma((min(cx * cy, DIRECT) - 1,)), dma((min(cx * cy, DIRECT) - 1,)),
            pltpu.SemaphoreType.REGULAR((cx - 1,)),
        ],
        compiler_params=pltpu.CompilerParams(collective_id=0, has_side_effects=True),
        name="cycle",
    )(*args, *thin)


def solution(mesh):
    return jax.shard_map(
        body,
        mesh=mesh,
        in_specs=(P("gx", "gy", None), P("gx", "gy", None), P("gx", "gy", None)),
        out_specs=P("gx", "gy", None),
        check_vma=False,
    )
```

```python
import functools

import jax
import jax.numpy as jnp
from jax import lax
from jax.experimental import pallas as pl
from jax.experimental.pallas import tpu as pltpu
from jax.sharding import PartitionSpec as P

NU = 3
CG_ITERS = 32
H = NU + 1
G = NU
WIDTH = (NU, NU - 1, NU)

relax_weight = 0.8
MESH = pl.DeviceIdType.MESH
DIRS = [(1, 0), (-1, 0), (0, 1), (0, -1), (1, 1), (1, -1), (-1, 1), (-1, -1)]


def inside(ix, iy, cx, cy):
    return (ix >= 0) & (ix < cx) & (iy >= 0) & (iy < cy)


UNROLL = 16


def rows_loop(lo, hi, step, carry):
    count = (hi - lo) // UNROLL

    def several(i, c):
        for r in range(UNROLL):
            c = step(lo + UNROLL * i + r, c)
        return c

    if count:
        carry = lax.fori_loop(0, count, several, carry)
    for x in range(lo + UNROLL * count, hi):
        carry = step(x, carry)
    return carry


ROWS = 16
DIRECT = 64


def blocks_loop(lo, hi, block, carry):
    count = (hi - lo) // ROWS
    if count > 1:
        carry = lax.fori_loop(0, count, lambda i, c: block(lo + ROWS * i, c, ROWS), carry)
    elif count:
        carry = block(lo, carry, ROWS)
    if (hi - lo) % ROWS:
        carry = block(lo + ROWS * count, carry, (hi - lo) % ROWS)
    return carry


def kernel(cx, cy, nx, ny, *refs):
    (k_in, f_in, u_in, k1, f1, u1, out,
     K, F, L0, L1, L2, L3, L4, L5, L6, CE, CN, CS, CU, CD, W, SK, SF, SU,
     YLO_K, YLO_F, YLO_U, YHI_K, YHI_F, YHI_U, XLO_K, XLO_F, XLO_U, XHI_K, XHI_F, XHI_U,
     XLO2, XHI2, YLO2, YHI2, QLO, QHI, PLO, PHI, GS, E, R,
     lsem, ssem, rsem, ssem2, rsem2,
     s1s, s1r, s2s, s2r, das, dar, chain) = refs
    X = nx + 2 * H
    Y = ny + 8
    ix = lax.axis_index("gx")
    iy = lax.axis_index("gy")
    full = [k_in, f_in, u_in]
    thin = [k1, f1, u1]
    ext = [K, F, L0]
    stage = [SK, SF, SU]
    XLO = [XLO_K, XLO_F, XLO_U]
    XHI = [XHI_K, XHI_F, XHI_U]
    YLO = [YLO_K, YLO_F, YLO_U]
    YHI = [YHI_K, YHI_F, YHI_U]

    direct = cx * cy <= DIRECT
    barrier = pltpu.get_barrier_semaphore()

    def greet_x(k, c):
        pl.semaphore_signal(barrier, inc=1, device_id=(lax.rem(ix + k, cx), iy), device_id_type=MESH)
        return c

    def greet_y(k, c):
        pl.semaphore_signal(barrier, inc=1, device_id=(ix, lax.rem(iy + k, cy)), device_id_type=MESH)
        return c

    for dx, dy in (DIRS[:2] if direct else []) + DIRS[4:]:
        @pl.when(inside(ix + dx, iy + dy, cx, cy))
        def _(dx=dx, dy=dy):
            pl.semaphore_signal(barrier, inc=1, device_id=(ix + dx, iy + dy), device_id_type=MESH)
    if not direct:
        lax.fori_loop(1, cx, greet_x, 0)
    lax.fori_loop(1, cy, greet_y, 0)

    local = [pltpu.make_async_copy(full[a], stage[a], lsem.at[a]) for a in range(3)]
    for copy in local:
        copy.start()

    sides_x = (ix > 0).astype(jnp.int32) + (ix < cx - 1).astype(jnp.int32)
    sides_y = (iy > 0).astype(jnp.int32) + (iy < cy - 1).astype(jnp.int32)
    pl.semaphore_wait(barrier, (sides_x if direct else cx - 1) + (cy - 1) + sides_x * sides_y)

    def chain_signal(k):
        for dx in (1, -1):
            @pl.when((ix + dx >= 0) & (ix + dx < cx))
            def _(dx=dx):
                pl.semaphore_signal(chain.at[k], inc=1, device_id=(ix + dx, iy), device_id_type=MESH)

    def chain_wait(k):
        pl.semaphore_wait(chain.at[k], sides_x)

    def spans(dx, w):
        src = {1: (nx - w, nx), -1: (0, w), 0: (0, nx)}[dx]
        dst = {1: (H - w, H), -1: (X - H, X - H + w), 0: (H, H + nx)}[dx]
        return src, dst

    def halo(a, d):
        dx, dy = DIRS[d]
        slot = a * 8 + d
        w = WIDTH[a]
        src_rows, dst_rows = spans(dx, w)
        if dy == 0:
            src = full[a].at[src_rows[0]:src_rows[1]]
            dst = (XLO if dx == 1 else XHI)[a]
        else:
            cols = (ny - w, ny) if dy == 1 else (0, w)
            src = thin[a].at[src_rows[0]:src_rows[1], cols[0]:cols[1]]
            dst = (YLO if dy == 1 else YHI)[a].at[dst_rows[0]:dst_rows[1]]
        return pltpu.make_async_remote_copy(
            src_ref=src, dst_ref=dst, send_sem=ssem.at[slot], recv_sem=rsem.at[slot],
            device_id=(ix + dx, iy + dy), device_id_type=MESH)

    def each(d, sign, act):
        dx, dy = DIRS[d]
        pl.when(inside(ix + sign * dx, iy + sign * dy, cx, cy))(act)

    links = cx - 1 if direct else 0
    if links:
        chain_signal(0)
    for d in range(4, 8):
        def start(d=d):
            for a in (0, 2, 1):
                halo(a, d).start()
        each(d, 1, start)
    for a in (0, 2, 1):
        for d in range(4):
            each(d, 1, lambda a=a, d=d: halo(a, d).start())

    def clear_when_absent(d):
        dx, dy = DIRS[d]

        @pl.when(jnp.logical_not(inside(ix - dx, iy - dy, cx, cy)))
        def _():
            for a in range(3):
                w = WIDTH[a]
                lo, hi = spans(dx, w)[1]
                if dy == 0:
                    (XLO if dx == 1 else XHI)[a][...] = jnp.zeros((w, ny, 128), jnp.float32)
                else:
                    (YLO if dy == 1 else YHI)[a][lo:hi] = jnp.zeros((hi - lo, w, 1, 128), jnp.float32)
            if dy == 0:
                (XLO2 if dx == 1 else XHI2)[...] = jnp.zeros((NU, ny, 128), jnp.float32)
            else:
                lo, hi = spans(dx, H)[1]
                (YLO2 if dy == 1 else YHI2)[lo:hi] = jnp.zeros((hi - lo, H, 128), jnp.float32)

    for d in range(8):
        clear_when_absent(d)

    for copy in local:
        copy.wait()

    def along_x(G, ss, rs):
        def of(k):
            return pltpu.make_async_remote_copy(
                src_ref=G.at[iy, ix], dst_ref=G.at[iy, ix], send_sem=ss.at[k - 1], recv_sem=rs.at[k - 1],
                device_id=(lax.rem(ix + k, cx), iy), device_id_type=MESH)
        return of

    def along_y(G, ss, rs):
        def of(k):
            return pltpu.make_async_remote_copy(
                src_ref=G.at[iy], dst_ref=G.at[iy], send_sem=ss.at[k - 1], recv_sem=rs.at[k - 1],
                device_id=(ix, lax.rem(iy + k, cy)), device_id_type=MESH)
        return of

    def around(i, k, count):
        return jnp.where(i + k < count, i + k, i + k - count)

    def to_all(method):
        for kx in [*range(1, cx), 0]:
            for ky in range(cy):
                k = kx * cy + ky
                if k:
                    copy = pltpu.make_async_remote_copy(
                        src_ref=GS.at[iy, ix], dst_ref=GS.at[iy, ix], send_sem=das.at[k - 1], recv_sem=dar.at[k - 1],
                        device_id=(around(ix, kx, cx), around(iy, ky, cy)), device_id_type=MESH)
                    getattr(copy, method)()

    def run(of, count, method):
        def go(k, c):
            getattr(of(k), method)()
            return c
        lax.fori_loop(1, count, go, 0)

    sum_x, sum_y = along_x(GS, s1s, s1r), along_y(GS, s2s, s2r)

    lane_row = lax.broadcasted_iota(jnp.int32, (1, 128), 1)

    def whole(v):
        return jnp.sum(jnp.sum(v, axis=0, keepdims=True), axis=1, keepdims=True)

    def in_lanes(values):
        row = jnp.zeros((1, 128), jnp.float32)
        for k, v in enumerate(values):
            row = jnp.where(lane_row == k, v, row)
        return row

    def place(x, c):
        for a in range(3):
            ext[a][x, G:G + ny, :] = stage[a][x - H]
        return c

    rows_loop(H, H + nx, place, 0)

    lane = lax.broadcasted_iota(jnp.int32, (Y, 128), 1)
    up_half = jnp.where(lane < 127, 0.5, 0.0)
    down_half = jnp.where(lane > 0, 0.5, 0.0)
    ALL, LOW, HIGH = (0, Y), (0, 8), (Y - 8, Y)

    def at(ref, x, g):
        return ref[x] if g == ALL else ref[x, g[0]:g[1], :]

    def put(ref, x, g, v):
        if g == ALL:
            ref[x] = v
        else:
            ref[x, g[0]:g[1], :] = v

    def next_y(ref, x, g, v):
        return pltpu.roll(v, g[1] - g[0] - 1, 0) if g[1] == Y else ref[x, g[0] + 1:g[1] + 1, :]

    def last_y(ref, x, g, v):
        return pltpu.roll(v, 1, 0) if g[0] == 0 else ref[x, g[0] - 1:g[1] - 1, :]

    def next_z(v):
        return pltpu.roll(v, 127, 1)

    def last_z(v):
        return pltpu.roll(v, 1, 1)

    def faces_at(g):
        n = g[1] - g[0]

        def block(x, c, rows):
            k, west = c
            ks = [k] + [at(K, x + 1 + r, g) for r in range(rows)]
            ups = [next_z(ks[r]) for r in range(rows)]
            downs = [last_z(ks[r]) for r in range(rows)]
            for r in range(rows):
                k = ks[r]
                east = 0.5 * (k + ks[r + 1])
                north = 0.5 * (k + next_y(K, x + r, g, k))
                south = 0.5 * (k + last_y(K, x + r, g, k))
                up = up_half[0:n] * (k + ups[r])
                down = down_half[0:n] * (k + downs[r])
                d = east + west + north + south + up + down
                put(CE, x + r, g, east)
                put(CN, x + r, g, north)
                put(CS, x + r, g, south)
                put(CU, x + r, g, up)
                put(CD, x + r, g, down)
                put(W, x + r, g, jnp.where(k > 0, relax_weight / jnp.where(k > 0, d, 1.0), 0.0))
                west = east
            return ks[rows], west
        return block

    def faces(lo, hi, slabs):
        def start(g):
            k, before = at(K, lo, g), at(K, lo - 1, g)
            west = 0.5 * (k + before)
            put(CE, lo - 1, g, west)
            return k, west

        def block(x, c, rows):
            return tuple(faces_at(g)(x, v, rows) for g, v in zip(slabs, c))

        blocks_loop(lo, hi, block, tuple(start(g) for g in slabs))

    def sweep_at(src, dst, g):
        def block(x, c, rows):
            u, west = c
            us = [u] + [at(src, x + 1 + r, g) for r in range(rows)]
            ups = [next_z(us[r]) for r in range(rows)]
            downs = [last_z(us[r]) for r in range(rows)]
            for r in range(rows):
                u = us[r]
                east = at(CE, x + r, g) * (us[r + 1] - u)
                north = at(CN, x + r, g) * (next_y(src, x + r, g, u) - u)
                if g == ALL:
                    south = pltpu.roll(north, 1, 0)
                else:
                    south = at(CS, x + r, g) * (u - last_y(src, x + r, g, u))
                change = ((east - west) + (north - south)
                          + (at(CU, x + r, g) * (ups[r] - u) + at(CD, x + r, g) * (downs[r] - u)))
                put(dst, x + r, g, u + at(W, x + r, g) * (at(F, x + r, g) + change))
                west = east
            return us[rows], west
        return block

    def sweep(src, dst, lo, hi, slabs):
        def start(g):
            u = at(src, lo, g)
            return u, at(CE, lo - 1, g) * (u - at(src, lo - 1, g))

        def block(x, c, rows):
            return tuple(sweep_at(src, dst, g)(x, v, rows) for g, v in zip(slabs, c))

        blocks_loop(lo, hi, block, tuple(start(g) for g in slabs))

    def interior(src, dst, s):
        sweep(src, dst, H + s, H + nx - s, [ALL])

    def rims(src, dst, s):
        for lo in (H - NU + s, H + nx - s):
            sweep(src, dst, lo, lo + NU, [ALL])
        sweep(src, dst, H + s, H + nx - s, [LOW, HIGH])

    faces(H + 1, H + nx - 1, [ALL])

    for k in range(links):
        chain_wait(k)
        if k + 1 < links:
            chain_signal(k + 1)
        if k == 0:
            interior(L0, L1, 1)
        if k == 1:
            interior(L1, L2, 2)
    if links < 1:
        interior(L0, L1, 1)
    if links < 2:
        interior(L1, L2, 2)
    interior(L2, L3, 3)

    def outer(x, c):
        return c[0] + SK[x, 0:1, :], c[1] + SK[x, ny - 1:ny, :]

    none = jnp.zeros((1, 128), jnp.float32)
    y_first, y_last = rows_loop(0, nx, outer, (none, none))
    edges = [whole(SK[0]), whole(SK[nx - 1]), whole(y_first), whole(y_last)]
    f_total = rows_loop(0, nx, lambda x, c: c + SF[x], jnp.zeros((ny, 128), jnp.float32))
    f_total = jnp.sum(f_total, axis=0, keepdims=True)

    def unpack(arrays):
        def one(x, c):
            for a in arrays:
                w = WIDTH[a]
                ext[a][x, G + ny:G + ny + w, :] = YHI[a][x, :, 0, :]
                ext[a][x, G - w:G, :] = YLO[a][x, :, 0, :]
            return c

        rows_loop(1, X - 1, one, 0)
        for a in arrays:
            w = WIDTH[a]
            for i in range(w):
                ext[a][H - w + i, G:G + ny, :] = XLO[a][i]
                ext[a][H + nx + i, G:G + ny, :] = XHI[a][i]

    for d in range(8):
        each(d, -1, lambda d=d: halo(0, d).wait_recv())
    unpack([0])
    for lo in (H - NU + 1, H + nx - 1):
        faces(lo, lo + NU, [ALL])
    faces(H + 1, H + nx - 1, [LOW, HIGH])
    for a in (2, 1):
        for d in range(8):
            each(d, -1, lambda a=a, d=d: halo(a, d).wait_recv())
    unpack([2, 1])
    rims(L0, L1, 1)
    rims(L1, L2, 2)
    rims(L2, L3, 3)

    def sides(x, c):
        return c[0] + CS[x, 0:8, :] * L3[x, 0:8, :], c[1] + CN[x, Y - 8:Y, :] * L3[x, Y - 8:Y, :]

    none = jnp.zeros((8, 128), jnp.float32)
    y_low, y_high = rows_loop(H, H + nx, sides, (none, none))
    y_low, y_high = y_low[G:G + 1], y_high[G - 1:G]
    x_low = jnp.sum(CE[H - 1, G:G + ny, :] * L3[H, G:G + ny, :], axis=0, keepdims=True)
    x_high = jnp.sum(CE[X - H - 1, G:G + ny, :] * L3[X - H - 1, G:G + ny, :], axis=0, keepdims=True)
    own = f_total - x_low - x_high - y_low - y_high
    GS[iy, ix] = in_lanes([whole(v) for v in (own, x_low, x_high, y_low, y_high)] + edges)
    if direct:
        to_all("start")
    else:
        run(sum_x, cx, "start")

    def pack(x, c):
        PLO[x] = L3[H + x, G:G + H, :]
        PHI[x] = L3[H + x, G + ny - H:G + ny, :]
        return c

    rows_loop(0, nx, pack, 0)
    for i in range(NU):
        QLO[i] = L3[H + i, G:G + ny, :]
        QHI[i] = L3[H + nx - NU + i, G:G + ny, :]

    def halo2(d):
        dx, dy = DIRS[d]
        src_rows = {1: (nx - H, nx), -1: (0, H), 0: (0, nx)}[dx]
        dst_rows = {1: (0, H), -1: (X - H, X), 0: (H, H + nx)}[dx]
        if dy == 0:
            src = QHI if dx == 1 else QLO
            dst = XLO2 if dx == 1 else XHI2
        else:
            src = (PHI if dy == 1 else PLO).at[src_rows[0]:src_rows[1]]
            dst = (YLO2 if dy == 1 else YHI2).at[dst_rows[0]:dst_rows[1]]
        return pltpu.make_async_remote_copy(
            src_ref=src, dst_ref=dst, send_sem=ssem2.at[d], recv_sem=rsem2.at[d],
            device_id=(ix + dx, iy + dy), device_id_type=MESH)

    if not direct:
        run(sum_x, cx, "wait_recv")
        run(sum_y, cy, "start")
    for d in range(8):
        each(d, 1, lambda d=d: halo2(d).start())
    interior(L3, L4, 1)
    interior(L4, L5, 2)
    interior(L5, L6, 3)

    row_y = lax.broadcasted_iota(jnp.int32, (cy, 128), 0)

    def tidy(G):
        for x in range(cx):
            for y in range(cy):
                R[x, y:y + 1, :] = G[y, x]
        return [R[x] for x in range(cx)]

    def lane_of(rows, k):
        return [jnp.broadcast_to(r[:, k:k + 1], (cy, 128)) for r in rows]

    def after_y(v):
        return jnp.where(row_y < cy - 1, pltpu.roll(v, cy - 1, 0), 0.0)

    def before_y(v):
        return jnp.where(row_y > 0, pltpu.roll(v, 1, 0), 0.0)

    if direct:
        to_all("wait_recv")
    else:
        run(sum_y, cy, "wait_recv")
    coarse_rows = tidy(GS)
    nil = jnp.zeros((cy, 128), jnp.float32)
    x_first, x_last, y_first, y_last = [lane_of(coarse_rows, k) for k in range(5, 9)]
    east = [0.5 * (a + b) for a, b in zip(x_last, x_first[1:] + [nil])]
    west = [0.5 * (a + b) for a, b in zip(x_first, [nil] + x_last[:-1])]
    north = [0.5 * (a + after_y(b)) for a, b in zip(y_last, y_first)]
    south = [0.5 * (a + before_y(b)) for a, b in zip(y_first, y_last)]
    diag = [a + b + c + d for a, b, c, d in zip(east, west, north, south)]
    north = [jnp.where(row_y < cy - 1, n, 0.0) for n in north]
    south = [pltpu.roll(n, 1, 0) for n in north]

    own, x_low, x_high, y_low, y_high = [lane_of(coarse_rows, k) for k in range(5)]
    coarse_source = [
        (a + after_y(b)) + (before_y(c) + d + e)
        for a, b, c, d, e in zip(own, y_low, y_high, x_low[1:] + [nil], [nil] + x_high[:-1])]

    def dot(a, b):
        total = a[0] * b[0]
        for x in range(1, cx):
            total = total + a[x] * b[x]
        return jnp.sum(total, axis=0, keepdims=True)

    def coarse_apply(p):
        product = []
        for x in range(cx):
            v = diag[x] * p[x] - north[x] * pltpu.roll(p[x], cy - 1, 0) - south[x] * pltpu.roll(p[x], 1, 0)
            if x < cx - 1:
                v = v - east[x] * p[x + 1]
            if x > 0:
                v = v - east[x - 1] * p[x - 1]
            product.append(v)
        return product

    def iterate_once(counter, carried):
        estimate, remainder, search, norm_now = carried
        product = coarse_apply(search)
        alpha = norm_now / dot(search, product)
        estimate = [e + alpha * s for e, s in zip(estimate, search)]
        remainder = [r - alpha * q for r, q in zip(remainder, product)]
        norm_next = dot(remainder, remainder)
        beta = norm_next / norm_now
        search = [r + beta * s for r, s in zip(remainder, search)]
        return estimate, remainder, search, norm_next

    state = ([jnp.zeros((cy, 128), jnp.float32)] * cx, coarse_source, coarse_source,
             dot(coarse_source, coarse_source))
    estimate = lax.fori_loop(0, CG_ITERS, iterate_once, state)[0]
    for x in range(cx):
        E[x] = estimate[x]

    own_share = E[ix, pl.ds(iy, 1), :]

    def share(dx, dy):
        jx, jy = ix + dx, iy + dy
        row = E[jnp.clip(jx, 0, cx - 1), pl.ds(jnp.clip(jy, 0, cy - 1), 1), :]
        return row * inside(jx, jy, cx, cy).astype(jnp.float32) - own_share

    for d in range(8):
        each(d, -1, lambda d=d: halo2(d).wait_recv())

    def edge(x, low, high):
        L3[x, 0:G, :] = YLO2[x, H - G:H, :] + low
        L3[x, G + ny:G + ny + NU, :] = YHI2[x, 0:NU, :] + high

    for dx, lo, got in ((-1, H - NU, XLO2), (1, H + nx, XHI2)):
        low, middle, high = [share(dx, dy) for dy in (-1, 0, 1)]
        for i in range(NU):
            L3[lo + i, G:G + ny, :] = got[i] + middle
            edge(lo + i, low, high)
    low, high = share(0, -1), share(0, 1)

    def inner(x, c):
        edge(x, low, high)
        return c

    rows_loop(H, H + nx, inner, 0)

    rims(L3, L4, 1)
    rims(L4, L5, 2)
    rims(L5, L6, 3)

    def give(x, c):
        out[x] = L6[H + x, G:G + ny, :] + own_share
        return c

    rows_loop(0, nx, give, 0)

    for d in range(8):
        each(d, 1, lambda d=d: halo2(d).wait_send())
    for d in range(8):
        def sent(d=d):
            for a in range(3):
                halo(a, d).wait_send()
        each(d, 1, sent)
    if direct:
        to_all("wait_send")
    else:
        run(sum_x, cx, "wait_send")
        run(sum_y, cy, "wait_send")


def body(conductivity, source, initial):
    nx, ny, nz = conductivity.shape
    cx, cy = lax.axis_size("gx"), lax.axis_size("gy")
    X, Y = nx + 2 * H, ny + 8
    args = (conductivity, source, initial)
    thin = tuple(a.reshape(nx, ny, 1, nz) for a in args)
    wide = pltpu.VMEM((X, Y, nz), jnp.float32)
    dma = pltpu.SemaphoreType.DMA

    def vmem(*shape):
        return pltpu.VMEM(shape, jnp.float32)

    return pl.pallas_call(
        functools.partial(kernel, cx, cy, nx, ny),
        out_shape=vmem(nx, ny, nz),
        in_specs=[pl.BlockSpec(memory_space=pltpu.HBM)] * 6,
        out_specs=pl.BlockSpec(memory_space=pltpu.VMEM),
        scratch_shapes=[wide] * 15 + [
            *[vmem(nx, ny, nz)] * 3,
            *[vmem(X, w, 1, nz) for w in WIDTH + WIDTH],
            *[vmem(w, ny, nz) for w in WIDTH + WIDTH],
            vmem(NU, ny, nz), vmem(NU, ny, nz), vmem(X, H, nz), vmem(X, H, nz), vmem(NU, ny, nz), vmem(NU, ny, nz),
            vmem(nx, H, nz), vmem(nx, H, nz),
            vmem(cy, cx, 1, nz), vmem(cx, cy, nz), vmem(cx, cy, nz),
            dma((3,)),
            dma((24,)), dma((24,)), dma((8,)), dma((8,)),
            dma((cx - 1,)), dma((cx - 1,)), dma((cy - 1,)), dma((cy - 1,)),
            dma((min(cx * cy, DIRECT) - 1,)), dma((min(cx * cy, DIRECT) - 1,)),
            pltpu.SemaphoreType.REGULAR((cx - 1,)),
        ],
        compiler_params=pltpu.CompilerParams(collective_id=0, has_side_effects=True),
        name="cycle",
    )(*args, *thin)


def solution(mesh):
    return jax.shard_map(
        body,
        mesh=mesh,
        in_specs=(P("gx", "gy", None), P("gx", "gy", None), P("gx", "gy", None)),
        out_specs=P("gx", "gy", None),
        check_vma=False,
    )
```

```python
import functools

import jax
import jax.numpy as jnp
from jax import lax
from jax.experimental import pallas as pl
from jax.experimental.pallas import tpu as pltpu
from jax.sharding import PartitionSpec as P

NU = 3
CG_ITERS = 32
H = NU + 1
G = NU
WIDTH = (NU, NU - 1, NU - 1)

relax_weight = 0.8
MESH = pl.DeviceIdType.MESH
DIRS = [(1, 0), (-1, 0), (0, 1), (0, -1), (1, 1), (1, -1), (-1, 1), (-1, -1)]


def inside(ix, iy, cx, cy):
    return (ix >= 0) & (ix < cx) & (iy >= 0) & (iy < cy)


UNROLL = 16


def rows_loop(lo, hi, step, carry):
    count = (hi - lo) // UNROLL

    def several(i, c):
        for r in range(UNROLL):
            c = step(lo + UNROLL * i + r, c)
        return c

    if count:
        carry = lax.fori_loop(0, count, several, carry)
    for x in range(lo + UNROLL * count, hi):
        carry = step(x, carry)
    return carry


ROWS = 16
DIRECT = 64


def blocks_loop(lo, hi, block, carry):
    count = (hi - lo) // ROWS
    if count > 1:
        carry = lax.fori_loop(0, count, lambda i, c: block(lo + ROWS * i, c, ROWS), carry)
    elif count:
        carry = block(lo, carry, ROWS)
    if (hi - lo) % ROWS:
        carry = block(lo + ROWS * count, carry, (hi - lo) % ROWS)
    return carry


def kernel(cx, cy, nx, ny, *refs):
    (k_in, f_in, u_in, k1, f1, u1, out,
     K, F, L0, L1, L2, L3, L4, L5, L6, CE, CN, CS, CU, CD, W, SK, SF, SU,
     YLO_K, YLO_F, YLO_U, YHI_K, YHI_F, YHI_U, XLO_K, XLO_F, XLO_U, XHI_K, XHI_F, XHI_U,
     FXLO, FXHI, FYLO, FYHI, XLO2, XHI2, YLO2, YHI2, QLO, QHI, PLO, PHI, GS, E, R,
     lsem, ssem, rsem, ssem2, rsem2,
     s1s, s1r, s2s, s2r, das, dar, chain) = refs
    X = nx + 2 * H
    Y = ny + 8
    ix = lax.axis_index("gx")
    iy = lax.axis_index("gy")
    full = [k_in, f_in, u_in]
    thin = [k1, f1, u1]
    ext = [K, F, L0]
    stage = [SK, SF, SU]
    XLO = [XLO_K, XLO_F, XLO_U]
    XHI = [XHI_K, XHI_F, XHI_U]
    YLO = [YLO_K, YLO_F, YLO_U]
    YHI = [YHI_K, YHI_F, YHI_U]

    direct = cx * cy <= DIRECT
    barrier = pltpu.get_barrier_semaphore()

    def greet_x(k, c):
        pl.semaphore_signal(barrier, inc=1, device_id=(lax.rem(ix + k, cx), iy), device_id_type=MESH)
        return c

    def greet_y(k, c):
        pl.semaphore_signal(barrier, inc=1, device_id=(ix, lax.rem(iy + k, cy)), device_id_type=MESH)
        return c

    for dx, dy in (DIRS[:2] if direct else []) + DIRS[4:]:
        @pl.when(inside(ix + dx, iy + dy, cx, cy))
        def _(dx=dx, dy=dy):
            pl.semaphore_signal(barrier, inc=1, device_id=(ix + dx, iy + dy), device_id_type=MESH)
    if not direct:
        lax.fori_loop(1, cx, greet_x, 0)
    lax.fori_loop(1, cy, greet_y, 0)

    local = [pltpu.make_async_copy(full[a], stage[a], lsem.at[a]) for a in range(3)]
    for copy in local:
        copy.start()

    sides_x = (ix > 0).astype(jnp.int32) + (ix < cx - 1).astype(jnp.int32)
    sides_y = (iy > 0).astype(jnp.int32) + (iy < cy - 1).astype(jnp.int32)
    pl.semaphore_wait(barrier, (sides_x if direct else cx - 1) + (cy - 1) + sides_x * sides_y)

    def chain_signal(k):
        for dx in (1, -1):
            @pl.when((ix + dx >= 0) & (ix + dx < cx))
            def _(dx=dx):
                pl.semaphore_signal(chain.at[k], inc=1, device_id=(ix + dx, iy), device_id_type=MESH)

    def chain_wait(k):
        pl.semaphore_wait(chain.at[k], sides_x)

    def spans(dx, w):
        src = {1: (nx - w, nx), -1: (0, w), 0: (0, nx)}[dx]
        dst = {1: (H - w, H), -1: (X - H, X - H + w), 0: (H, H + nx)}[dx]
        return src, dst

    def halo(a, d):
        dx, dy = DIRS[d]
        slot = a * 8 + d
        w = WIDTH[a]
        src_rows, dst_rows = spans(dx, w)
        if dy == 0:
            src = full[a].at[src_rows[0]:src_rows[1]] if a != 1 else (FXHI if dx == 1 else FXLO)
            dst = (XLO if dx == 1 else XHI)[a]
        else:
            cols = (ny - w, ny) if dy == 1 else (0, w)
            src = thin[a].at[src_rows[0]:src_rows[1], cols[0]:cols[1]]
            if a == 1 and dx == 0:
                src = FYHI if dy == 1 else FYLO
            dst = (YLO if dy == 1 else YHI)[a].at[dst_rows[0]:dst_rows[1]]
        return pltpu.make_async_remote_copy(
            src_ref=src, dst_ref=dst, send_sem=ssem.at[slot], recv_sem=rsem.at[slot],
            device_id=(ix + dx, iy + dy), device_id_type=MESH)

    def each(d, sign, act):
        dx, dy = DIRS[d]
        pl.when(inside(ix + sign * dx, iy + sign * dy, cx, cy))(act)

    links = cx - 1 if direct else 0
    if links:
        chain_signal(0)
    for d in range(4, 8):
        def start(d=d):
            for a in (0, 2, 1):
                halo(a, d).start()
        each(d, 1, start)
    for a in (0, 2):
        for d in range(4):
            each(d, 1, lambda a=a, d=d: halo(a, d).start())

    def clear_when_absent(d):
        dx, dy = DIRS[d]

        @pl.when(jnp.logical_not(inside(ix - dx, iy - dy, cx, cy)))
        def _():
            for a in range(3):
                w = WIDTH[a]
                lo, hi = spans(dx, w)[1]
                if dy == 0:
                    (XLO if dx == 1 else XHI)[a][...] = jnp.zeros((w, ny, 128), jnp.float32)
                else:
                    (YLO if dy == 1 else YHI)[a][lo:hi] = jnp.zeros((hi - lo, w, 1, 128), jnp.float32)
            if dy == 0:
                (XLO2 if dx == 1 else XHI2)[...] = jnp.zeros((NU, ny, 128), jnp.float32)
            else:
                lo, hi = spans(dx, H)[1]
                (YLO2 if dy == 1 else YHI2)[lo:hi] = jnp.zeros((hi - lo, H, 128), jnp.float32)

    for d in range(8):
        clear_when_absent(d)

    for copy in local:
        copy.wait()

    def push(x, back):
        return SF[x] + 0.5 * (SK[x] + SK[back]) * SU[back]

    FXLO[0] = SF[0]
    FXLO[1] = push(1, 2)
    FXHI[0] = push(nx - 2, nx - 3)
    FXHI[1] = SF[nx - 1]

    def push_y(x, c):
        low = SF[x, 0:8, :] + 0.5 * (SK[x, 0:8, :] + SK[x, 1:9, :]) * SU[x, 1:9, :]
        high = SF[x, ny - 8:ny, :] + 0.5 * (SK[x, ny - 8:ny, :] + SK[x, ny - 9:ny - 1, :]) * SU[x, ny - 9:ny - 1, :]
        FYLO[x, 0] = SF[x, 0:1, :]
        FYLO[x, 1] = low[1:2]
        FYHI[x, 0] = high[6:7]
        FYHI[x, 1] = SF[x, ny - 1:ny, :]
        return c

    rows_loop(0, nx, push_y, 0)
    for d in range(4):
        each(d, 1, lambda d=d: halo(1, d).start())

    def along_x(G, ss, rs):
        def of(k):
            return pltpu.make_async_remote_copy(
                src_ref=G.at[iy, ix], dst_ref=G.at[iy, ix], send_sem=ss.at[k - 1], recv_sem=rs.at[k - 1],
                device_id=(lax.rem(ix + k, cx), iy), device_id_type=MESH)
        return of

    def along_y(G, ss, rs):
        def of(k):
            return pltpu.make_async_remote_copy(
                src_ref=G.at[iy], dst_ref=G.at[iy], send_sem=ss.at[k - 1], recv_sem=rs.at[k - 1],
                device_id=(ix, lax.rem(iy + k, cy)), device_id_type=MESH)
        return of

    def around(i, k, count):
        return jnp.where(i + k < count, i + k, i + k - count)

    def to_all(method):
        for kx in [*range(1, cx), 0]:
            for ky in range(cy):
                k = kx * cy + ky
                if k:
                    copy = pltpu.make_async_remote_copy(
                        src_ref=GS.at[iy, ix], dst_ref=GS.at[iy, ix], send_sem=das.at[k - 1], recv_sem=dar.at[k - 1],
                        device_id=(around(ix, kx, cx), around(iy, ky, cy)), device_id_type=MESH)
                    getattr(copy, method)()

    def run(of, count, method):
        def go(k, c):
            getattr(of(k), method)()
            return c
        lax.fori_loop(1, count, go, 0)

    sum_x, sum_y = along_x(GS, s1s, s1r), along_y(GS, s2s, s2r)

    lane_row = lax.broadcasted_iota(jnp.int32, (1, 128), 1)

    def whole(v):
        return jnp.sum(jnp.sum(v, axis=0, keepdims=True), axis=1, keepdims=True)

    def in_lanes(values):
        row = jnp.zeros((1, 128), jnp.float32)
        for k, v in enumerate(values):
            row = jnp.where(lane_row == k, v, row)
        return row

    def place(x, c):
        for a in range(3):
            ext[a][x, G:G + ny, :] = stage[a][x - H]
        return c

    def clear(x, c):
        L0[x, 0:8, :] = jnp.zeros((8, 128), jnp.float32)
        L0[x, Y - 8:Y, :] = jnp.zeros((8, 128), jnp.float32)
        return c

    rows_loop(1, X - 1, clear, 0)
    for x in (H - NU, H + nx + NU - 1):
        L0[x] = jnp.zeros((Y, 128), jnp.float32)
    rows_loop(H, H + nx, place, 0)

    lane = lax.broadcasted_iota(jnp.int32, (Y, 128), 1)
    up_half = jnp.where(lane < 127, 0.5, 0.0)
    down_half = jnp.where(lane > 0, 0.5, 0.0)
    ALL, LOW, HIGH = (0, Y), (0, 8), (Y - 8, Y)

    def at(ref, x, g):
        return ref[x] if g == ALL else ref[x, g[0]:g[1], :]

    def put(ref, x, g, v):
        if g == ALL:
            ref[x] = v
        else:
            ref[x, g[0]:g[1], :] = v

    def next_y(ref, x, g, v):
        return pltpu.roll(v, g[1] - g[0] - 1, 0) if g[1] == Y else ref[x, g[0] + 1:g[1] + 1, :]

    def last_y(ref, x, g, v):
        return pltpu.roll(v, 1, 0) if g[0] == 0 else ref[x, g[0] - 1:g[1] - 1, :]

    def next_z(v):
        return pltpu.roll(v, 127, 1)

    def last_z(v):
        return pltpu.roll(v, 1, 1)

    def faces_at(g):
        n = g[1] - g[0]

        def block(x, c, rows):
            k, west = c
            ks = [k] + [at(K, x + 1 + r, g) for r in range(rows)]
            ups = [next_z(ks[r]) for r in range(rows)]
            downs = [last_z(ks[r]) for r in range(rows)]
            for r in range(rows):
                k = ks[r]
                east = 0.5 * (k + ks[r + 1])
                north = 0.5 * (k + next_y(K, x + r, g, k))
                south = 0.5 * (k + last_y(K, x + r, g, k))
                up = up_half[0:n] * (k + ups[r])
                down = down_half[0:n] * (k + downs[r])
                d = east + west + north + south + up + down
                put(CE, x + r, g, east)
                put(CN, x + r, g, north)
                put(CS, x + r, g, south)
                put(CU, x + r, g, up)
                put(CD, x + r, g, down)
                put(W, x + r, g, jnp.where(k > 0, relax_weight / jnp.where(k > 0, d, 1.0), 0.0))
                west = east
            return ks[rows], west
        return block

    def faces(lo, hi, slabs):
        def start(g):
            k, before = at(K, lo, g), at(K, lo - 1, g)
            west = 0.5 * (k + before)
            put(CE, lo - 1, g, west)
            return k, west

        def block(x, c, rows):
            return tuple(faces_at(g)(x, v, rows) for g, v in zip(slabs, c))

        blocks_loop(lo, hi, block, tuple(start(g) for g in slabs))

    def sweep_at(src, dst, g):
        def block(x, c, rows):
            u, west = c
            us = [u] + [at(src, x + 1 + r, g) for r in range(rows)]
            ups = [next_z(us[r]) for r in range(rows)]
            downs = [last_z(us[r]) for r in range(rows)]
            for r in range(rows):
                u = us[r]
                east = at(CE, x + r, g) * (us[r + 1] - u)
                north = at(CN, x + r, g) * (next_y(src, x + r, g, u) - u)
                if g == ALL:
                    south = pltpu.roll(north, 1, 0)
                else:
                    south = at(CS, x + r, g) * (u - last_y(src, x + r, g, u))
                change = ((east - west) + (north - south)
                          + (at(CU, x + r, g) * (ups[r] - u) + at(CD, x + r, g) * (downs[r] - u)))
                put(dst, x + r, g, u + at(W, x + r, g) * (at(F, x + r, g) + change))
                west = east
            return us[rows], west
        return block

    def sweep(src, dst, lo, hi, slabs):
        def start(g):
            u = at(src, lo, g)
            return u, at(CE, lo - 1, g) * (u - at(src, lo - 1, g))

        def block(x, c, rows):
            return tuple(sweep_at(src, dst, g)(x, v, rows) for g, v in zip(slabs, c))

        blocks_loop(lo, hi, block, tuple(start(g) for g in slabs))

    def interior(src, dst, s):
        sweep(src, dst, H + s, H + nx - s, [ALL])

    def rims(src, dst, s):
        for lo in (H - NU + s, H + nx - s):
            sweep(src, dst, lo, lo + NU, [ALL])
        sweep(src, dst, H + s, H + nx - s, [LOW, HIGH])

    faces(H + 1, H + nx - 1, [ALL])

    for k in range(links):
        chain_wait(k)
        if k + 1 < links:
            chain_signal(k + 1)
        if k == 0:
            interior(L0, L1, 1)
        if k == 1:
            interior(L1, L2, 2)
    if links < 1:
        interior(L0, L1, 1)
    if links < 2:
        interior(L1, L2, 2)
    interior(L2, L3, 3)

    def outer(x, c):
        return c[0] + SK[x, 0:1, :], c[1] + SK[x, ny - 1:ny, :]

    none = jnp.zeros((1, 128), jnp.float32)
    y_first, y_last = rows_loop(0, nx, outer, (none, none))
    edges = [whole(SK[0]), whole(SK[nx - 1]), whole(y_first), whole(y_last)]
    f_total = rows_loop(0, nx, lambda x, c: c + SF[x], jnp.zeros((ny, 128), jnp.float32))
    f_total = jnp.sum(f_total, axis=0, keepdims=True)

    def unpack(arrays):
        def one(x, c):
            for a in arrays:
                w = WIDTH[a]
                ext[a][x, G + ny:G + ny + w, :] = YHI[a][x, :, 0, :]
                ext[a][x, G - w:G, :] = YLO[a][x, :, 0, :]
            return c

        rows_loop(1, X - 1, one, 0)
        for a in arrays:
            w = WIDTH[a]
            for i in range(w):
                ext[a][H - w + i, G:G + ny, :] = XLO[a][i]
                ext[a][H + nx + i, G:G + ny, :] = XHI[a][i]

    for d in range(8):
        each(d, -1, lambda d=d: halo(0, d).wait_recv())
    unpack([0])
    for lo in (H - NU + 1, H + nx - 1):
        faces(lo, lo + NU, [ALL])
    faces(H + 1, H + nx - 1, [LOW, HIGH])
    for a in (2, 1):
        for d in range(8):
            each(d, -1, lambda a=a, d=d: halo(a, d).wait_recv())
    unpack([2, 1])
    rims(L0, L1, 1)
    rims(L1, L2, 2)
    rims(L2, L3, 3)

    def sides(x, c):
        return c[0] + CS[x, 0:8, :] * L3[x, 0:8, :], c[1] + CN[x, Y - 8:Y, :] * L3[x, Y - 8:Y, :]

    none = jnp.zeros((8, 128), jnp.float32)
    y_low, y_high = rows_loop(H, H + nx, sides, (none, none))
    y_low, y_high = y_low[G:G + 1], y_high[G - 1:G]
    x_low = jnp.sum(CE[H - 1, G:G + ny, :] * L3[H, G:G + ny, :], axis=0, keepdims=True)
    x_high = jnp.sum(CE[X - H - 1, G:G + ny, :] * L3[X - H - 1, G:G + ny, :], axis=0, keepdims=True)
    own = f_total - x_low - x_high - y_low - y_high
    GS[iy, ix] = in_lanes([whole(v) for v in (own, x_low, x_high, y_low, y_high)] + edges)
    if direct:
        to_all("start")
    else:
        run(sum_x, cx, "start")

    part = lax.broadcasted_iota(jnp.int32, (H, 128), 0)

    def pack(x, c):
        PLO[x] = L3[H + x, G:G + H, :] - jnp.where(part == NU - 1, L0[H + x, G:G + H, :], 0.0)
        PHI[x] = L3[H + x, G + ny - H:G + ny, :] - jnp.where(part == H - NU, L0[H + x, G + ny - H:G + ny, :], 0.0)
        return c

    rows_loop(0, nx, pack, 0)
    for i in range(NU):
        QLO[i] = L3[H + i, G:G + ny, :]
        QHI[i] = L3[H + nx - NU + i, G:G + ny, :]
    QLO[NU - 1] = QLO[NU - 1] - L0[H + NU - 1, G:G + ny, :]
    QHI[0] = QHI[0] - L0[H + nx - NU, G:G + ny, :]

    def halo2(d):
        dx, dy = DIRS[d]
        src_rows = {1: (nx - H, nx), -1: (0, H), 0: (0, nx)}[dx]
        dst_rows = {1: (0, H), -1: (X - H, X), 0: (H, H + nx)}[dx]
        if dy == 0:
            src = QHI if dx == 1 else QLO
            dst = XLO2 if dx == 1 else XHI2
        else:
            src = (PHI if dy == 1 else PLO).at[src_rows[0]:src_rows[1]]
            dst = (YLO2 if dy == 1 else YHI2).at[dst_rows[0]:dst_rows[1]]
        return pltpu.make_async_remote_copy(
            src_ref=src, dst_ref=dst, send_sem=ssem2.at[d], recv_sem=rsem2.at[d],
            device_id=(ix + dx, iy + dy), device_id_type=MESH)

    if not direct:
        run(sum_x, cx, "wait_recv")
        run(sum_y, cy, "start")
    for d in range(8):
        each(d, 1, lambda d=d: halo2(d).start())
    interior(L3, L4, 1)
    interior(L4, L5, 2)
    interior(L5, L6, 3)

    row_y = lax.broadcasted_iota(jnp.int32, (cy, 128), 0)

    def tidy(G):
        for x in range(cx):
            for y in range(cy):
                R[x, y:y + 1, :] = G[y, x]
        return [R[x] for x in range(cx)]

    def lane_of(rows, k):
        return [jnp.broadcast_to(r[:, k:k + 1], (cy, 128)) for r in rows]

    def after_y(v):
        return jnp.where(row_y < cy - 1, pltpu.roll(v, cy - 1, 0), 0.0)

    def before_y(v):
        return jnp.where(row_y > 0, pltpu.roll(v, 1, 0), 0.0)

    if direct:
        to_all("wait_recv")
    else:
        run(sum_y, cy, "wait_recv")
    coarse_rows = tidy(GS)
    nil = jnp.zeros((cy, 128), jnp.float32)
    x_first, x_last, y_first, y_last = [lane_of(coarse_rows, k) for k in range(5, 9)]
    east = [0.5 * (a + b) for a, b in zip(x_last, x_first[1:] + [nil])]
    west = [0.5 * (a + b) for a, b in zip(x_first, [nil] + x_last[:-1])]
    north = [0.5 * (a + after_y(b)) for a, b in zip(y_last, y_first)]
    south = [0.5 * (a + before_y(b)) for a, b in zip(y_first, y_last)]
    diag = [a + b + c + d for a, b, c, d in zip(east, west, north, south)]
    north = [jnp.where(row_y < cy - 1, n, 0.0) for n in north]
    south = [pltpu.roll(n, 1, 0) for n in north]

    own, x_low, x_high, y_low, y_high = [lane_of(coarse_rows, k) for k in range(5)]
    coarse_source = [
        (a + after_y(b)) + (before_y(c) + d + e)
        for a, b, c, d, e in zip(own, y_low, y_high, x_low[1:] + [nil], [nil] + x_high[:-1])]

    def dot(a, b):
        terms = [p * q for p, q in zip(a, b)]
        while len(terms) > 1:
            terms = [sum(terms[i + 1:i + 2], terms[i]) for i in range(0, len(terms), 2)]
        return jnp.sum(terms[0], axis=0, keepdims=True)

    def coarse_apply(p):
        product = []
        for x in range(cx):
            v = diag[x] * p[x]
            if x < cx - 1:
                v = v - east[x] * p[x + 1]
            if x > 0:
                v = v - east[x - 1] * p[x - 1]
            product.append(v - (north[x] * pltpu.roll(p[x], cy - 1, 0) + south[x] * pltpu.roll(p[x], 1, 0)))
        return product

    def iterate_once(counter, carried):
        estimate, remainder, search, norm_now, inverse = carried
        product = coarse_apply(search)
        alpha = norm_now / dot(search, product)
        estimate = [e + alpha * s for e, s in zip(estimate, search)]
        remainder = [r - alpha * q for r, q in zip(remainder, product)]
        norm_next = dot(remainder, remainder)
        beta = norm_next * inverse
        search = [r + beta * s for r, s in zip(remainder, search)]
        return estimate, remainder, search, norm_next, 1.0 / norm_next

    norm = dot(coarse_source, coarse_source)
    state = ([jnp.zeros((cy, 128), jnp.float32)] * cx, coarse_source, coarse_source, norm, 1.0 / norm)
    estimate = lax.fori_loop(0, CG_ITERS, iterate_once, state)[0]
    for x in range(cx):
        E[x] = estimate[x]

    own_share = E[ix, pl.ds(iy, 1), :]

    def share(dx, dy):
        jx, jy = ix + dx, iy + dy
        row = E[jnp.clip(jx, 0, cx - 1), pl.ds(jnp.clip(jy, 0, cy - 1), 1), :]
        return row * inside(jx, jy, cx, cy).astype(jnp.float32) - own_share

    for d in range(8):
        each(d, -1, lambda d=d: halo2(d).wait_recv())

    def edge(x, low, high):
        L3[x, 0:G, :] = YLO2[x, H - G:H, :] + low
        L3[x, G + ny:G + ny + NU, :] = YHI2[x, 0:NU, :] + high

    for dx, lo, got in ((-1, H - NU, XLO2), (1, H + nx, XHI2)):
        low, middle, high = [share(dx, dy) for dy in (-1, 0, 1)]
        for i in range(NU):
            L3[lo + i, G:G + ny, :] = got[i] + middle
            edge(lo + i, low, high)
    low, high = share(0, -1), share(0, 1)

    def inner(x, c):
        edge(x, low, high)
        return c

    rows_loop(H, H + nx, inner, 0)

    rims(L3, L4, 1)
    rims(L4, L5, 2)
    rims(L5, L6, 3)

    def give(x, c):
        out[x] = L6[H + x, G:G + ny, :] + own_share
        return c

    rows_loop(0, nx, give, 0)

    for d in range(8):
        each(d, 1, lambda d=d: halo2(d).wait_send())
    for d in range(8):
        def sent(d=d):
            for a in range(3):
                halo(a, d).wait_send()
        each(d, 1, sent)
    if direct:
        to_all("wait_send")
    else:
        run(sum_x, cx, "wait_send")
        run(sum_y, cy, "wait_send")


def body(conductivity, source, initial):
    nx, ny, nz = conductivity.shape
    cx, cy = lax.axis_size("gx"), lax.axis_size("gy")
    X, Y = nx + 2 * H, ny + 8
    args = (conductivity, source, initial)
    thin = tuple(a.reshape(nx, ny, 1, nz) for a in args)
    wide = pltpu.VMEM((X, Y, nz), jnp.float32)
    dma = pltpu.SemaphoreType.DMA

    def vmem(*shape):
        return pltpu.VMEM(shape, jnp.float32)

    return pl.pallas_call(
        functools.partial(kernel, cx, cy, nx, ny),
        out_shape=vmem(nx, ny, nz),
        in_specs=[pl.BlockSpec(memory_space=pltpu.HBM)] * 6,
        out_specs=pl.BlockSpec(memory_space=pltpu.VMEM),
        scratch_shapes=[wide] * 15 + [
            *[vmem(nx, ny, nz)] * 3,
            *[vmem(X, w, 1, nz) for w in WIDTH + WIDTH],
            *[vmem(w, ny, nz) for w in WIDTH + WIDTH],
            vmem(NU - 1, ny, nz), vmem(NU - 1, ny, nz), vmem(nx, NU - 1, 1, nz), vmem(nx, NU - 1, 1, nz),
            vmem(NU, ny, nz), vmem(NU, ny, nz), vmem(X, H, nz), vmem(X, H, nz), vmem(NU, ny, nz), vmem(NU, ny, nz),
            vmem(nx, H, nz), vmem(nx, H, nz),
            vmem(cy, cx, 1, nz), vmem(cx, cy, nz), vmem(cx, cy, nz),
            dma((3,)),
            dma((24,)), dma((24,)), dma((8,)), dma((8,)),
            dma((cx - 1,)), dma((cx - 1,)), dma((cy - 1,)), dma((cy - 1,)),
            dma((min(cx * cy, DIRECT) - 1,)), dma((min(cx * cy, DIRECT) - 1,)),
            pltpu.SemaphoreType.REGULAR((cx - 1,)),
        ],
        compiler_params=pltpu.CompilerParams(collective_id=0, has_side_effects=True),
        name="cycle",
    )(*args, *thin)


def solution(mesh):
    return jax.shard_map(
        body,
        mesh=mesh,
        in_specs=(P("gx", "gy", None), P("gx", "gy", None), P("gx", "gy", None)),
        out_specs=P("gx", "gy", None),
        check_vma=False,
    )
```

```python
import functools

import jax
import jax.numpy as jnp
from jax import lax
from jax.experimental import pallas as pl
from jax.experimental.pallas import tpu as pltpu
from jax.sharding import PartitionSpec as P

NU = 3
CG_ITERS = 32
H = NU + 1
G = NU
WIDTH = (NU, NU - 1, NU - 1)

relax_weight = 0.8
MESH = pl.DeviceIdType.MESH
DIRS = [(1, 0), (-1, 0), (0, 1), (0, -1), (1, 1), (1, -1), (-1, 1), (-1, -1)]


def inside(ix, iy, cx, cy):
    return (ix >= 0) & (ix < cx) & (iy >= 0) & (iy < cy)


UNROLL = 16


def rows_loop(lo, hi, step, carry):
    count = (hi - lo) // UNROLL

    def several(i, c):
        for r in range(UNROLL):
            c = step(lo + UNROLL * i + r, c)
        return c

    if count:
        carry = lax.fori_loop(0, count, several, carry)
    for x in range(lo + UNROLL * count, hi):
        carry = step(x, carry)
    return carry


ROWS = 16
DIRECT = 64


def blocks_loop(lo, hi, block, carry):
    count = (hi - lo) // ROWS
    if count > 1:
        carry = lax.fori_loop(0, count, lambda i, c: block(lo + ROWS * i, c, ROWS), carry)
    elif count:
        carry = block(lo, carry, ROWS)
    if (hi - lo) % ROWS:
        carry = block(lo + ROWS * count, carry, (hi - lo) % ROWS)
    return carry


def kernel(cx, cy, nx, ny, *refs):
    (k_in, f_in, u_in, k1, f1, u1, out,
     K, F, L0, L1, L2, L3, L4, L5, L6, CE, CN, CS, CU, CD, W, SK, SF, SU,
     YLO_K, YLO_F, YLO_U, YHI_K, YHI_F, YHI_U, XLO_K, XLO_F, XLO_U, XHI_K, XHI_F, XHI_U,
     FXLO, FXHI, FYLO, FYHI, XLO2, XHI2, YLO2, YHI2, QLO, QHI, PLO, PHI, GS, E, R,
     lsem, ssem, rsem, ssem2, rsem2,
     s1s, s1r, s2s, s2r, das, dar, chain) = refs
    X = nx + 2 * H
    Y = ny + 8
    ix = lax.axis_index("gx")
    iy = lax.axis_index("gy")
    full = [k_in, f_in, u_in]
    thin = [k1, f1, u1]
    ext = [K, F, L0]
    stage = [SK, SF, SU]
    XLO = [XLO_K, XLO_F, XLO_U]
    XHI = [XHI_K, XHI_F, XHI_U]
    YLO = [YLO_K, YLO_F, YLO_U]
    YHI = [YHI_K, YHI_F, YHI_U]

    direct = cx * cy <= DIRECT
    barrier = pltpu.get_barrier_semaphore()

    def greet_x(k, c):
        pl.semaphore_signal(barrier, inc=1, device_id=(lax.rem(ix + k, cx), iy), device_id_type=MESH)
        return c

    def greet_y(k, c):
        pl.semaphore_signal(barrier, inc=1, device_id=(ix, lax.rem(iy + k, cy)), device_id_type=MESH)
        return c

    for dx, dy in (DIRS[:2] if direct else []) + DIRS[4:]:
        @pl.when(inside(ix + dx, iy + dy, cx, cy))
        def _(dx=dx, dy=dy):
            pl.semaphore_signal(barrier, inc=1, device_id=(ix + dx, iy + dy), device_id_type=MESH)
    if not direct:
        lax.fori_loop(1, cx, greet_x, 0)
    lax.fori_loop(1, cy, greet_y, 0)

    local = [pltpu.make_async_copy(full[a], stage[a], lsem.at[a]) for a in range(3)]
    for copy in local:
        copy.start()

    sides_x = (ix > 0).astype(jnp.int32) + (ix < cx - 1).astype(jnp.int32)
    sides_y = (iy > 0).astype(jnp.int32) + (iy < cy - 1).astype(jnp.int32)
    pl.semaphore_wait(barrier, (sides_x if direct else cx - 1) + (cy - 1) + sides_x * sides_y)

    def chain_signal(k):
        for dx in (1, -1):
            @pl.when((ix + dx >= 0) & (ix + dx < cx))
            def _(dx=dx):
                pl.semaphore_signal(chain.at[k], inc=1, device_id=(ix + dx, iy), device_id_type=MESH)

    def chain_wait(k):
        pl.semaphore_wait(chain.at[k], sides_x)

    def spans(dx, w):
        src = {1: (nx - w, nx), -1: (0, w), 0: (0, nx)}[dx]
        dst = {1: (H - w, H), -1: (X - H, X - H + w), 0: (H, H + nx)}[dx]
        return src, dst

    def halo(a, d):
        dx, dy = DIRS[d]
        slot = a * 8 + d
        w = WIDTH[a]
        src_rows, dst_rows = spans(dx, w)
        if dy == 0:
            src = full[a].at[src_rows[0]:src_rows[1]] if a != 1 else (FXHI if dx == 1 else FXLO)
            dst = (XLO if dx == 1 else XHI)[a]
        else:
            cols = (ny - w, ny) if dy == 1 else (0, w)
            src = thin[a].at[src_rows[0]:src_rows[1], cols[0]:cols[1]]
            if a == 1 and dx == 0:
                src = FYHI if dy == 1 else FYLO
            dst = (YLO if dy == 1 else YHI)[a].at[dst_rows[0]:dst_rows[1]]
        return pltpu.make_async_remote_copy(
            src_ref=src, dst_ref=dst, send_sem=ssem.at[slot], recv_sem=rsem.at[slot],
            device_id=(ix + dx, iy + dy), device_id_type=MESH)

    def each(d, sign, act):
        dx, dy = DIRS[d]
        pl.when(inside(ix + sign * dx, iy + sign * dy, cx, cy))(act)

    links = cx - 1 if direct else 0
    if links:
        chain_signal(0)
    for d in range(4, 8):
        def start(d=d):
            for a in (0, 2, 1):
                halo(a, d).start()
        each(d, 1, start)
    for a in (0, 2):
        for d in range(4):
            each(d, 1, lambda a=a, d=d: halo(a, d).start())

    def clear_when_absent(d):
        dx, dy = DIRS[d]

        @pl.when(jnp.logical_not(inside(ix - dx, iy - dy, cx, cy)))
        def _():
            for a in range(3):
                w = WIDTH[a]
                lo, hi = spans(dx, w)[1]
                if dy == 0:
                    (XLO if dx == 1 else XHI)[a][...] = jnp.zeros((w, ny, 128), jnp.float32)
                else:
                    (YLO if dy == 1 else YHI)[a][lo:hi] = jnp.zeros((hi - lo, w, 1, 128), jnp.float32)
            if dy == 0:
                (XLO2 if dx == 1 else XHI2)[...] = jnp.zeros((NU, ny, 128), jnp.float32)
            else:
                lo, hi = spans(dx, H)[1]
                (YLO2 if dy == 1 else YHI2)[lo:hi] = jnp.zeros((hi - lo, H, 128), jnp.float32)

    for d in range(8):
        clear_when_absent(d)

    for copy in local:
        copy.wait()

    def push(x, back):
        return SF[x] + 0.5 * (SK[x] + SK[back]) * SU[back]

    FXLO[0] = SF[0]
    FXLO[1] = push(1, 2)
    FXHI[0] = push(nx - 2, nx - 3)
    FXHI[1] = SF[nx - 1]

    def push_y(x, c):
        low = SF[x, 0:8, :] + 0.5 * (SK[x, 0:8, :] + SK[x, 1:9, :]) * SU[x, 1:9, :]
        high = SF[x, ny - 8:ny, :] + 0.5 * (SK[x, ny - 8:ny, :] + SK[x, ny - 9:ny - 1, :]) * SU[x, ny - 9:ny - 1, :]
        FYLO[x, 0] = SF[x, 0:1, :]
        FYLO[x, 1] = low[1:2]
        FYHI[x, 0] = high[6:7]
        FYHI[x, 1] = SF[x, ny - 1:ny, :]
        return c

    rows_loop(0, nx, push_y, 0)
    for d in range(4):
        each(d, 1, lambda d=d: halo(1, d).start())

    def along_x(G, ss, rs):
        def of(k):
            return pltpu.make_async_remote_copy(
                src_ref=G.at[iy, ix], dst_ref=G.at[iy, ix], send_sem=ss.at[k - 1], recv_sem=rs.at[k - 1],
                device_id=(lax.rem(ix + k, cx), iy), device_id_type=MESH)
        return of

    def along_y(G, ss, rs):
        def of(k):
            return pltpu.make_async_remote_copy(
                src_ref=G.at[iy], dst_ref=G.at[iy], send_sem=ss.at[k - 1], recv_sem=rs.at[k - 1],
                device_id=(ix, lax.rem(iy + k, cy)), device_id_type=MESH)
        return of

    def around(i, k, count):
        return jnp.where(i + k < count, i + k, i + k - count)

    def to_all(method):
        for kx in [*range(1, cx), 0]:
            for ky in range(cy):
                k = kx * cy + ky
                if k:
                    copy = pltpu.make_async_remote_copy(
                        src_ref=GS.at[iy, ix], dst_ref=GS.at[iy, ix], send_sem=das.at[k - 1], recv_sem=dar.at[k - 1],
                        device_id=(around(ix, kx, cx), around(iy, ky, cy)), device_id_type=MESH)
                    getattr(copy, method)()

    def run(of, count, method):
        def go(k, c):
            getattr(of(k), method)()
            return c
        lax.fori_loop(1, count, go, 0)

    sum_x, sum_y = along_x(GS, s1s, s1r), along_y(GS, s2s, s2r)

    lane_row = lax.broadcasted_iota(jnp.int32, (1, 128), 1)

    def whole(v):
        return jnp.sum(jnp.sum(v, axis=0, keepdims=True), axis=1, keepdims=True)

    def in_lanes(values):
        row = jnp.zeros((1, 128), jnp.float32)
        for k, v in enumerate(values):
            row = jnp.where(lane_row == k, v, row)
        return row

    def place(x, c):
        for a in range(3):
            ext[a][x, G:G + ny, :] = stage[a][x - H]
        return c

    def clear(x, c):
        L0[x, 0:8, :] = jnp.zeros((8, 128), jnp.float32)
        L0[x, Y - 8:Y, :] = jnp.zeros((8, 128), jnp.float32)
        return c

    rows_loop(1, X - 1, clear, 0)
    for x in (H - NU, H + nx + NU - 1):
        L0[x] = jnp.zeros((Y, 128), jnp.float32)
    rows_loop(H, H + nx, place, 0)

    lane = lax.broadcasted_iota(jnp.int32, (Y, 128), 1)
    up_half = jnp.where(lane < 127, 0.5, 0.0)
    down_half = jnp.where(lane > 0, 0.5, 0.0)
    ALL, LOW, HIGH = (0, Y), (0, 8), (Y - 8, Y)

    def at(ref, x, g):
        return ref[x] if g == ALL else ref[x, g[0]:g[1], :]

    def put(ref, x, g, v):
        if g == ALL:
            ref[x] = v
        else:
            ref[x, g[0]:g[1], :] = v

    def next_y(ref, x, g, v):
        return pltpu.roll(v, g[1] - g[0] - 1, 0) if g[1] == Y else ref[x, g[0] + 1:g[1] + 1, :]

    def last_y(ref, x, g, v):
        return pltpu.roll(v, 1, 0) if g[0] == 0 else ref[x, g[0] - 1:g[1] - 1, :]

    def next_z(v):
        return pltpu.roll(v, 127, 1)

    def last_z(v):
        return pltpu.roll(v, 1, 1)

    def faces_at(g):
        n = g[1] - g[0]

        def block(x, c, rows):
            k, west = c
            ks = [k] + [at(K, x + 1 + r, g) for r in range(rows)]
            ups = [next_z(ks[r]) for r in range(rows)]
            downs = [last_z(ks[r]) for r in range(rows)]
            for r in range(rows):
                k = ks[r]
                east = 0.5 * (k + ks[r + 1])
                north = 0.5 * (k + next_y(K, x + r, g, k))
                south = 0.5 * (k + last_y(K, x + r, g, k))
                up = up_half[0:n] * (k + ups[r])
                down = down_half[0:n] * (k + downs[r])
                d = east + west + north + south + up + down
                put(CE, x + r, g, east)
                put(CN, x + r, g, north)
                put(CS, x + r, g, south)
                put(CU, x + r, g, up)
                put(CD, x + r, g, down)
                put(W, x + r, g, jnp.where(k > 0, relax_weight / jnp.where(k > 0, d, 1.0), 0.0))
                west = east
            return ks[rows], west
        return block

    def faces(lo, hi, slabs):
        def start(g):
            k, before = at(K, lo, g), at(K, lo - 1, g)
            west = 0.5 * (k + before)
            put(CE, lo - 1, g, west)
            return k, west

        def block(x, c, rows):
            return tuple(faces_at(g)(x, v, rows) for g, v in zip(slabs, c))

        blocks_loop(lo, hi, block, tuple(start(g) for g in slabs))

    def sweep_at(src, dst, g):
        def block(x, c, rows):
            u, west = c
            us = [u] + [at(src, x + 1 + r, g) for r in range(rows)]
            ups = [next_z(us[r]) for r in range(rows)]
            downs = [last_z(us[r]) for r in range(rows)]
            for r in range(rows):
                u = us[r]
                east = at(CE, x + r, g) * (us[r + 1] - u)
                north = at(CN, x + r, g) * (next_y(src, x + r, g, u) - u)
                if g == ALL:
                    south = pltpu.roll(north, 1, 0)
                else:
                    south = at(CS, x + r, g) * (u - last_y(src, x + r, g, u))
                change = ((east - west) + (north - south)
                          + (at(CU, x + r, g) * (ups[r] - u) + at(CD, x + r, g) * (downs[r] - u)))
                put(dst, x + r, g, u + at(W, x + r, g) * (at(F, x + r, g) + change))
                west = east
            return us[rows], west
        return block

    def sweep(src, dst, lo, hi, slabs):
        def start(g):
            u = at(src, lo, g)
            return u, at(CE, lo - 1, g) * (u - at(src, lo - 1, g))

        def block(x, c, rows):
            return tuple(sweep_at(src, dst, g)(x, v, rows) for g, v in zip(slabs, c))

        blocks_loop(lo, hi, block, tuple(start(g) for g in slabs))

    def interior(src, dst, s):
        sweep(src, dst, H + s, H + nx - s, [ALL])

    def rims(src, dst, s):
        for lo in (H - NU + s, H + nx - s):
            sweep(src, dst, lo, lo + NU, [ALL])
        sweep(src, dst, H + s, H + nx - s, [LOW, HIGH])

    faces(H + 1, H + nx - 1, [ALL])

    for k in range(links):
        chain_wait(k)
        if k + 1 < links:
            chain_signal(k + 1)
        if k == 0:
            interior(L0, L1, 1)
        if k == 1:
            interior(L1, L2, 2)
    if links < 1:
        interior(L0, L1, 1)
    if links < 2:
        interior(L1, L2, 2)
    interior(L2, L3, 3)

    def outer(x, c):
        return c[0] + SK[x, 0:1, :], c[1] + SK[x, ny - 1:ny, :]

    none = jnp.zeros((1, 128), jnp.float32)
    y_first, y_last = rows_loop(0, nx, outer, (none, none))
    edges = [whole(SK[0]), whole(SK[nx - 1]), whole(y_first), whole(y_last)]
    f_total = rows_loop(0, nx, lambda x, c: c + SF[x], jnp.zeros((ny, 128), jnp.float32))
    f_total = jnp.sum(f_total, axis=0, keepdims=True)

    def unpack(arrays):
        def one(x, c):
            for a in arrays:
                w = WIDTH[a]
                ext[a][x, G + ny:G + ny + w, :] = YHI[a][x, :, 0, :]
                ext[a][x, G - w:G, :] = YLO[a][x, :, 0, :]
            return c

        rows_loop(1, X - 1, one, 0)
        for a in arrays:
            w = WIDTH[a]
            for i in range(w):
                ext[a][H - w + i, G:G + ny, :] = XLO[a][i]
                ext[a][H + nx + i, G:G + ny, :] = XHI[a][i]

    for d in range(8):
        each(d, -1, lambda d=d: halo(0, d).wait_recv())
    unpack([0])
    for lo in (H - NU + 1, H + nx - 1):
        faces(lo, lo + NU, [ALL])
    faces(H + 1, H + nx - 1, [LOW, HIGH])
    for a in (2, 1):
        for d in range(8):
            each(d, -1, lambda a=a, d=d: halo(a, d).wait_recv())
    unpack([2, 1])
    rims(L0, L1, 1)
    rims(L1, L2, 2)
    rims(L2, L3, 3)

    def sides(x, c):
        return c[0] + CS[x, 0:8, :] * L3[x, 0:8, :], c[1] + CN[x, Y - 8:Y, :] * L3[x, Y - 8:Y, :]

    none = jnp.zeros((8, 128), jnp.float32)
    y_low, y_high = rows_loop(H, H + nx, sides, (none, none))
    y_low, y_high = y_low[G:G + 1], y_high[G - 1:G]
    x_low = jnp.sum(CE[H - 1, G:G + ny, :] * L3[H, G:G + ny, :], axis=0, keepdims=True)
    x_high = jnp.sum(CE[X - H - 1, G:G + ny, :] * L3[X - H - 1, G:G + ny, :], axis=0, keepdims=True)
    own = f_total - x_low - x_high - y_low - y_high
    GS[iy, ix] = in_lanes([whole(v) for v in (own, x_low, x_high, y_low, y_high)] + edges)
    if direct:
        to_all("start")
    else:
        run(sum_x, cx, "start")

    part = lax.broadcasted_iota(jnp.int32, (H, 128), 0)

    def pack(x, c):
        PLO[x] = L3[H + x, G:G + H, :] - jnp.where(part == NU - 1, L0[H + x, G:G + H, :], 0.0)
        PHI[x] = L3[H + x, G + ny - H:G + ny, :] - jnp.where(part == H - NU, L0[H + x, G + ny - H:G + ny, :], 0.0)
        return c

    rows_loop(0, nx, pack, 0)
    for i in range(NU):
        QLO[i] = L3[H + i, G:G + ny, :]
        QHI[i] = L3[H + nx - NU + i, G:G + ny, :]
    QLO[NU - 1] = QLO[NU - 1] - L0[H + NU - 1, G:G + ny, :]
    QHI[0] = QHI[0] - L0[H + nx - NU, G:G + ny, :]

    def halo2(d):
        dx, dy = DIRS[d]
        src_rows = {1: (nx - H, nx), -1: (0, H), 0: (0, nx)}[dx]
        dst_rows = {1: (0, H), -1: (X - H, X), 0: (H, H + nx)}[dx]
        if dy == 0:
            src = QHI if dx == 1 else QLO
            dst = XLO2 if dx == 1 else XHI2
        else:
            src = (PHI if dy == 1 else PLO).at[src_rows[0]:src_rows[1]]
            dst = (YLO2 if dy == 1 else YHI2).at[dst_rows[0]:dst_rows[1]]
        return pltpu.make_async_remote_copy(
            src_ref=src, dst_ref=dst, send_sem=ssem2.at[d], recv_sem=rsem2.at[d],
            device_id=(ix + dx, iy + dy), device_id_type=MESH)

    if not direct:
        run(sum_x, cx, "wait_recv")
        run(sum_y, cy, "start")
    for d in range(8):
        each(d, 1, lambda d=d: halo2(d).start())
    interior(L3, L4, 1)
    interior(L4, L5, 2)
    interior(L5, L6, 3)

    row_y = lax.broadcasted_iota(jnp.int32, (cy, 128), 0)

    def tidy(G):
        for x in range(cx):
            for y in range(cy):
                R[x, y:y + 1, :] = G[y, x]
        return [R[x] for x in range(cx)]

    def lane_of(rows, k):
        return [jnp.broadcast_to(r[:, k:k + 1], (cy, 128)) for r in rows]

    def after_y(v):
        return jnp.where(row_y < cy - 1, pltpu.roll(v, cy - 1, 0), 0.0)

    def before_y(v):
        return jnp.where(row_y > 0, pltpu.roll(v, 1, 0), 0.0)

    if direct:
        to_all("wait_recv")
    else:
        run(sum_y, cy, "wait_recv")
    coarse_rows = tidy(GS)
    nil = jnp.zeros((cy, 128), jnp.float32)
    x_first, x_last, y_first, y_last = [lane_of(coarse_rows, k) for k in range(5, 9)]
    east = [0.5 * (a + b) for a, b in zip(x_last, x_first[1:] + [nil])]
    west = [0.5 * (a + b) for a, b in zip(x_first, [nil] + x_last[:-1])]
    north = [0.5 * (a + after_y(b)) for a, b in zip(y_last, y_first)]
    south = [0.5 * (a + before_y(b)) for a, b in zip(y_first, y_last)]
    diag = [a + b + c + d for a, b, c, d in zip(east, west, north, south)]
    north = [jnp.where(row_y < cy - 1, n, 0.0) for n in north]
    south = [pltpu.roll(n, 1, 0) for n in north]

    own, x_low, x_high, y_low, y_high = [lane_of(coarse_rows, k) for k in range(5)]
    coarse_source = [
        (a + after_y(b)) + (before_y(c) + d + e)
        for a, b, c, d, e in zip(own, y_low, y_high, x_low[1:] + [nil], [nil] + x_high[:-1])]

    def dot(a, b):
        terms = [p * q for p, q in zip(a, b)]
        while len(terms) > 1:
            terms = [sum(terms[i + 1:i + 2], terms[i]) for i in range(0, len(terms), 2)]
        return jnp.sum(terms[0], axis=0, keepdims=True)

    def coarse_apply(p):
        product = []
        for x in range(cx):
            v = diag[x] * p[x]
            if x < cx - 1:
                v = v - east[x] * p[x + 1]
            if x > 0:
                v = v - east[x - 1] * p[x - 1]
            product.append(v - (north[x] * pltpu.roll(p[x], cy - 1, 0) + south[x] * pltpu.roll(p[x], 1, 0)))
        return product

    def iterate_once(counter, carried):
        estimate, remainder, search, product, norm_now, inverse, energy = carried
        alpha = norm_now / energy
        estimate = [e + alpha * s for e, s in zip(estimate, search)]
        remainder = [r - alpha * q for r, q in zip(remainder, product)]
        applied = coarse_apply(remainder)
        norm_next = dot(remainder, remainder)
        beta = norm_next * inverse
        energy = dot(remainder, applied) - (beta * beta) * energy
        search = [r + beta * s for r, s in zip(remainder, search)]
        product = [v + beta * q for v, q in zip(applied, product)]
        return estimate, remainder, search, product, norm_next, 1.0 / norm_next, energy

    norm = dot(coarse_source, coarse_source)
    applied = coarse_apply(coarse_source)
    state = ([jnp.zeros((cy, 128), jnp.float32)] * cx, coarse_source, coarse_source, applied, norm, 1.0 / norm,
             dot(coarse_source, applied))
    estimate = lax.fori_loop(0, CG_ITERS, iterate_once, state)[0]
    for x in range(cx):
        E[x] = estimate[x]

    own_share = E[ix, pl.ds(iy, 1), :]

    def share(dx, dy):
        jx, jy = ix + dx, iy + dy
        row = E[jnp.clip(jx, 0, cx - 1), pl.ds(jnp.clip(jy, 0, cy - 1), 1), :]
        return row * inside(jx, jy, cx, cy).astype(jnp.float32) - own_share

    for d in range(8):
        each(d, -1, lambda d=d: halo2(d).wait_recv())

    def edge(x, low, high):
        L3[x, 0:G, :] = YLO2[x, H - G:H, :] + low
        L3[x, G + ny:G + ny + NU, :] = YHI2[x, 0:NU, :] + high

    for dx, lo, got in ((-1, H - NU, XLO2), (1, H + nx, XHI2)):
        low, middle, high = [share(dx, dy) for dy in (-1, 0, 1)]
        for i in range(NU):
            L3[lo + i, G:G + ny, :] = got[i] + middle
            edge(lo + i, low, high)
    low, high = share(0, -1), share(0, 1)

    def inner(x, c):
        edge(x, low, high)
        return c

    rows_loop(H, H + nx, inner, 0)

    rims(L3, L4, 1)
    rims(L4, L5, 2)
    rims(L5, L6, 3)

    def give(x, c):
        out[x] = L6[H + x, G:G + ny, :] + own_share
        return c

    rows_loop(0, nx, give, 0)

    for d in range(8):
        each(d, 1, lambda d=d: halo2(d).wait_send())
    for d in range(8):
        def sent(d=d):
            for a in range(3):
                halo(a, d).wait_send()
        each(d, 1, sent)
    if direct:
        to_all("wait_send")
    else:
        run(sum_x, cx, "wait_send")
        run(sum_y, cy, "wait_send")


def body(conductivity, source, initial):
    nx, ny, nz = conductivity.shape
    cx, cy = lax.axis_size("gx"), lax.axis_size("gy")
    X, Y = nx + 2 * H, ny + 8
    args = (conductivity, source, initial)
    thin = tuple(a.reshape(nx, ny, 1, nz) for a in args)
    wide = pltpu.VMEM((X, Y, nz), jnp.float32)
    dma = pltpu.SemaphoreType.DMA

    def vmem(*shape):
        return pltpu.VMEM(shape, jnp.float32)

    return pl.pallas_call(
        functools.partial(kernel, cx, cy, nx, ny),
        out_shape=vmem(nx, ny, nz),
        in_specs=[pl.BlockSpec(memory_space=pltpu.HBM)] * 6,
        out_specs=pl.BlockSpec(memory_space=pltpu.VMEM),
        scratch_shapes=[wide] * 15 + [
            *[vmem(nx, ny, nz)] * 3,
            *[vmem(X, w, 1, nz) for w in WIDTH + WIDTH],
            *[vmem(w, ny, nz) for w in WIDTH + WIDTH],
            vmem(NU - 1, ny, nz), vmem(NU - 1, ny, nz), vmem(nx, NU - 1, 1, nz), vmem(nx, NU - 1, 1, nz),
            vmem(NU, ny, nz), vmem(NU, ny, nz), vmem(X, H, nz), vmem(X, H, nz), vmem(NU, ny, nz), vmem(NU, ny, nz),
            vmem(nx, H, nz), vmem(nx, H, nz),
            vmem(cy, cx, 1, nz), vmem(cx, cy, nz), vmem(cx, cy, nz),
            dma((3,)),
            dma((24,)), dma((24,)), dma((8,)), dma((8,)),
            dma((cx - 1,)), dma((cx - 1,)), dma((cy - 1,)), dma((cy - 1,)),
            dma((min(cx * cy, DIRECT) - 1,)), dma((min(cx * cy, DIRECT) - 1,)),
            pltpu.SemaphoreType.REGULAR((cx - 1,)),
        ],
        compiler_params=pltpu.CompilerParams(collective_id=0, has_side_effects=True),
        name="cycle",
    )(*args, *thin)


def solution(mesh):
    return jax.shard_map(
        body,
        mesh=mesh,
        in_specs=(P("gx", "gy", None), P("gx", "gy", None), P("gx", "gy", None)),
        out_specs=P("gx", "gy", None),
        check_vma=False,
    )
```

```python
import functools

import jax
import jax.numpy as jnp
from jax import lax
from jax.experimental import pallas as pl
from jax.experimental.pallas import tpu as pltpu
from jax.sharding import PartitionSpec as P

NU = 3
CG_ITERS = 32
H = NU + 1
G = NU
COARSE = 5
WIDTH = (NU, NU - 1, NU - 1)

relax_weight = 0.8
MESH = pl.DeviceIdType.MESH
DIRS = [(1, 0), (-1, 0), (0, 1), (0, -1), (1, 1), (1, -1), (-1, 1), (-1, -1)]


def inside(ix, iy, cx, cy):
    return (ix >= 0) & (ix < cx) & (iy >= 0) & (iy < cy)


UNROLL = 16


def rows_loop(lo, hi, step, carry):
    count = (hi - lo) // UNROLL

    def several(i, c):
        for r in range(UNROLL):
            c = step(lo + UNROLL * i + r, c)
        return c

    if count:
        carry = lax.fori_loop(0, count, several, carry)
    for x in range(lo + UNROLL * count, hi):
        carry = step(x, carry)
    return carry


ROWS = 16
DIRECT = 64


def blocks_loop(lo, hi, block, carry):
    count = (hi - lo) // ROWS
    if count > 1:
        carry = lax.fori_loop(0, count, lambda i, c: block(lo + ROWS * i, c, ROWS), carry)
    elif count:
        carry = block(lo, carry, ROWS)
    if (hi - lo) % ROWS:
        carry = block(lo + ROWS * count, carry, (hi - lo) % ROWS)
    return carry


def kernel(cx, cy, nx, ny, *refs):
    (k_in, f_in, u_in, k1, f1, u1, out,
     K, F, L0, L1, L2, L3, L4, L5, L6, CE, CN, CS, CU, CD, W, SK, SF, SU,
     YLO_K, YLO_F, YLO_U, YHI_K, YHI_F, YHI_U, XLO_K, XLO_F, XLO_U, XHI_K, XHI_F, XHI_U,
     FXLO, FXHI, FYLO, FYHI, XLO2, XHI2, YLO2, YHI2, QLO, QHI, PLO, PHI, GS, E, R,
     lsem, ssem, rsem, ssem2, rsem2,
     s1s, s1r, s2s, s2r, das, dar, chain) = refs
    X = nx + 2 * H
    Y = ny + 8
    ix = lax.axis_index("gx")
    iy = lax.axis_index("gy")
    full = [k_in, f_in, u_in]
    thin = [k1, f1, u1]
    ext = [K, F, L0]
    stage = [SK, SF, SU]
    XLO = [XLO_K, XLO_F, XLO_U]
    XHI = [XHI_K, XHI_F, XHI_U]
    YLO = [YLO_K, YLO_F, YLO_U]
    YHI = [YHI_K, YHI_F, YHI_U]

    direct = cx * cy <= DIRECT
    barrier = pltpu.get_barrier_semaphore()

    def greet_x(k, c):
        pl.semaphore_signal(barrier, inc=1, device_id=(lax.rem(ix + k, cx), iy), device_id_type=MESH)
        return c

    def greet_y(k, c):
        pl.semaphore_signal(barrier, inc=1, device_id=(ix, lax.rem(iy + k, cy)), device_id_type=MESH)
        return c

    for dx, dy in (DIRS[:2] if direct else []) + DIRS[4:]:
        @pl.when(inside(ix + dx, iy + dy, cx, cy))
        def _(dx=dx, dy=dy):
            pl.semaphore_signal(barrier, inc=1, device_id=(ix + dx, iy + dy), device_id_type=MESH)
    if not direct:
        lax.fori_loop(1, cx, greet_x, 0)
    lax.fori_loop(1, cy, greet_y, 0)

    local = [pltpu.make_async_copy(full[a], stage[a], lsem.at[a]) for a in range(3)]
    for copy in local:
        copy.start()

    sides_x = (ix > 0).astype(jnp.int32) + (ix < cx - 1).astype(jnp.int32)
    sides_y = (iy > 0).astype(jnp.int32) + (iy < cy - 1).astype(jnp.int32)
    pl.semaphore_wait(barrier, (sides_x if direct else cx - 1) + (cy - 1) + sides_x * sides_y)

    def chain_signal(k):
        for dx in (1, -1):
            @pl.when((ix + dx >= 0) & (ix + dx < cx))
            def _(dx=dx):
                pl.semaphore_signal(chain.at[k], inc=1, device_id=(ix + dx, iy), device_id_type=MESH)

    def chain_wait(k):
        pl.semaphore_wait(chain.at[k], sides_x)

    def spans(dx, w):
        src = {1: (nx - w, nx), -1: (0, w), 0: (0, nx)}[dx]
        dst = {1: (H - w, H), -1: (X - H, X - H + w), 0: (H, H + nx)}[dx]
        return src, dst

    def halo(a, d):
        dx, dy = DIRS[d]
        slot = a * 8 + d
        w = WIDTH[a]
        src_rows, dst_rows = spans(dx, w)
        if dy == 0:
            src = full[a].at[src_rows[0]:src_rows[1]] if a != 1 else (FXHI if dx == 1 else FXLO)
            dst = (XLO if dx == 1 else XHI)[a]
        else:
            cols = (ny - w, ny) if dy == 1 else (0, w)
            src = thin[a].at[src_rows[0]:src_rows[1], cols[0]:cols[1]]
            if a == 1 and dx == 0:
                src = FYHI if dy == 1 else FYLO
            dst = (YLO if dy == 1 else YHI)[a].at[dst_rows[0]:dst_rows[1]]
        return pltpu.make_async_remote_copy(
            src_ref=src, dst_ref=dst, send_sem=ssem.at[slot], recv_sem=rsem.at[slot],
            device_id=(ix + dx, iy + dy), device_id_type=MESH)

    def each(d, sign, act):
        dx, dy = DIRS[d]
        pl.when(inside(ix + sign * dx, iy + sign * dy, cx, cy))(act)

    links = cx - 1 if direct else 0
    if links:
        chain_signal(0)
    for d in range(4, 8):
        def start(d=d):
            for a in (0, 2, 1):
                halo(a, d).start()
        each(d, 1, start)
    for a in (0, 2):
        for d in range(4):
            each(d, 1, lambda a=a, d=d: halo(a, d).start())

    def clear_when_absent(d):
        dx, dy = DIRS[d]

        @pl.when(jnp.logical_not(inside(ix - dx, iy - dy, cx, cy)))
        def _():
            for a in range(3):
                w = WIDTH[a]
                lo, hi = spans(dx, w)[1]
                if dy == 0:
                    (XLO if dx == 1 else XHI)[a][...] = jnp.zeros((w, ny, 128), jnp.float32)
                else:
                    (YLO if dy == 1 else YHI)[a][lo:hi] = jnp.zeros((hi - lo, w, 1, 128), jnp.float32)
            if dy == 0:
                (XLO2 if dx == 1 else XHI2)[...] = jnp.zeros((NU, ny, 128), jnp.float32)
            else:
                lo, hi = spans(dx, H)[1]
                (YLO2 if dy == 1 else YHI2)[lo:hi] = jnp.zeros((hi - lo, H, 128), jnp.float32)

    for d in range(8):
        clear_when_absent(d)

    for copy in local:
        copy.wait()

    def push(x, back):
        return SF[x] + 0.5 * (SK[x] + SK[back]) * SU[back]

    FXLO[0] = SF[0]
    FXLO[1] = push(1, 2)
    FXHI[0] = push(nx - 2, nx - 3)
    FXHI[1] = SF[nx - 1]

    def push_y(x, c):
        low = SF[x, 0:8, :] + 0.5 * (SK[x, 0:8, :] + SK[x, 1:9, :]) * SU[x, 1:9, :]
        high = SF[x, ny - 8:ny, :] + 0.5 * (SK[x, ny - 8:ny, :] + SK[x, ny - 9:ny - 1, :]) * SU[x, ny - 9:ny - 1, :]
        FYLO[x, 0] = SF[x, 0:1, :]
        FYLO[x, 1] = low[1:2]
        FYHI[x, 0] = high[6:7]
        FYHI[x, 1] = SF[x, ny - 1:ny, :]
        return c

    rows_loop(0, nx, push_y, 0)
    for d in range(4):
        each(d, 1, lambda d=d: halo(1, d).start())

    def along_x(G, ss, rs):
        def of(k):
            return pltpu.make_async_remote_copy(
                src_ref=G.at[iy, ix], dst_ref=G.at[iy, ix], send_sem=ss.at[k - 1], recv_sem=rs.at[k - 1],
                device_id=(lax.rem(ix + k, cx), iy), device_id_type=MESH)
        return of

    def along_y(G, ss, rs):
        def of(k):
            return pltpu.make_async_remote_copy(
                src_ref=G.at[iy], dst_ref=G.at[iy], send_sem=ss.at[k - 1], recv_sem=rs.at[k - 1],
                device_id=(ix, lax.rem(iy + k, cy)), device_id_type=MESH)
        return of

    def around(i, k, count):
        return jnp.where(i + k < count, i + k, i + k - count)

    def to_all(method):
        for kx in [*range(1, cx), 0]:
            for ky in range(cy):
                k = kx * cy + ky
                if k:
                    copy = pltpu.make_async_remote_copy(
                        src_ref=GS.at[iy, ix], dst_ref=GS.at[iy, ix], send_sem=das.at[k - 1], recv_sem=dar.at[k - 1],
                        device_id=(around(ix, kx, cx), around(iy, ky, cy)), device_id_type=MESH)
                    getattr(copy, method)()

    def run(of, count, method):
        def go(k, c):
            getattr(of(k), method)()
            return c
        lax.fori_loop(1, count, go, 0)

    sum_x, sum_y = along_x(GS, s1s, s1r), along_y(GS, s2s, s2r)

    lane_row = lax.broadcasted_iota(jnp.int32, (1, 128), 1)

    def whole(v):
        return jnp.sum(jnp.sum(v, axis=0, keepdims=True), axis=1, keepdims=True)

    def in_lanes(values, first=0, row=0.0):
        for k, v in enumerate(values):
            row = jnp.where(lane_row == first + k, v, row)
        return row

    def place(x, c):
        for a in range(3):
            ext[a][x, G:G + ny, :] = stage[a][x - H]
        return c

    def clear(x, c):
        L0[x, 0:8, :] = jnp.zeros((8, 128), jnp.float32)
        L0[x, Y - 8:Y, :] = jnp.zeros((8, 128), jnp.float32)
        return c

    rows_loop(1, X - 1, clear, 0)
    for x in (H - NU, H + nx + NU - 1):
        L0[x] = jnp.zeros((Y, 128), jnp.float32)
    rows_loop(H, H + nx, place, 0)

    lane = lax.broadcasted_iota(jnp.int32, (Y, 128), 1)
    up_half = jnp.where(lane < 127, 0.5, 0.0)
    down_half = jnp.where(lane > 0, 0.5, 0.0)
    ALL, LOW, HIGH = (0, Y), (0, 8), (Y - 8, Y)

    def at(ref, x, g):
        return ref[x] if g == ALL else ref[x, g[0]:g[1], :]

    def put(ref, x, g, v):
        if g == ALL:
            ref[x] = v
        else:
            ref[x, g[0]:g[1], :] = v

    def next_y(ref, x, g, v):
        return pltpu.roll(v, g[1] - g[0] - 1, 0) if g[1] == Y else ref[x, g[0] + 1:g[1] + 1, :]

    def last_y(ref, x, g, v):
        return pltpu.roll(v, 1, 0) if g[0] == 0 else ref[x, g[0] - 1:g[1] - 1, :]

    def next_z(v):
        return pltpu.roll(v, 127, 1)

    def last_z(v):
        return pltpu.roll(v, 1, 1)

    def faces_at(g):
        n = g[1] - g[0]

        def block(x, c, rows):
            k, west = c
            ks = [k] + [at(K, x + 1 + r, g) for r in range(rows)]
            ups = [next_z(ks[r]) for r in range(rows)]
            downs = [last_z(ks[r]) for r in range(rows)]
            for r in range(rows):
                k = ks[r]
                east = 0.5 * (k + ks[r + 1])
                north = 0.5 * (k + next_y(K, x + r, g, k))
                south = 0.5 * (k + last_y(K, x + r, g, k))
                up = up_half[0:n] * (k + ups[r])
                down = down_half[0:n] * (k + downs[r])
                d = east + west + north + south + up + down
                put(CE, x + r, g, east)
                put(CN, x + r, g, north)
                put(CS, x + r, g, south)
                put(CU, x + r, g, up)
                put(CD, x + r, g, down)
                put(W, x + r, g, jnp.where(k > 0, relax_weight / jnp.where(k > 0, d, 1.0), 0.0))
                west = east
            return ks[rows], west
        return block

    def faces(lo, hi, slabs):
        def start(g):
            k, before = at(K, lo, g), at(K, lo - 1, g)
            west = 0.5 * (k + before)
            put(CE, lo - 1, g, west)
            return k, west

        def block(x, c, rows):
            return tuple(faces_at(g)(x, v, rows) for g, v in zip(slabs, c))

        blocks_loop(lo, hi, block, tuple(start(g) for g in slabs))

    def sweep_at(src, dst, g):
        def block(x, c, rows):
            u, west = c
            us = [u] + [at(src, x + 1 + r, g) for r in range(rows)]
            ups = [next_z(us[r]) for r in range(rows)]
            downs = [last_z(us[r]) for r in range(rows)]
            for r in range(rows):
                u = us[r]
                east = at(CE, x + r, g) * (us[r + 1] - u)
                north = at(CN, x + r, g) * (next_y(src, x + r, g, u) - u)
                if g == ALL:
                    south = pltpu.roll(north, 1, 0)
                else:
                    south = at(CS, x + r, g) * (u - last_y(src, x + r, g, u))
                change = ((east - west) + (north - south)
                          + (at(CU, x + r, g) * (ups[r] - u) + at(CD, x + r, g) * (downs[r] - u)))
                put(dst, x + r, g, u + at(W, x + r, g) * (at(F, x + r, g) + change))
                west = east
            return us[rows], west
        return block

    def sweep(src, dst, lo, hi, slabs):
        def start(g):
            u = at(src, lo, g)
            return u, at(CE, lo - 1, g) * (u - at(src, lo - 1, g))

        def block(x, c, rows):
            return tuple(sweep_at(src, dst, g)(x, v, rows) for g, v in zip(slabs, c))

        blocks_loop(lo, hi, block, tuple(start(g) for g in slabs))

    def interior(src, dst, s):
        sweep(src, dst, H + s, H + nx - s, [ALL])

    def rims(src, dst, s):
        for lo in (H - NU + s, H + nx - s):
            sweep(src, dst, lo, lo + NU, [ALL])
        sweep(src, dst, H + s, H + nx - s, [LOW, HIGH])

    faces(H + 1, H + nx - 1, [ALL])

    for k in range(links):
        chain_wait(k)
        if k + 1 < links:
            chain_signal(k + 1)
        if k == 0:
            interior(L0, L1, 1)
        if k == 1:
            interior(L1, L2, 2)
    if links < 1:
        interior(L0, L1, 1)
    if links < 2:
        interior(L1, L2, 2)
    interior(L2, L3, 3)

    def outer(x, c):
        return c[0] + SK[x, 0:1, :], c[1] + SK[x, ny - 1:ny, :]

    none = jnp.zeros((1, 128), jnp.float32)
    y_first, y_last = rows_loop(0, nx, outer, (none, none))
    edges = in_lanes([whole(v) for v in (SK[0], SK[nx - 1], y_first, y_last)], COARSE)
    f_total = rows_loop(0, nx, lambda x, c: c + SF[x], jnp.zeros((ny, 128), jnp.float32))
    f_total = jnp.sum(f_total, axis=0, keepdims=True)

    def unpack(arrays):
        def one(x, c):
            for a in arrays:
                w = WIDTH[a]
                ext[a][x, G + ny:G + ny + w, :] = YHI[a][x, :, 0, :]
                ext[a][x, G - w:G, :] = YLO[a][x, :, 0, :]
            return c

        rows_loop(1, X - 1, one, 0)
        for a in arrays:
            w = WIDTH[a]
            for i in range(w):
                ext[a][H - w + i, G:G + ny, :] = XLO[a][i]
                ext[a][H + nx + i, G:G + ny, :] = XHI[a][i]

    for d in range(8):
        each(d, -1, lambda d=d: halo(0, d).wait_recv())
    unpack([0])
    for lo in (H - NU + 1, H + nx - 1):
        faces(lo, lo + NU, [ALL])
    faces(H + 1, H + nx - 1, [LOW, HIGH])
    for a in (2, 1):
        for d in range(8):
            each(d, -1, lambda a=a, d=d: halo(a, d).wait_recv())
    unpack([2, 1])
    rims(L0, L1, 1)
    rims(L1, L2, 2)
    rims(L2, L3, 3)

    def sides(x, c):
        return (c[2], c[3], c[0] + CS[x, 0:8, :] * L3[x, 0:8, :], c[1] + CN[x, Y - 8:Y, :] * L3[x, Y - 8:Y, :])

    c = rows_loop(H, H + nx, sides, (jnp.zeros((8, 128), jnp.float32),) * 4)
    y_low, y_high = (c[0] + c[2])[G:G + 1], (c[1] + c[3])[G - 1:G]
    x_low = jnp.sum(CE[H - 1, G:G + ny, :] * L3[H, G:G + ny, :], axis=0, keepdims=True)
    x_high = jnp.sum(CE[X - H - 1, G:G + ny, :] * L3[X - H - 1, G:G + ny, :], axis=0, keepdims=True)
    own = f_total - x_low - x_high - y_low - y_high
    GS[iy, ix] = in_lanes([whole(v) for v in (own, x_low, x_high, y_low, y_high)], 0, edges)
    if direct:
        to_all("start")
    else:
        run(sum_x, cx, "start")

    part = lax.broadcasted_iota(jnp.int32, (H, 128), 0)

    def pack(x, c):
        PLO[x] = L3[H + x, G:G + H, :] - jnp.where(part == NU - 1, L0[H + x, G:G + H, :], 0.0)
        PHI[x] = L3[H + x, G + ny - H:G + ny, :] - jnp.where(part == H - NU, L0[H + x, G + ny - H:G + ny, :], 0.0)
        return c

    rows_loop(0, nx, pack, 0)
    for i in range(NU):
        QLO[i] = L3[H + i, G:G + ny, :]
        QHI[i] = L3[H + nx - NU + i, G:G + ny, :]
    QLO[NU - 1] = QLO[NU - 1] - L0[H + NU - 1, G:G + ny, :]
    QHI[0] = QHI[0] - L0[H + nx - NU, G:G + ny, :]

    def halo2(d):
        dx, dy = DIRS[d]
        src_rows = {1: (nx - H, nx), -1: (0, H), 0: (0, nx)}[dx]
        dst_rows = {1: (0, H), -1: (X - H, X), 0: (H, H + nx)}[dx]
        if dy == 0:
            src = QHI if dx == 1 else QLO
            dst = XLO2 if dx == 1 else XHI2
        else:
            src = (PHI if dy == 1 else PLO).at[src_rows[0]:src_rows[1]]
            dst = (YLO2 if dy == 1 else YHI2).at[dst_rows[0]:dst_rows[1]]
        return pltpu.make_async_remote_copy(
            src_ref=src, dst_ref=dst, send_sem=ssem2.at[d], recv_sem=rsem2.at[d],
            device_id=(ix + dx, iy + dy), device_id_type=MESH)

    if not direct:
        run(sum_x, cx, "wait_recv")
        run(sum_y, cy, "start")
    interior(L3, L4, 1)
    interior(L4, L5, 2)
    for d in range(8):
        each(d, 1, lambda d=d: halo2(d).start())
    interior(L5, L6, 3)

    row_y = lax.broadcasted_iota(jnp.int32, (cy, 128), 0)

    def tidy(G):
        for x in range(cx):
            for y in range(cy):
                R[x, y:y + 1, :] = G[y, x]
        return [R[x] for x in range(cx)]

    def lane_of(rows, k):
        return [jnp.broadcast_to(r[:, k:k + 1], (cy, 128)) for r in rows]

    def after_y(v):
        return jnp.where(row_y < cy - 1, pltpu.roll(v, cy - 1, 0), 0.0)

    def before_y(v):
        return jnp.where(row_y > 0, pltpu.roll(v, 1, 0), 0.0)

    if direct:
        to_all("wait_recv")
    else:
        run(sum_y, cy, "wait_recv")
    coarse_rows = tidy(GS)
    nil = jnp.zeros((cy, 128), jnp.float32)
    x_first, x_last, y_first, y_last = [lane_of(coarse_rows, COARSE + k) for k in range(4)]
    east = [0.5 * (a + b) for a, b in zip(x_last, x_first[1:] + [nil])]
    west = [0.5 * (a + b) for a, b in zip(x_first, [nil] + x_last[:-1])]
    north = [0.5 * (a + after_y(b)) for a, b in zip(y_last, y_first)]
    south = [0.5 * (a + before_y(b)) for a, b in zip(y_first, y_last)]
    diag = [a + b + c + d for a, b, c, d in zip(east, west, north, south)]
    north = [jnp.where(row_y < cy - 1, n, 0.0) for n in north]
    south = [pltpu.roll(n, 1, 0) for n in north]

    own, x_low, x_high, y_low, y_high = [lane_of(coarse_rows, k) for k in range(COARSE)]
    coarse_source = [
        (a + after_y(b)) + (before_y(c) + d + e)
        for a, b, c, d, e in zip(own, y_low, y_high, x_low[1:] + [nil], [nil] + x_high[:-1])]

    def dot(a, b):
        terms = [p * q for p, q in zip(a, b)]
        while len(terms) > 1:
            terms = [sum(terms[i + 1:i + 2], terms[i]) for i in range(0, len(terms), 2)]
        return jnp.sum(terms[0], axis=0, keepdims=True)

    def coarse_apply(p):
        product = []
        for x in range(cx):
            v = diag[x] * p[x]
            if x < cx - 1:
                v = v - east[x] * p[x + 1]
            if x > 0:
                v = v - east[x - 1] * p[x - 1]
            product.append(v - (north[x] * pltpu.roll(p[x], cy - 1, 0) + south[x] * pltpu.roll(p[x], 1, 0)))
        return product

    def iterate_once(counter, carried):
        estimate, remainder, search, product, norm_now, inverse, energy = carried
        alpha = norm_now / energy
        estimate = [e + alpha * s for e, s in zip(estimate, search)]
        remainder = [r - alpha * q for r, q in zip(remainder, product)]
        applied = coarse_apply(remainder)
        norm_next = dot(remainder, remainder)
        beta = norm_next * inverse
        energy = dot(remainder, applied) - (beta * beta) * energy
        search = [r + beta * s for r, s in zip(remainder, search)]
        product = [v + beta * q for v, q in zip(applied, product)]
        return estimate, remainder, search, product, norm_next, 1.0 / norm_next, energy

    norm = dot(coarse_source, coarse_source)
    applied = coarse_apply(coarse_source)
    state = ([jnp.zeros((cy, 128), jnp.float32)] * cx, coarse_source, coarse_source, applied, norm, 1.0 / norm,
             dot(coarse_source, applied))
    estimate = lax.fori_loop(0, CG_ITERS, iterate_once, state)[0]
    for x in range(cx):
        E[x] = estimate[x]

    own_share = E[ix, pl.ds(iy, 1), :]

    def share(dx, dy):
        jx, jy = ix + dx, iy + dy
        row = E[jnp.clip(jx, 0, cx - 1), pl.ds(jnp.clip(jy, 0, cy - 1), 1), :]
        return row * inside(jx, jy, cx, cy).astype(jnp.float32) - own_share

    for d in range(8):
        each(d, -1, lambda d=d: halo2(d).wait_recv())

    def edge(x, low, high):
        L3[x, 0:G, :] = YLO2[x, H - G:H, :] + low
        L3[x, G + ny:G + ny + NU, :] = YHI2[x, 0:NU, :] + high

    for dx, lo, got in ((-1, H - NU, XLO2), (1, H + nx, XHI2)):
        low, middle, high = [share(dx, dy) for dy in (-1, 0, 1)]
        for i in range(NU):
            L3[lo + i, G:G + ny, :] = got[i] + middle
            edge(lo + i, low, high)
    low, high = share(0, -1), share(0, 1)

    def inner(x, c):
        edge(x, low, high)
        return c

    rows_loop(H, H + nx, inner, 0)

    rims(L3, L4, 1)
    rims(L4, L5, 2)
    rims(L5, L6, 3)

    def give(x, c):
        out[x] = L6[H + x, G:G + ny, :] + own_share
        return c

    rows_loop(0, nx, give, 0)

    for d in range(8):
        each(d, 1, lambda d=d: halo2(d).wait_send())
    for d in range(8):
        def sent(d=d):
            for a in range(3):
                halo(a, d).wait_send()
        each(d, 1, sent)
    if direct:
        to_all("wait_send")
    else:
        run(sum_x, cx, "wait_send")
        run(sum_y, cy, "wait_send")


def body(conductivity, source, initial):
    nx, ny, nz = conductivity.shape
    cx, cy = lax.axis_size("gx"), lax.axis_size("gy")
    X, Y = nx + 2 * H, ny + 8
    args = (conductivity, source, initial)
    thin = tuple(a.reshape(nx, ny, 1, nz) for a in args)
    wide = pltpu.VMEM((X, Y, nz), jnp.float32)
    dma = pltpu.SemaphoreType.DMA

    def vmem(*shape):
        return pltpu.VMEM(shape, jnp.float32)

    return pl.pallas_call(
        functools.partial(kernel, cx, cy, nx, ny),
        out_shape=vmem(nx, ny, nz),
        in_specs=[pl.BlockSpec(memory_space=pltpu.HBM)] * 6,
        out_specs=pl.BlockSpec(memory_space=pltpu.VMEM),
        scratch_shapes=[wide] * 15 + [
            *[vmem(nx, ny, nz)] * 3,
            *[vmem(X, w, 1, nz) for w in WIDTH + WIDTH],
            *[vmem(w, ny, nz) for w in WIDTH + WIDTH],
            vmem(NU - 1, ny, nz), vmem(NU - 1, ny, nz), vmem(nx, NU - 1, 1, nz), vmem(nx, NU - 1, 1, nz),
            vmem(NU, ny, nz), vmem(NU, ny, nz), vmem(X, H, nz), vmem(X, H, nz), vmem(NU, ny, nz), vmem(NU, ny, nz),
            vmem(nx, H, nz), vmem(nx, H, nz),
            vmem(cy, cx, 1, nz), vmem(cx, cy, nz), vmem(cx, cy, nz),
            dma((3,)),
            dma((24,)), dma((24,)), dma((8,)), dma((8,)),
            dma((cx - 1,)), dma((cx - 1,)), dma((cy - 1,)), dma((cy - 1,)),
            dma((min(cx * cy, DIRECT) - 1,)), dma((min(cx * cy, DIRECT) - 1,)),
            pltpu.SemaphoreType.REGULAR((cx - 1,)),
        ],
        compiler_params=pltpu.CompilerParams(collective_id=0, has_side_effects=True),
        name="cycle",
    )(*args, *thin)


def solution(mesh):
    return jax.shard_map(
        body,
        mesh=mesh,
        in_specs=(P("gx", "gy", None), P("gx", "gy", None), P("gx", "gy", None)),
        out_specs=P("gx", "gy", None),
        check_vma=False,
    )
```

```python
import functools

import jax
import jax.numpy as jnp
from jax import lax
from jax.experimental import pallas as pl
from jax.experimental.pallas import tpu as pltpu
from jax.sharding import PartitionSpec as P

NU = 3
CG_ITERS = 32
H = NU + 1
G = NU
COARSE = 5
WIDTH = (NU, NU - 1, NU - 1)

relax_weight = 0.8
MESH = pl.DeviceIdType.MESH
DIRS = [(1, 0), (-1, 0), (0, 1), (0, -1), (1, 1), (1, -1), (-1, 1), (-1, -1)]


def inside(ix, iy, cx, cy):
    return (ix >= 0) & (ix < cx) & (iy >= 0) & (iy < cy)


UNROLL = 16


def rows_loop(lo, hi, step, carry):
    count = (hi - lo) // UNROLL

    def several(i, c):
        for r in range(UNROLL):
            c = step(lo + UNROLL * i + r, c)
        return c

    if count:
        carry = lax.fori_loop(0, count, several, carry)
    for x in range(lo + UNROLL * count, hi):
        carry = step(x, carry)
    return carry


ROWS = 16
DIRECT = 64


def blocks_loop(lo, hi, block, carry):
    count = (hi - lo) // ROWS
    if count > 1:
        carry = lax.fori_loop(0, count, lambda i, c: block(lo + ROWS * i, c, ROWS), carry)
    elif count:
        carry = block(lo, carry, ROWS)
    if (hi - lo) % ROWS:
        carry = block(lo + ROWS * count, carry, (hi - lo) % ROWS)
    return carry


def kernel(cx, cy, nx, ny, *refs):
    (k_in, f_in, u_in, k1, f1, u1, out,
     K, F, L0, L1, L2, L3, L4, L5, L6, CE, CN, CS, CU, CD, W, SK, SF, SU,
     YLO_K, YLO_F, YLO_U, YHI_K, YHI_F, YHI_U, XLO_K, XLO_F, XLO_U, XHI_K, XHI_F, XHI_U,
     FXLO, FXHI, FYLO, FYHI, XLO2, XHI2, YLO2, YHI2, QLO, QHI, PLO, PHI, GS, E, R,
     lsem, ssem, rsem, ssem2, rsem2,
     s1s, s1r, s2s, s2r, das, dar, chain) = refs
    X = nx + 2 * H
    Y = ny + 8
    ix = lax.axis_index("gx")
    iy = lax.axis_index("gy")
    full = [k_in, f_in, u_in]
    thin = [k1, f1, u1]
    ext = [K, F, L0]
    stage = [SK, SF, SU]
    XLO = [XLO_K, XLO_F, XLO_U]
    XHI = [XHI_K, XHI_F, XHI_U]
    YLO = [YLO_K, YLO_F, YLO_U]
    YHI = [YHI_K, YHI_F, YHI_U]

    direct = cx * cy <= DIRECT
    barrier = pltpu.get_barrier_semaphore()

    def greet_x(k, c):
        pl.semaphore_signal(barrier, inc=1, device_id=(lax.rem(ix + k, cx), iy), device_id_type=MESH)
        return c

    def greet_y(k, c):
        pl.semaphore_signal(barrier, inc=1, device_id=(ix, lax.rem(iy + k, cy)), device_id_type=MESH)
        return c

    for dx, dy in (DIRS[:2] if direct else []) + DIRS[4:]:
        @pl.when(inside(ix + dx, iy + dy, cx, cy))
        def _(dx=dx, dy=dy):
            pl.semaphore_signal(barrier, inc=1, device_id=(ix + dx, iy + dy), device_id_type=MESH)
    if not direct:
        lax.fori_loop(1, cx, greet_x, 0)
    lax.fori_loop(1, cy, greet_y, 0)

    local = [pltpu.make_async_copy(full[a], stage[a], lsem.at[a]) for a in range(3)]
    for copy in local:
        copy.start()

    sides_x = (ix > 0).astype(jnp.int32) + (ix < cx - 1).astype(jnp.int32)
    sides_y = (iy > 0).astype(jnp.int32) + (iy < cy - 1).astype(jnp.int32)
    pl.semaphore_wait(barrier, (sides_x if direct else cx - 1) + (cy - 1) + sides_x * sides_y)

    def chain_signal(k):
        for dx in (1, -1):
            @pl.when((ix + dx >= 0) & (ix + dx < cx))
            def _(dx=dx):
                pl.semaphore_signal(chain.at[k], inc=1, device_id=(ix + dx, iy), device_id_type=MESH)

    def chain_wait(k):
        pl.semaphore_wait(chain.at[k], sides_x)

    def spans(dx, w):
        src = {1: (nx - w, nx), -1: (0, w), 0: (0, nx)}[dx]
        dst = {1: (H - w, H), -1: (X - H, X - H + w), 0: (H, H + nx)}[dx]
        return src, dst

    def halo(a, d):
        dx, dy = DIRS[d]
        slot = a * 8 + d
        w = WIDTH[a]
        src_rows, dst_rows = spans(dx, w)
        if dy == 0:
            src = full[a].at[src_rows[0]:src_rows[1]] if a != 1 else (FXHI if dx == 1 else FXLO)
            dst = (XLO if dx == 1 else XHI)[a]
        else:
            cols = (ny - w, ny) if dy == 1 else (0, w)
            src = thin[a].at[src_rows[0]:src_rows[1], cols[0]:cols[1]]
            if a == 1 and dx == 0:
                src = FYHI if dy == 1 else FYLO
            dst = (YLO if dy == 1 else YHI)[a].at[dst_rows[0]:dst_rows[1]]
        return pltpu.make_async_remote_copy(
            src_ref=src, dst_ref=dst, send_sem=ssem.at[slot], recv_sem=rsem.at[slot],
            device_id=(ix + dx, iy + dy), device_id_type=MESH)

    def each(d, sign, act):
        dx, dy = DIRS[d]
        pl.when(inside(ix + sign * dx, iy + sign * dy, cx, cy))(act)

    links = cx - 1 if direct else 0
    if links:
        chain_signal(0)
    for d in range(4, 8):
        def start(d=d):
            for a in (0, 2, 1):
                halo(a, d).start()
        each(d, 1, start)
    for a in (0, 2):
        for d in range(4):
            each(d, 1, lambda a=a, d=d: halo(a, d).start())

    def clear_when_absent(d):
        dx, dy = DIRS[d]

        @pl.when(jnp.logical_not(inside(ix - dx, iy - dy, cx, cy)))
        def _():
            for a in range(3):
                w = WIDTH[a]
                lo, hi = spans(dx, w)[1]
                if dy == 0:
                    (XLO if dx == 1 else XHI)[a][...] = jnp.zeros((w, ny, 128), jnp.float32)
                else:
                    (YLO if dy == 1 else YHI)[a][lo:hi] = jnp.zeros((hi - lo, w, 1, 128), jnp.float32)
            if dy == 0:
                (XLO2 if dx == 1 else XHI2)[...] = jnp.zeros((NU, ny, 128), jnp.float32)
            else:
                lo, hi = spans(dx, H)[1]
                (YLO2 if dy == 1 else YHI2)[lo:hi] = jnp.zeros((hi - lo, H, 128), jnp.float32)

    for d in range(8):
        clear_when_absent(d)

    for copy in local:
        copy.wait()

    def push(x, back):
        return SF[x] + 0.5 * (SK[x] + SK[back]) * SU[back]

    FXLO[0] = SF[0]
    FXLO[1] = push(1, 2)
    FXHI[0] = push(nx - 2, nx - 3)
    FXHI[1] = SF[nx - 1]

    def push_y(x, c):
        low = SF[x, 0:8, :] + 0.5 * (SK[x, 0:8, :] + SK[x, 1:9, :]) * SU[x, 1:9, :]
        high = SF[x, ny - 8:ny, :] + 0.5 * (SK[x, ny - 8:ny, :] + SK[x, ny - 9:ny - 1, :]) * SU[x, ny - 9:ny - 1, :]
        FYLO[x, 0] = SF[x, 0:1, :]
        FYLO[x, 1] = low[1:2]
        FYHI[x, 0] = high[6:7]
        FYHI[x, 1] = SF[x, ny - 1:ny, :]
        return c

    rows_loop(0, nx, push_y, 0)
    for d in range(4):
        each(d, 1, lambda d=d: halo(1, d).start())

    def along_x(G, ss, rs):
        def of(k):
            return pltpu.make_async_remote_copy(
                src_ref=G.at[iy, ix], dst_ref=G.at[iy, ix], send_sem=ss.at[k - 1], recv_sem=rs.at[k - 1],
                device_id=(lax.rem(ix + k, cx), iy), device_id_type=MESH)
        return of

    def along_y(G, ss, rs):
        def of(k):
            return pltpu.make_async_remote_copy(
                src_ref=G.at[iy], dst_ref=G.at[iy], send_sem=ss.at[k - 1], recv_sem=rs.at[k - 1],
                device_id=(ix, lax.rem(iy + k, cy)), device_id_type=MESH)
        return of

    def around(i, k, count):
        return jnp.where(i + k < count, i + k, i + k - count)

    def to_all(method):
        for kx in [*range(1, cx), 0]:
            for ky in range(cy):
                k = kx * cy + ky
                if k:
                    copy = pltpu.make_async_remote_copy(
                        src_ref=GS.at[iy, ix], dst_ref=GS.at[iy, ix], send_sem=das.at[k - 1], recv_sem=dar.at[k - 1],
                        device_id=(around(ix, kx, cx), around(iy, ky, cy)), device_id_type=MESH)
                    getattr(copy, method)()

    def run(of, count, method):
        def go(k, c):
            getattr(of(k), method)()
            return c
        lax.fori_loop(1, count, go, 0)

    sum_x, sum_y = along_x(GS, s1s, s1r), along_y(GS, s2s, s2r)

    lane_row = lax.broadcasted_iota(jnp.int32, (1, 128), 1)

    def whole(v):
        return jnp.sum(jnp.sum(v, axis=0, keepdims=True), axis=1, keepdims=True)

    def in_lanes(values, first=0, row=0.0):
        for k, v in enumerate(values):
            row = jnp.where(lane_row == first + k, v, row)
        return row

    def place(x, c):
        for a in range(3):
            ext[a][x, G:G + ny, :] = stage[a][x - H]
        return c

    def clear(x, c):
        L0[x, 0:8, :] = jnp.zeros((8, 128), jnp.float32)
        L0[x, Y - 8:Y, :] = jnp.zeros((8, 128), jnp.float32)
        return c

    rows_loop(1, X - 1, clear, 0)
    for x in (H - NU, H + nx + NU - 1):
        L0[x] = jnp.zeros((Y, 128), jnp.float32)
    rows_loop(H, H + nx, place, 0)

    lane = lax.broadcasted_iota(jnp.int32, (Y, 128), 1)
    up_half = jnp.where(lane < 127, 0.5, 0.0)
    down_half = jnp.where(lane > 0, 0.5, 0.0)
    ALL, LOW, HIGH = (0, Y), (0, 8), (Y - 8, Y)

    def at(ref, x, g):
        return ref[x] if g == ALL else ref[x, g[0]:g[1], :]

    def put(ref, x, g, v):
        if g == ALL:
            ref[x] = v
        else:
            ref[x, g[0]:g[1], :] = v

    def next_y(ref, x, g, v):
        return pltpu.roll(v, g[1] - g[0] - 1, 0) if g[1] == Y else ref[x, g[0] + 1:g[1] + 1, :]

    def last_y(ref, x, g, v):
        return pltpu.roll(v, 1, 0) if g[0] == 0 else ref[x, g[0] - 1:g[1] - 1, :]

    def next_z(v):
        return pltpu.roll(v, 127, 1)

    def last_z(v):
        return pltpu.roll(v, 1, 1)

    def faces_at(g):
        n = g[1] - g[0]

        def block(x, c, rows):
            k, west = c
            ks = [k] + [at(K, x + 1 + r, g) for r in range(rows)]
            ups = [next_z(ks[r]) for r in range(rows)]
            downs = [last_z(ks[r]) for r in range(rows)]
            for r in range(rows):
                k = ks[r]
                east = 0.5 * (k + ks[r + 1])
                north = 0.5 * (k + next_y(K, x + r, g, k))
                south = 0.5 * (k + last_y(K, x + r, g, k))
                up = up_half[0:n] * (k + ups[r])
                down = down_half[0:n] * (k + downs[r])
                d = east + west + north + south + up + down
                put(CE, x + r, g, east)
                put(CN, x + r, g, north)
                put(CS, x + r, g, south)
                put(CU, x + r, g, up)
                put(CD, x + r, g, down)
                put(W, x + r, g, jnp.where(k > 0, relax_weight / jnp.where(k > 0, d, 1.0), 0.0))
                west = east
            return ks[rows], west
        return block

    def faces(lo, hi, slabs):
        def start(g):
            k, before = at(K, lo, g), at(K, lo - 1, g)
            west = 0.5 * (k + before)
            put(CE, lo - 1, g, west)
            return k, west

        def block(x, c, rows):
            return tuple(faces_at(g)(x, v, rows) for g, v in zip(slabs, c))

        blocks_loop(lo, hi, block, tuple(start(g) for g in slabs))

    def sweep_at(src, dst, g):
        def block(x, c, rows):
            u, west = c
            us = [u] + [at(src, x + 1 + r, g) for r in range(rows)]
            ups = [next_z(us[r]) for r in range(rows)]
            downs = [last_z(us[r]) for r in range(rows)]
            for r in range(rows):
                u = us[r]
                east = at(CE, x + r, g) * (us[r + 1] - u)
                north = at(CN, x + r, g) * (next_y(src, x + r, g, u) - u)
                if g == ALL:
                    south = pltpu.roll(north, 1, 0)
                else:
                    south = at(CS, x + r, g) * (u - last_y(src, x + r, g, u))
                change = ((east - west) + (north - south)
                          + (at(CU, x + r, g) * (ups[r] - u) + at(CD, x + r, g) * (downs[r] - u)))
                put(dst, x + r, g, u + at(W, x + r, g) * (at(F, x + r, g) + change))
                west = east
            return us[rows], west
        return block

    def sweep(src, dst, lo, hi, slabs):
        def start(g):
            u = at(src, lo, g)
            return u, at(CE, lo - 1, g) * (u - at(src, lo - 1, g))

        def block(x, c, rows):
            return tuple(sweep_at(src, dst, g)(x, v, rows) for g, v in zip(slabs, c))

        blocks_loop(lo, hi, block, tuple(start(g) for g in slabs))

    def interior(src, dst, s):
        sweep(src, dst, H + s, H + nx - s, [ALL])

    def end_rims(src, dst, s):
        for lo in (H - NU + s, H + nx - s):
            sweep(src, dst, lo, lo + NU, [ALL])

    def side_rims(src, dst, s):
        sweep(src, dst, H + s, H + nx - s, [LOW, HIGH])

    def rims(src, dst, s):
        end_rims(src, dst, s)
        side_rims(src, dst, s)

    faces(H + 1, H + nx - 1, [ALL])

    for k in range(links):
        chain_wait(k)
        if k + 1 < links:
            chain_signal(k + 1)
        if k == 0:
            interior(L0, L1, 1)
        if k == 1:
            interior(L1, L2, 2)
    if links < 1:
        interior(L0, L1, 1)
    if links < 2:
        interior(L1, L2, 2)
    interior(L2, L3, 3)

    def outer(x, c):
        return c[0] + SK[x, 0:1, :], c[1] + SK[x, ny - 1:ny, :]

    none = jnp.zeros((1, 128), jnp.float32)
    y_first, y_last = rows_loop(0, nx, outer, (none, none))
    edges = in_lanes([whole(v) for v in (SK[0], SK[nx - 1], y_first, y_last)], COARSE)
    f_total = rows_loop(0, nx, lambda x, c: c + SF[x], jnp.zeros((ny, 128), jnp.float32))
    f_total = jnp.sum(f_total, axis=0, keepdims=True)

    def unpack_y(arrays, lo, hi):
        def one(x, c):
            for a in arrays:
                w = WIDTH[a]
                ext[a][x, G + ny:G + ny + w, :] = YHI[a][x, :, 0, :]
                ext[a][x, G - w:G, :] = YLO[a][x, :, 0, :]
            return c

        rows_loop(lo, hi, one, 0)

    def unpack_x(arrays):
        unpack_y(arrays, 1, H)
        unpack_y(arrays, H + nx, X - 1)
        for a in arrays:
            w = WIDTH[a]
            for i in range(w):
                ext[a][H - w + i, G:G + ny, :] = XLO[a][i]
                ext[a][H + nx + i, G:G + ny, :] = XHI[a][i]

    def arrive(arrays, ds):
        for a in arrays:
            for d in ds:
                each(d, -1, lambda a=a, d=d: halo(a, d).wait_recv())

    ALONG_Y, OTHERS = (2, 3), (0, 1, 4, 5, 6, 7)
    arrive([0], ALONG_Y)
    unpack_y([0], H, H + nx)
    faces(H + 1, H + nx - 1, [LOW, HIGH])
    arrive([0], OTHERS)
    unpack_x([0])
    for lo in (H - NU + 1, H + nx - 1):
        faces(lo, lo + NU, [ALL])
    levels = [L0, L1, L2, L3]

    def side(low):
        arrive([2, 1], (2,) if low else (3,))

        def one(x, c):
            for a in (2, 1):
                w = WIDTH[a]
                if low:
                    ext[a][x, G - w:G, :] = YLO[a][x, :, 0, :]
                else:
                    ext[a][x, G + ny:G + ny + w, :] = YHI[a][x, :, 0, :]
            return c

        rows_loop(H, H + nx, one, 0)
        for k in range(1, NU + 1):
            sweep(levels[k - 1], levels[k], H + k, H + nx - k, [LOW if low else HIGH])

    @pl.when(lax.rem(iy, 2) == 0)
    def _():
        side(False)
        side(True)

    @pl.when(lax.rem(iy, 2) == 1)
    def _():
        side(True)
        side(False)

    arrive([2, 1], OTHERS)
    unpack_x([2, 1])
    for k in range(1, NU + 1):
        end_rims(levels[k - 1], levels[k], k)

    def sides(x, c):
        return (c[2], c[3], c[0] + CS[x, 0:8, :] * L3[x, 0:8, :], c[1] + CN[x, Y - 8:Y, :] * L3[x, Y - 8:Y, :])

    c = rows_loop(H, H + nx, sides, (jnp.zeros((8, 128), jnp.float32),) * 4)
    y_low, y_high = (c[0] + c[2])[G:G + 1], (c[1] + c[3])[G - 1:G]
    x_low = jnp.sum(CE[H - 1, G:G + ny, :] * L3[H, G:G + ny, :], axis=0, keepdims=True)
    x_high = jnp.sum(CE[X - H - 1, G:G + ny, :] * L3[X - H - 1, G:G + ny, :], axis=0, keepdims=True)
    own = f_total - x_low - x_high - y_low - y_high
    GS[iy, ix] = in_lanes([whole(v) for v in (own, x_low, x_high, y_low, y_high)], 0, edges)
    if direct:
        to_all("start")
    else:
        run(sum_x, cx, "start")

    part = lax.broadcasted_iota(jnp.int32, (H, 128), 0)

    def pack(x, c):
        PLO[x] = L3[H + x, G:G + H, :] - jnp.where(part == NU - 1, L0[H + x, G:G + H, :], 0.0)
        PHI[x] = L3[H + x, G + ny - H:G + ny, :] - jnp.where(part == H - NU, L0[H + x, G + ny - H:G + ny, :], 0.0)
        return c

    rows_loop(0, nx, pack, 0)
    for i in range(NU):
        QLO[i] = L3[H + i, G:G + ny, :]
        QHI[i] = L3[H + nx - NU + i, G:G + ny, :]
    QLO[NU - 1] = QLO[NU - 1] - L0[H + NU - 1, G:G + ny, :]
    QHI[0] = QHI[0] - L0[H + nx - NU, G:G + ny, :]

    def halo2(d):
        dx, dy = DIRS[d]
        src_rows = {1: (nx - H, nx), -1: (0, H), 0: (0, nx)}[dx]
        dst_rows = {1: (0, H), -1: (X - H, X), 0: (H, H + nx)}[dx]
        if dy == 0:
            src = QHI if dx == 1 else QLO
            dst = XLO2 if dx == 1 else XHI2
        else:
            src = (PHI if dy == 1 else PLO).at[src_rows[0]:src_rows[1]]
            dst = (YLO2 if dy == 1 else YHI2).at[dst_rows[0]:dst_rows[1]]
        return pltpu.make_async_remote_copy(
            src_ref=src, dst_ref=dst, send_sem=ssem2.at[d], recv_sem=rsem2.at[d],
            device_id=(ix + dx, iy + dy), device_id_type=MESH)

    if not direct:
        run(sum_x, cx, "wait_recv")
        run(sum_y, cy, "start")
    interior(L3, L4, 1)
    interior(L4, L5, 2)
    for d in range(8):
        each(d, 1, lambda d=d: halo2(d).start())
    interior(L5, L6, 3)

    row_y = lax.broadcasted_iota(jnp.int32, (cy, 128), 0)

    def tidy(G):
        for x in range(cx):
            for y in range(cy):
                R[x, y:y + 1, :] = G[y, x]
        return [R[x] for x in range(cx)]

    def lane_of(rows, k):
        return [jnp.broadcast_to(r[:, k:k + 1], (cy, 128)) for r in rows]

    def after_y(v):
        return jnp.where(row_y < cy - 1, pltpu.roll(v, cy - 1, 0), 0.0)

    def before_y(v):
        return jnp.where(row_y > 0, pltpu.roll(v, 1, 0), 0.0)

    if direct:
        to_all("wait_recv")
    else:
        run(sum_y, cy, "wait_recv")
    coarse_rows = tidy(GS)
    nil = jnp.zeros((cy, 128), jnp.float32)
    x_first, x_last, y_first, y_last = [lane_of(coarse_rows, COARSE + k) for k in range(4)]
    east = [0.5 * (a + b) for a, b in zip(x_last, x_first[1:] + [nil])]
    west = [0.5 * (a + b) for a, b in zip(x_first, [nil] + x_last[:-1])]
    north = [0.5 * (a + after_y(b)) for a, b in zip(y_last, y_first)]
    south = [0.5 * (a + before_y(b)) for a, b in zip(y_first, y_last)]
    diag = [a + b + c + d for a, b, c, d in zip(east, west, north, south)]
    north = [jnp.where(row_y < cy - 1, n, 0.0) for n in north]
    south = [pltpu.roll(n, 1, 0) for n in north]

    own, x_low, x_high, y_low, y_high = [lane_of(coarse_rows, k) for k in range(COARSE)]
    coarse_source = [
        (a + after_y(b)) + (before_y(c) + d + e)
        for a, b, c, d, e in zip(own, y_low, y_high, x_low[1:] + [nil], [nil] + x_high[:-1])]

    def dot(a, b):
        terms = [p * q for p, q in zip(a, b)]
        while len(terms) > 1:
            terms = [sum(terms[i + 1:i + 2], terms[i]) for i in range(0, len(terms), 2)]
        return jnp.sum(terms[0], axis=0, keepdims=True)

    def coarse_apply(p):
        product = []
        for x in range(cx):
            v = diag[x] * p[x]
            if x < cx - 1:
                v = v - east[x] * p[x + 1]
            if x > 0:
                v = v - east[x - 1] * p[x - 1]
            product.append(v - (north[x] * pltpu.roll(p[x], cy - 1, 0) + south[x] * pltpu.roll(p[x], 1, 0)))
        return product

    def iterate_once(counter, carried):
        estimate, remainder, search, product, norm_now, inverse, energy = carried
        alpha = norm_now / energy
        estimate = [e + alpha * s for e, s in zip(estimate, search)]
        remainder = [r - alpha * q for r, q in zip(remainder, product)]
        applied = coarse_apply(remainder)
        norm_next = dot(remainder, remainder)
        beta = norm_next * inverse
        energy = dot(remainder, applied) - (beta * beta) * energy
        search = [r + beta * s for r, s in zip(remainder, search)]
        product = [v + beta * q for v, q in zip(applied, product)]
        return estimate, remainder, search, product, norm_next, 1.0 / norm_next, energy

    norm = dot(coarse_source, coarse_source)
    applied = coarse_apply(coarse_source)
    state = ([jnp.zeros((cy, 128), jnp.float32)] * cx, coarse_source, coarse_source, applied, norm, 1.0 / norm,
             dot(coarse_source, applied))
    estimate = lax.fori_loop(0, CG_ITERS, iterate_once, state)[0]
    for x in range(cx):
        E[x] = estimate[x]

    own_share = E[ix, pl.ds(iy, 1), :]

    def share(dx, dy):
        jx, jy = ix + dx, iy + dy
        row = E[jnp.clip(jx, 0, cx - 1), pl.ds(jnp.clip(jy, 0, cy - 1), 1), :]
        return row * inside(jx, jy, cx, cy).astype(jnp.float32) - own_share

    for d in range(8):
        each(d, -1, lambda d=d: halo2(d).wait_recv())

    def edge(x, low, high):
        L3[x, 0:G, :] = YLO2[x, H - G:H, :] + low
        L3[x, G + ny:G + ny + NU, :] = YHI2[x, 0:NU, :] + high

    for dx, lo, got in ((-1, H - NU, XLO2), (1, H + nx, XHI2)):
        low, middle, high = [share(dx, dy) for dy in (-1, 0, 1)]
        for i in range(NU):
            L3[lo + i, G:G + ny, :] = got[i] + middle
            edge(lo + i, low, high)
    low, high = share(0, -1), share(0, 1)

    def inner(x, c):
        edge(x, low, high)
        return c

    rows_loop(H, H + nx, inner, 0)

    rims(L3, L4, 1)
    rims(L4, L5, 2)
    rims(L5, L6, 3)

    def give(x, c):
        out[x] = L6[H + x, G:G + ny, :] + own_share
        return c

    rows_loop(0, nx, give, 0)

    for d in range(8):
        each(d, 1, lambda d=d: halo2(d).wait_send())
    for d in range(8):
        def sent(d=d):
            for a in range(3):
                halo(a, d).wait_send()
        each(d, 1, sent)
    if direct:
        to_all("wait_send")
    else:
        run(sum_x, cx, "wait_send")
        run(sum_y, cy, "wait_send")


def body(conductivity, source, initial):
    nx, ny, nz = conductivity.shape
    cx, cy = lax.axis_size("gx"), lax.axis_size("gy")
    X, Y = nx + 2 * H, ny + 8
    args = (conductivity, source, initial)
    thin = tuple(a.reshape(nx, ny, 1, nz) for a in args)
    wide = pltpu.VMEM((X, Y, nz), jnp.float32)
    dma = pltpu.SemaphoreType.DMA

    def vmem(*shape):
        return pltpu.VMEM(shape, jnp.float32)

    return pl.pallas_call(
        functools.partial(kernel, cx, cy, nx, ny),
        out_shape=vmem(nx, ny, nz),
        in_specs=[pl.BlockSpec(memory_space=pltpu.HBM)] * 6,
        out_specs=pl.BlockSpec(memory_space=pltpu.VMEM),
        scratch_shapes=[wide] * 15 + [
            *[vmem(nx, ny, nz)] * 3,
            *[vmem(X, w, 1, nz) for w in WIDTH + WIDTH],
            *[vmem(w, ny, nz) for w in WIDTH + WIDTH],
            vmem(NU - 1, ny, nz), vmem(NU - 1, ny, nz), vmem(nx, NU - 1, 1, nz), vmem(nx, NU - 1, 1, nz),
            vmem(NU, ny, nz), vmem(NU, ny, nz), vmem(X, H, nz), vmem(X, H, nz), vmem(NU, ny, nz), vmem(NU, ny, nz),
            vmem(nx, H, nz), vmem(nx, H, nz),
            vmem(cy, cx, 1, nz), vmem(cx, cy, nz), vmem(cx, cy, nz),
            dma((3,)),
            dma((24,)), dma((24,)), dma((8,)), dma((8,)),
            dma((cx - 1,)), dma((cx - 1,)), dma((cy - 1,)), dma((cy - 1,)),
            dma((min(cx * cy, DIRECT) - 1,)), dma((min(cx * cy, DIRECT) - 1,)),
            pltpu.SemaphoreType.REGULAR((cx - 1,)),
        ],
        compiler_params=pltpu.CompilerParams(collective_id=0, has_side_effects=True),
        name="cycle",
    )(*args, *thin)


def solution(mesh):
    return jax.shard_map(
        body,
        mesh=mesh,
        in_specs=(P("gx", "gy", None), P("gx", "gy", None), P("gx", "gy", None)),
        out_specs=P("gx", "gy", None),
        check_vma=False,
    )
```

```python
import functools

import jax
import jax.numpy as jnp
from jax import lax
from jax.experimental import pallas as pl
from jax.experimental.pallas import tpu as pltpu
from jax.sharding import PartitionSpec as P

NU = 3
CG_ITERS = 32
H = NU + 1
G = NU
COARSE = 5
WIDTH = (NU, NU - 1, NU - 1)

relax_weight = 0.8
MESH = pl.DeviceIdType.MESH
DIRS = [(1, 0), (-1, 0), (0, 1), (0, -1), (1, 1), (1, -1), (-1, 1), (-1, -1)]


def inside(ix, iy, cx, cy):
    return (ix >= 0) & (ix < cx) & (iy >= 0) & (iy < cy)


UNROLL = 16


def rows_loop(lo, hi, step, carry):
    count = (hi - lo) // UNROLL

    def several(i, c):
        for r in range(UNROLL):
            c = step(lo + UNROLL * i + r, c)
        return c

    if count:
        carry = lax.fori_loop(0, count, several, carry)
    for x in range(lo + UNROLL * count, hi):
        carry = step(x, carry)
    return carry


ROWS = 16
DIRECT = 64


def blocks_loop(lo, hi, block, carry):
    count = (hi - lo) // ROWS
    if count > 1:
        carry = lax.fori_loop(0, count, lambda i, c: block(lo + ROWS * i, c, ROWS), carry)
    elif count:
        carry = block(lo, carry, ROWS)
    if (hi - lo) % ROWS:
        carry = block(lo + ROWS * count, carry, (hi - lo) % ROWS)
    return carry


def kernel(cx, cy, nx, ny, *refs):
    (k_in, f_in, u_in, k1, f1, u1, out,
     K, F, L0, L1, L2, L3, L4, L5, L6, CE, CN, CS, CU, CD, W, SK, SF, SU,
     YLO_K, YLO_F, YLO_U, YHI_K, YHI_F, YHI_U, XLO_K, XLO_F, XLO_U, XHI_K, XHI_F, XHI_U,
     FXLO, FXHI, FYLO, FYHI, XLO2, XHI2, YLO2, YHI2, QLO, QHI, PLO, PHI, GS, E, R,
     lsem, ssem, rsem, ssem2, rsem2,
     s1s, s1r, s2s, s2r, das, dar, chain) = refs
    X = nx + 2 * H
    Y = ny + 8
    ix = lax.axis_index("gx")
    iy = lax.axis_index("gy")
    full = [k_in, f_in, u_in]
    thin = [k1, f1, u1]
    ext = [K, F, L0]
    stage = [SK, SF, SU]
    XLO = [XLO_K, XLO_F, XLO_U]
    XHI = [XHI_K, XHI_F, XHI_U]
    YLO = [YLO_K, YLO_F, YLO_U]
    YHI = [YHI_K, YHI_F, YHI_U]

    direct = cx * cy <= DIRECT
    barrier = pltpu.get_barrier_semaphore()

    def greet_x(k, c):
        pl.semaphore_signal(barrier, inc=1, device_id=(lax.rem(ix + k, cx), iy), device_id_type=MESH)
        return c

    def greet_y(k, c):
        pl.semaphore_signal(barrier, inc=1, device_id=(ix, lax.rem(iy + k, cy)), device_id_type=MESH)
        return c

    for dx, dy in (DIRS[:2] if direct else []) + DIRS[4:]:
        @pl.when(inside(ix + dx, iy + dy, cx, cy))
        def _(dx=dx, dy=dy):
            pl.semaphore_signal(barrier, inc=1, device_id=(ix + dx, iy + dy), device_id_type=MESH)
    if not direct:
        lax.fori_loop(1, cx, greet_x, 0)
    lax.fori_loop(1, cy, greet_y, 0)

    local = [pltpu.make_async_copy(full[a], stage[a], lsem.at[a]) for a in range(3)]
    for copy in local:
        copy.start()

    sides_x = (ix > 0).astype(jnp.int32) + (ix < cx - 1).astype(jnp.int32)
    sides_y = (iy > 0).astype(jnp.int32) + (iy < cy - 1).astype(jnp.int32)
    pl.semaphore_wait(barrier, (sides_x if direct else cx - 1) + (cy - 1) + sides_x * sides_y)

    def chain_signal(k):
        for dx in (1, -1):
            @pl.when((ix + dx >= 0) & (ix + dx < cx))
            def _(dx=dx):
                pl.semaphore_signal(chain.at[k], inc=1, device_id=(ix + dx, iy), device_id_type=MESH)

    def chain_wait(k):
        pl.semaphore_wait(chain.at[k], sides_x)

    def spans(dx, w):
        src = {1: (nx - w, nx), -1: (0, w), 0: (0, nx)}[dx]
        dst = {1: (H - w, H), -1: (X - H, X - H + w), 0: (H, H + nx)}[dx]
        return src, dst

    def halo(a, d):
        dx, dy = DIRS[d]
        slot = a * 8 + d
        w = WIDTH[a]
        src_rows, dst_rows = spans(dx, w)
        if dy == 0:
            src = full[a].at[src_rows[0]:src_rows[1]] if a != 1 else (FXHI if dx == 1 else FXLO)
            dst = (XLO if dx == 1 else XHI)[a]
        else:
            cols = (ny - w, ny) if dy == 1 else (0, w)
            src = thin[a].at[src_rows[0]:src_rows[1], cols[0]:cols[1]]
            if a == 1 and dx == 0:
                src = FYHI if dy == 1 else FYLO
            dst = (YLO if dy == 1 else YHI)[a].at[dst_rows[0]:dst_rows[1]]
        return pltpu.make_async_remote_copy(
            src_ref=src, dst_ref=dst, send_sem=ssem.at[slot], recv_sem=rsem.at[slot],
            device_id=(ix + dx, iy + dy), device_id_type=MESH)

    def each(d, sign, act):
        dx, dy = DIRS[d]
        pl.when(inside(ix + sign * dx, iy + sign * dy, cx, cy))(act)

    links = cx - 1 if direct else 0
    if links:
        chain_signal(0)
    for d in range(4, 8):
        def start(d=d):
            for a in (0, 2, 1):
                halo(a, d).start()
        each(d, 1, start)
    for a in (0, 2):
        for d in range(4):
            each(d, 1, lambda a=a, d=d: halo(a, d).start())

    def clear_when_absent(d):
        dx, dy = DIRS[d]

        @pl.when(jnp.logical_not(inside(ix - dx, iy - dy, cx, cy)))
        def _():
            for a in range(3):
                w = WIDTH[a]
                lo, hi = spans(dx, w)[1]
                if dy == 0:
                    (XLO if dx == 1 else XHI)[a][...] = jnp.zeros((w, ny, 128), jnp.float32)
                else:
                    (YLO if dy == 1 else YHI)[a][lo:hi] = jnp.zeros((hi - lo, w, 1, 128), jnp.float32)
            if dy == 0:
                (XLO2 if dx == 1 else XHI2)[...] = jnp.zeros((NU, ny, 128), jnp.float32)
            else:
                lo, hi = spans(dx, H)[1]
                (YLO2 if dy == 1 else YHI2)[lo:hi] = jnp.zeros((hi - lo, H, 128), jnp.float32)

    for d in range(8):
        clear_when_absent(d)

    for copy in local:
        copy.wait()

    def push(x, back):
        return SF[x] + 0.5 * (SK[x] + SK[back]) * SU[back]

    FXLO[0] = SF[0]
    FXLO[1] = push(1, 2)
    FXHI[0] = push(nx - 2, nx - 3)
    FXHI[1] = SF[nx - 1]

    def push_y(x, c):
        low = SF[x, 0:8, :] + 0.5 * (SK[x, 0:8, :] + SK[x, 1:9, :]) * SU[x, 1:9, :]
        high = SF[x, ny - 8:ny, :] + 0.5 * (SK[x, ny - 8:ny, :] + SK[x, ny - 9:ny - 1, :]) * SU[x, ny - 9:ny - 1, :]
        FYLO[x, 0] = SF[x, 0:1, :]
        FYLO[x, 1] = low[1:2]
        FYHI[x, 0] = high[6:7]
        FYHI[x, 1] = SF[x, ny - 1:ny, :]
        return c

    rows_loop(0, nx, push_y, 0)
    for d in range(4):
        each(d, 1, lambda d=d: halo(1, d).start())

    def along_x(G, ss, rs):
        def of(k):
            return pltpu.make_async_remote_copy(
                src_ref=G.at[iy, ix], dst_ref=G.at[iy, ix], send_sem=ss.at[k - 1], recv_sem=rs.at[k - 1],
                device_id=(lax.rem(ix + k, cx), iy), device_id_type=MESH)
        return of

    def along_y(G, ss, rs):
        def of(k):
            return pltpu.make_async_remote_copy(
                src_ref=G.at[iy], dst_ref=G.at[iy], send_sem=ss.at[k - 1], recv_sem=rs.at[k - 1],
                device_id=(ix, lax.rem(iy + k, cy)), device_id_type=MESH)
        return of

    def around(i, k, count):
        return jnp.where(i + k < count, i + k, i + k - count)

    def to_all(method):
        for kx in [*range(1, cx), 0]:
            for ky in range(cy):
                k = kx * cy + ky
                if k:
                    copy = pltpu.make_async_remote_copy(
                        src_ref=GS.at[iy, ix], dst_ref=GS.at[iy, ix], send_sem=das.at[k - 1], recv_sem=dar.at[k - 1],
                        device_id=(around(ix, kx, cx), around(iy, ky, cy)), device_id_type=MESH)
                    getattr(copy, method)()

    def run(of, count, method):
        def go(k, c):
            getattr(of(k), method)()
            return c
        lax.fori_loop(1, count, go, 0)

    sum_x, sum_y = along_x(GS, s1s, s1r), along_y(GS, s2s, s2r)

    lane_row = lax.broadcasted_iota(jnp.int32, (1, 128), 1)

    def whole(v):
        return jnp.sum(jnp.sum(v, axis=0, keepdims=True), axis=1, keepdims=True)

    def in_lanes(values, first=0, row=0.0):
        for k, v in enumerate(values):
            row = jnp.where(lane_row == first + k, v, row)
        return row

    def place(x, c):
        for a in range(3):
            ext[a][x, G:G + ny, :] = stage[a][x - H]
        return c

    def clear(x, c):
        L0[x, 0:8, :] = jnp.zeros((8, 128), jnp.float32)
        L0[x, Y - 8:Y, :] = jnp.zeros((8, 128), jnp.float32)
        return c

    rows_loop(1, X - 1, clear, 0)
    for x in (H - NU, H + nx + NU - 1):
        L0[x] = jnp.zeros((Y, 128), jnp.float32)
    rows_loop(H, H + nx, place, 0)

    lane = lax.broadcasted_iota(jnp.int32, (Y, 128), 1)
    up_half = jnp.where(lane < 127, 0.5, 0.0)
    down_half = jnp.where(lane > 0, 0.5, 0.0)
    ALL, LOW, HIGH = (0, Y), (0, 8), (Y - 8, Y)

    def at(ref, x, g):
        return ref[x] if g == ALL else ref[x, g[0]:g[1], :]

    def put(ref, x, g, v):
        if g == ALL:
            ref[x] = v
        else:
            ref[x, g[0]:g[1], :] = v

    def next_y(ref, x, g, v):
        return pltpu.roll(v, g[1] - g[0] - 1, 0) if g[1] == Y else ref[x, g[0] + 1:g[1] + 1, :]

    def last_y(ref, x, g, v):
        return pltpu.roll(v, 1, 0) if g[0] == 0 else ref[x, g[0] - 1:g[1] - 1, :]

    def next_z(v):
        return pltpu.roll(v, 127, 1)

    def last_z(v):
        return pltpu.roll(v, 1, 1)

    def faces_at(g):
        n = g[1] - g[0]

        def block(x, c, rows):
            k, west = c
            ks = [k] + [at(K, x + 1 + r, g) for r in range(rows)]
            ups = [next_z(ks[r]) for r in range(rows)]
            downs = [last_z(ks[r]) for r in range(rows)]
            for r in range(rows):
                k = ks[r]
                east = 0.5 * (k + ks[r + 1])
                north = 0.5 * (k + next_y(K, x + r, g, k))
                south = 0.5 * (k + last_y(K, x + r, g, k))
                up = up_half[0:n] * (k + ups[r])
                down = down_half[0:n] * (k + downs[r])
                d = east + west + north + south + up + down
                put(CE, x + r, g, east)
                put(CN, x + r, g, north)
                put(CS, x + r, g, south)
                put(CU, x + r, g, up)
                put(CD, x + r, g, down)
                put(W, x + r, g, jnp.where(k > 0, relax_weight / jnp.where(k > 0, d, 1.0), 0.0))
                west = east
            return ks[rows], west
        return block

    def faces(lo, hi, slabs):
        def start(g):
            k, before = at(K, lo, g), at(K, lo - 1, g)
            west = 0.5 * (k + before)
            put(CE, lo - 1, g, west)
            return k, west

        def block(x, c, rows):
            return tuple(faces_at(g)(x, v, rows) for g, v in zip(slabs, c))

        blocks_loop(lo, hi, block, tuple(start(g) for g in slabs))

    def sweep_at(src, dst, g):
        def block(x, c, rows):
            u, west = c
            us = [u] + [at(src, x + 1 + r, g) for r in range(rows)]
            ups = [next_z(us[r]) for r in range(rows)]
            downs = [last_z(us[r]) for r in range(rows)]
            for r in range(rows):
                u = us[r]
                east = at(CE, x + r, g) * (us[r + 1] - u)
                north = at(CN, x + r, g) * (next_y(src, x + r, g, u) - u)
                if g == ALL:
                    south = pltpu.roll(north, 1, 0)
                else:
                    south = at(CS, x + r, g) * (u - last_y(src, x + r, g, u))
                change = ((east - west) + (north - south)
                          + (at(CU, x + r, g) * (ups[r] - u) + at(CD, x + r, g) * (downs[r] - u)))
                put(dst, x + r, g, u + at(W, x + r, g) * (at(F, x + r, g) + change))
                west = east
            return us[rows], west
        return block

    def sweep(src, dst, lo, hi, slabs):
        def start(g):
            u = at(src, lo, g)
            return u, at(CE, lo - 1, g) * (u - at(src, lo - 1, g))

        def block(x, c, rows):
            return tuple(sweep_at(src, dst, g)(x, v, rows) for g, v in zip(slabs, c))

        blocks_loop(lo, hi, block, tuple(start(g) for g in slabs))

    def interior(src, dst, s):
        sweep(src, dst, H + s, H + nx - s, [ALL])

    def end_rims(src, dst, s):
        for lo in (H - NU + s, H + nx - s):
            sweep(src, dst, lo, lo + NU, [ALL])

    def side_rims(src, dst, s):
        sweep(src, dst, H + s, H + nx - s, [LOW, HIGH])

    def rims(src, dst, s):
        end_rims(src, dst, s)
        side_rims(src, dst, s)

    faces(H + 1, H + nx - 1, [ALL])

    for k in range(links):
        chain_wait(k)
        if k + 1 < links:
            chain_signal(k + 1)
        if k == 0:
            interior(L0, L1, 1)
        if k == 1:
            interior(L1, L2, 2)
    if links < 1:
        interior(L0, L1, 1)
    if links < 2:
        interior(L1, L2, 2)
    interior(L2, L3, 3)

    def outer(x, c):
        return c[0] + SK[x, 0:1, :], c[1] + SK[x, ny - 1:ny, :]

    none = jnp.zeros((1, 128), jnp.float32)
    y_first, y_last = rows_loop(0, nx, outer, (none, none))
    edges = in_lanes([whole(v) for v in (SK[0], SK[nx - 1], y_first, y_last)], COARSE)
    f_total = rows_loop(0, nx, lambda x, c: c + SF[x], jnp.zeros((ny, 128), jnp.float32))
    f_total = jnp.sum(f_total, axis=0, keepdims=True)

    def unpack_y(arrays, lo, hi):
        def one(x, c):
            for a in arrays:
                w = WIDTH[a]
                ext[a][x, G + ny:G + ny + w, :] = YHI[a][x, :, 0, :]
                ext[a][x, G - w:G, :] = YLO[a][x, :, 0, :]
            return c

        rows_loop(lo, hi, one, 0)

    def unpack_x(arrays):
        unpack_y(arrays, 1, H)
        unpack_y(arrays, H + nx, X - 1)
        for a in arrays:
            w = WIDTH[a]
            for i in range(w):
                ext[a][H - w + i, G:G + ny, :] = XLO[a][i]
                ext[a][H + nx + i, G:G + ny, :] = XHI[a][i]

    def arrive(arrays, ds):
        for a in arrays:
            for d in ds:
                each(d, -1, lambda a=a, d=d: halo(a, d).wait_recv())

    ALONG_Y, OTHERS = (2, 3), (0, 1, 4, 5, 6, 7)
    arrive([0], ALONG_Y)
    unpack_y([0], H, H + nx)
    faces(H + 1, H + nx - 1, [LOW, HIGH])
    levels = [L0, L1, L2, L3]

    def side(low):
        arrive([2, 1], (2,) if low else (3,))

        def one(x, c):
            for a in (2, 1):
                w = WIDTH[a]
                if low:
                    ext[a][x, G - w:G, :] = YLO[a][x, :, 0, :]
                else:
                    ext[a][x, G + ny:G + ny + w, :] = YHI[a][x, :, 0, :]
            return c

        rows_loop(H, H + nx, one, 0)
        for k in range(1, NU + 1):
            sweep(levels[k - 1], levels[k], H + k, H + nx - k, [LOW if low else HIGH])

    @pl.when(lax.rem(iy, 2) == 0)
    def _():
        side(False)
        side(True)

    @pl.when(lax.rem(iy, 2) == 1)
    def _():
        side(True)
        side(False)

    arrive([0], OTHERS)
    unpack_x([0])
    for lo in (H - NU + 1, H + nx - 1):
        faces(lo, lo + NU, [ALL])
    arrive([2, 1], OTHERS)
    unpack_x([2, 1])
    for k in range(1, NU + 1):
        end_rims(levels[k - 1], levels[k], k)

    def sides(x, c):
        return (c[2], c[3], c[0] + CS[x, 0:8, :] * L3[x, 0:8, :], c[1] + CN[x, Y - 8:Y, :] * L3[x, Y - 8:Y, :])

    c = rows_loop(H, H + nx, sides, (jnp.zeros((8, 128), jnp.float32),) * 4)
    y_low, y_high = (c[0] + c[2])[G:G + 1], (c[1] + c[3])[G - 1:G]
    x_low = jnp.sum(CE[H - 1, G:G + ny, :] * L3[H, G:G + ny, :], axis=0, keepdims=True)
    x_high = jnp.sum(CE[X - H - 1, G:G + ny, :] * L3[X - H - 1, G:G + ny, :], axis=0, keepdims=True)
    own = f_total - x_low - x_high - y_low - y_high
    GS[iy, ix] = in_lanes([whole(v) for v in (own, x_low, x_high, y_low, y_high)], 0, edges)
    if direct:
        to_all("start")
    else:
        run(sum_x, cx, "start")

    part = lax.broadcasted_iota(jnp.int32, (H, 128), 0)

    def pack(x, c):
        PLO[x] = L3[H + x, G:G + H, :] - jnp.where(part == NU - 1, L0[H + x, G:G + H, :], 0.0)
        PHI[x] = L3[H + x, G + ny - H:G + ny, :] - jnp.where(part == H - NU, L0[H + x, G + ny - H:G + ny, :], 0.0)
        return c

    rows_loop(0, nx, pack, 0)
    for i in range(NU):
        QLO[i] = L3[H + i, G:G + ny, :]
        QHI[i] = L3[H + nx - NU + i, G:G + ny, :]
    QLO[NU - 1] = QLO[NU - 1] - L0[H + NU - 1, G:G + ny, :]
    QHI[0] = QHI[0] - L0[H + nx - NU, G:G + ny, :]

    def halo2(d):
        dx, dy = DIRS[d]
        src_rows = {1: (nx - H, nx), -1: (0, H), 0: (0, nx)}[dx]
        dst_rows = {1: (0, H), -1: (X - H, X), 0: (H, H + nx)}[dx]
        if dy == 0:
            src = QHI if dx == 1 else QLO
            dst = XLO2 if dx == 1 else XHI2
        else:
            src = (PHI if dy == 1 else PLO).at[src_rows[0]:src_rows[1]]
            dst = (YLO2 if dy == 1 else YHI2).at[dst_rows[0]:dst_rows[1]]
        return pltpu.make_async_remote_copy(
            src_ref=src, dst_ref=dst, send_sem=ssem2.at[d], recv_sem=rsem2.at[d],
            device_id=(ix + dx, iy + dy), device_id_type=MESH)

    if not direct:
        run(sum_x, cx, "wait_recv")
        run(sum_y, cy, "start")
    interior(L3, L4, 1)
    interior(L4, L5, 2)
    for d in range(8):
        each(d, 1, lambda d=d: halo2(d).start())
    interior(L5, L6, 3)

    row_y = lax.broadcasted_iota(jnp.int32, (cy, 128), 0)

    def tidy(G):
        for x in range(cx):
            for y in range(cy):
                R[x, y:y + 1, :] = G[y, x]
        return [R[x] for x in range(cx)]

    def lane_of(rows, k):
        return [jnp.broadcast_to(r[:, k:k + 1], (cy, 128)) for r in rows]

    def after_y(v):
        return jnp.where(row_y < cy - 1, pltpu.roll(v, cy - 1, 0), 0.0)

    def before_y(v):
        return jnp.where(row_y > 0, pltpu.roll(v, 1, 0), 0.0)

    if direct:
        to_all("wait_recv")
    else:
        run(sum_y, cy, "wait_recv")
    coarse_rows = tidy(GS)
    nil = jnp.zeros((cy, 128), jnp.float32)
    x_first, x_last, y_first, y_last = [lane_of(coarse_rows, COARSE + k) for k in range(4)]
    east = [0.5 * (a + b) for a, b in zip(x_last, x_first[1:] + [nil])]
    west = [0.5 * (a + b) for a, b in zip(x_first, [nil] + x_last[:-1])]
    north = [0.5 * (a + after_y(b)) for a, b in zip(y_last, y_first)]
    south = [0.5 * (a + before_y(b)) for a, b in zip(y_first, y_last)]
    diag = [a + b + c + d for a, b, c, d in zip(east, west, north, south)]
    north = [jnp.where(row_y < cy - 1, n, 0.0) for n in north]
    south = [pltpu.roll(n, 1, 0) for n in north]

    own, x_low, x_high, y_low, y_high = [lane_of(coarse_rows, k) for k in range(COARSE)]
    coarse_source = [
        (a + after_y(b)) + (before_y(c) + d + e)
        for a, b, c, d, e in zip(own, y_low, y_high, x_low[1:] + [nil], [nil] + x_high[:-1])]

    def dot(a, b):
        terms = [p * q for p, q in zip(a, b)]
        while len(terms) > 1:
            terms = [sum(terms[i + 1:i + 2], terms[i]) for i in range(0, len(terms), 2)]
        return jnp.sum(terms[0], axis=0, keepdims=True)

    def coarse_apply(p):
        product = []
        for x in range(cx):
            v = diag[x] * p[x]
            if x < cx - 1:
                v = v - east[x] * p[x + 1]
            if x > 0:
                v = v - east[x - 1] * p[x - 1]
            product.append(v - (north[x] * pltpu.roll(p[x], cy - 1, 0) + south[x] * pltpu.roll(p[x], 1, 0)))
        return product

    def iterate_once(counter, carried):
        estimate, remainder, search, product, norm_now, inverse, energy = carried
        alpha = norm_now / energy
        estimate = [e + alpha * s for e, s in zip(estimate, search)]
        remainder = [r - alpha * q for r, q in zip(remainder, product)]
        applied = coarse_apply(remainder)
        norm_next = dot(remainder, remainder)
        beta = norm_next * inverse
        energy = dot(remainder, applied) - (beta * beta) * energy
        search = [r + beta * s for r, s in zip(remainder, search)]
        product = [v + beta * q for v, q in zip(applied, product)]
        return estimate, remainder, search, product, norm_next, 1.0 / norm_next, energy

    norm = dot(coarse_source, coarse_source)
    applied = coarse_apply(coarse_source)
    state = ([jnp.zeros((cy, 128), jnp.float32)] * cx, coarse_source, coarse_source, applied, norm, 1.0 / norm,
             dot(coarse_source, applied))
    estimate = lax.fori_loop(0, CG_ITERS, iterate_once, state)[0]
    for x in range(cx):
        E[x] = estimate[x]

    own_share = E[ix, pl.ds(iy, 1), :]

    def share(dx, dy):
        jx, jy = ix + dx, iy + dy
        row = E[jnp.clip(jx, 0, cx - 1), pl.ds(jnp.clip(jy, 0, cy - 1), 1), :]
        return row * inside(jx, jy, cx, cy).astype(jnp.float32) - own_share

    for d in range(8):
        each(d, -1, lambda d=d: halo2(d).wait_recv())

    def edge(x, low, high):
        L3[x, 0:G, :] = YLO2[x, H - G:H, :] + low
        L3[x, G + ny:G + ny + NU, :] = YHI2[x, 0:NU, :] + high

    for dx, lo, got in ((-1, H - NU, XLO2), (1, H + nx, XHI2)):
        low, middle, high = [share(dx, dy) for dy in (-1, 0, 1)]
        for i in range(NU):
            L3[lo + i, G:G + ny, :] = got[i] + middle
            edge(lo + i, low, high)
    low, high = share(0, -1), share(0, 1)

    def inner(x, c):
        edge(x, low, high)
        return c

    rows_loop(H, H + nx, inner, 0)

    rims(L3, L4, 1)
    rims(L4, L5, 2)
    rims(L5, L6, 3)

    def give(x, c):
        out[x] = L6[H + x, G:G + ny, :] + own_share
        return c

    rows_loop(0, nx, give, 0)

    for d in range(8):
        each(d, 1, lambda d=d: halo2(d).wait_send())
    for d in range(8):
        def sent(d=d):
            for a in range(3):
                halo(a, d).wait_send()
        each(d, 1, sent)
    if direct:
        to_all("wait_send")
    else:
        run(sum_x, cx, "wait_send")
        run(sum_y, cy, "wait_send")


def body(conductivity, source, initial):
    nx, ny, nz = conductivity.shape
    cx, cy = lax.axis_size("gx"), lax.axis_size("gy")
    X, Y = nx + 2 * H, ny + 8
    args = (conductivity, source, initial)
    thin = tuple(a.reshape(nx, ny, 1, nz) for a in args)
    wide = pltpu.VMEM((X, Y, nz), jnp.float32)
    dma = pltpu.SemaphoreType.DMA

    def vmem(*shape):
        return pltpu.VMEM(shape, jnp.float32)

    return pl.pallas_call(
        functools.partial(kernel, cx, cy, nx, ny),
        out_shape=vmem(nx, ny, nz),
        in_specs=[pl.BlockSpec(memory_space=pltpu.HBM)] * 6,
        out_specs=pl.BlockSpec(memory_space=pltpu.VMEM),
        scratch_shapes=[wide] * 15 + [
            *[vmem(nx, ny, nz)] * 3,
            *[vmem(X, w, 1, nz) for w in WIDTH + WIDTH],
            *[vmem(w, ny, nz) for w in WIDTH + WIDTH],
            vmem(NU - 1, ny, nz), vmem(NU - 1, ny, nz), vmem(nx, NU - 1, 1, nz), vmem(nx, NU - 1, 1, nz),
            vmem(NU, ny, nz), vmem(NU, ny, nz), vmem(X, H, nz), vmem(X, H, nz), vmem(NU, ny, nz), vmem(NU, ny, nz),
            vmem(nx, H, nz), vmem(nx, H, nz),
            vmem(cy, cx, 1, nz), vmem(cx, cy, nz), vmem(cx, cy, nz),
            dma((3,)),
            dma((24,)), dma((24,)), dma((8,)), dma((8,)),
            dma((cx - 1,)), dma((cx - 1,)), dma((cy - 1,)), dma((cy - 1,)),
            dma((min(cx * cy, DIRECT) - 1,)), dma((min(cx * cy, DIRECT) - 1,)),
            pltpu.SemaphoreType.REGULAR((cx - 1,)),
        ],
        compiler_params=pltpu.CompilerParams(collective_id=0, has_side_effects=True),
        name="cycle",
    )(*args, *thin)


def solution(mesh):
    return jax.shard_map(
        body,
        mesh=mesh,
        in_specs=(P("gx", "gy", None), P("gx", "gy", None), P("gx", "gy", None)),
        out_specs=P("gx", "gy", None),
        check_vma=False,
    )
```
